32 devices in a mesh: sec: 2 (over x), col: 2 (over y), elem: 8 (over z, core).
Axes of the slice: x: 2, y: 2, z: 4, core: 2. Of those that a mesh axis runs over, the one named last changes fastest.
Arguments:
- probes: float32 [64, 48, 256], P('col', 'elem'), may hold values from -6 to 6
- jacobian: float32 [2, 48, 7, 256, 256], P('sec', 'elem'), may hold values from -0.0625 to 0.0625
- neighbors: int32 [48, 7], P('elem'), may hold values from 0 to 47, as said below
- stations: int32 [512], P('elem'), may hold values from 0 to 47, as said below
- obs_weights: float32 [512, 256], P('elem'), may hold values from -0.75 to 0.75
Outputs:
- hess_probes: float32 [64, 48, 256], P('col', 'elem', 'sec')
- gram: float32 [64, 64], P('col')
The draws below stay inside these ranges and needn't reach their ends.
Inputs may be any that keep to these rules, and one draw needn't show every extreme that they name: `neighbors`: row e lists the 7 elements e - 3 to e + 3, taken modulo 48, each once, in an order drawn for each row. Station i lies in one of the 6 elements from (i // 64) * 6 on; every element holds one or more stations.
All inputs are finite; a program needn't handle non-finite values.
Results may differ from the reference program's by a relative error of at most 0.0001.
Values sent between devices are 32-bit elements; how exact they have to be, the bound alone decides.
A program may use at most 64 MiB of HBM per device.

```python
from functools import partial
import jax
import jax.numpy as jnp
from jax import lax

ORDER = 256
NBRS = 7
EL_DEV = 6
STAT_DEV = 64
STEPS = 2
SECS = 2
ELEMS = 48
COLS = 64
STATIONS = 512


def draw_neighbors(key, part):
    element_ids = jnp.arange(ELEMS, dtype=jnp.int32)
    row_keys = jax.random.split(jax.random.fold_in(key, 11), ELEMS)
    shuffle = partial(jax.random.permutation, x=NBRS)
    orders = jax.vmap(shuffle)(row_keys).astype(jnp.int32)
    radius = (NBRS - 1) // 2
    return ((element_ids[:, None] + orders - radius) % ELEMS).astype(jnp.int32)


def draw_stations(key, part):
    positions = jnp.arange(STATIONS, dtype=jnp.int32)
    block_ids = positions // STAT_DEV
    in_block = positions % STAT_DEV
    key_first, key_second = jax.random.split(jax.random.fold_in(key, 23))
    offsets = jax.random.randint(key_first, (STATIONS // STAT_DEV,), 0, EL_DEV).astype(jnp.int32)
    extras = jax.random.randint(key_second, (STATIONS,), 0, EL_DEV).astype(jnp.int32)
    within = jnp.where(in_block < EL_DEV, (in_block + offsets[block_ids]) % EL_DEV, extras)
    return (block_ids * EL_DEV + within).astype(jnp.int32)


def levels(own_key, shape, cuts, smallest, top_value):
    loudness = 1.0
    for dim, blocks in cuts:
        draws = jax.random.uniform(jax.random.fold_in(jax.random.fold_in(own_key, 6), dim), (blocks,), jnp.float32, smallest / len(cuts), top_value / len(cuts))
        loudness = loudness * jnp.repeat(jnp.exp(draws), shape[dim] // blocks).reshape((-1,) + (1,) * (len(shape) - 1 - dim))
    return loudness


def gaussian(own_key, dims, scale, reach, pieces=(), held_as=jnp.bfloat16):
    entries = scale * jax.random.normal(own_key, dims, jnp.float32)
    if pieces:
        entries = entries * levels(own_key, dims, pieces, -0.22, 0.18)
    return jnp.clip(entries, -reach, reach).astype(held_as)


def setup_inputs(seed: int = 0) -> dict:
    key_list = jax.random.split(jax.random.key(seed), 6)
    probes = gaussian(key_list[0], (COLS, ELEMS, ORDER), 1.0, 6.0, ((0, 2), (1, 8)), jnp.float32)
    jacobian = gaussian(key_list[1], (SECS, ELEMS, NBRS, ORDER, ORDER), (4 * NBRS * ORDER) ** -0.5, 0.0625, ((0, 2), (1, 8)), jnp.float32)
    neighbors = draw_neighbors(jax.random.fold_in(key_list[5], 71), 0)
    stations = draw_stations(jax.random.fold_in(key_list[5], 71), 0)
    obs_weights = gaussian(key_list[4], (STATIONS, ORDER), (ORDER // 4) ** -0.5, 0.75, ((0, 8),), jnp.float32)
    return {"probes": probes, "jacobian": jacobian, "neighbors": neighbors, "stations": stations, "obs_weights": obs_weights}


PRECISE = lax.Precision.HIGHEST


def tangent(vector, blocks, neighbors):
    gathered = jnp.take(vector, neighbors, axis=1)
    return vector + jnp.einsum("cekI,ekJI->ceJ", gathered, blocks, precision=PRECISE)


def adjoint_step(vector, blocks, neighbors):
    products = jnp.einsum("ceJ,ekJI->cekI", vector, blocks, precision=PRECISE)
    flattened = products.reshape(products.shape[0], -1, products.shape[-1])
    returned = jnp.zeros_like(vector).at[:, neighbors.reshape(-1)].add(flattened)
    return vector + returned


def observe(vector, stations, obs_weights):
    sampled = jnp.take(vector, stations, axis=1)
    readings = jnp.einsum("csI,sI->cs", sampled, obs_weights, precision=PRECISE)
    weighted = readings[:, :, None] * obs_weights[None, :, :]
    return jnp.zeros_like(vector).at[:, stations].add(weighted)


def reference(probes, jacobian, neighbors, stations, obs_weights):
    states = []
    current = probes
    for section in range(SECS):
        for repeat in range(STEPS):
            current = tangent(current, jacobian[section], neighbors)
        states.append(current)
    adjoint = observe(states[-1], stations, obs_weights)
    for section in range(SECS - 1, -1, -1):
        for repeat in range(STEPS):
            adjoint = adjoint_step(adjoint, jacobian[section], neighbors)
        if section > 0:
            adjoint = adjoint + observe(states[section - 1], stations, obs_weights)
    flat_probes = probes.reshape(COLS, -1)
    flat_hess = adjoint.reshape(COLS, -1)
    gram = jnp.einsum("ax,bx->ab", flat_probes, flat_hess, precision=PRECISE) / (ELEMS * ORDER)
    return adjoint, gram
```

```python
import functools
import math

import jax
import jax.numpy as jnp
from jax import lax
from jax.experimental import pallas as pl
from jax.experimental.pallas import tpu as pltpu
from jax.sharding import PartitionSpec as P

STEPS = 2
MESH = pl.DeviceIdType.MESH
F32 = jnp.float32
BF16 = jnp.bfloat16
LANES = 128


def halves(value):
    high = value.astype(BF16)
    low = (value - high.astype(F32)).astype(BF16)
    return high, low


def product(a, b, transposed):
    dims = (((1,), (1 if transposed else 0,)), ((), ()))
    return lax.dot_general(a, b, dims, preferred_element_type=F32)


def product3(stack, high, low, transposed):
    rows = stack.shape[0] // 2
    first = product(stack, high, transposed)
    second = product(stack[:rows], low, transposed)
    return first[:rows] + (first[rows:] + second)


def kernel(
    sizes,
    neighbors,
    stations,
    probes_hbm,
    jacobian_hbm,
    weights_hbm,
    hess_ref,
    gram_ref,
    *scratch,
):
    cols, elems, order, nbrs, stats, n_elem, n_col = sizes
    radius = (nbrs - 1) // 2
    width = radius * order
    half = order // 2
    seats = LANES // 2
    jac_f32 = scratch[:elems]
    jac_high = scratch[elems : 2 * elems]
    jac_low = scratch[2 * elems : 3 * elems]
    (
        probes_ref, weights_ref, state, field, halo_left, halo_right,
        adjoint, adjoint_in, observed, out_left, out_right, back_left, back_right,
        back_across, out_half, back_half, readings, partial, partial_in, upper, upper_in,
        u_high, u_low, placed_field, once, once_field, once_halo, once_left, once_right,
        answer_out, answer_in,
        load_sem, send_sem, recv_sem,
    ) = scratch[3 * elems :]
    section = lax.axis_index("sec")
    column = lax.axis_index("col")
    block = lax.axis_index("elem")
    left = lax.rem(block + n_elem - 1, n_elem)
    right = lax.rem(block + 1, n_elem)
    even = lax.rem(block, 2) == 0
    far = jnp.where(even, left, right)
    other = 1 - section
    first_elem = block * elems
    elem_total = elems * n_elem
    rounds = int(math.log2(n_elem))
    edge = radius + elems
    full = elems * order
    last = STEPS - 1
    LEFT, RIGHT = 0, 1
    neighbour = (left, right)
    halo_in = (halo_left, halo_right)
    out = (out_left, out_right)
    back = (back_left, back_right)
    once_in = (once_left, once_right)
    own = (slice(0, width), slice(full - width, full))
    own_ds = (pl.ds(0, width), pl.ds(full - width, width))
    own_elems = (range(0, radius), range(elems - radius, elems))
    own_span = ((radius, 2 * radius), (edge - radius, edge))

    def by_parity(run):
        @pl.when(even)
        def _():
            run(RIGHT, LEFT)

        @pl.when(jnp.logical_not(even))
        def _():
            run(LEFT, RIGHT)

    probe_load = pltpu.make_async_copy(probes_hbm, probes_ref, load_sem.at[elems])
    probe_load.start()
    jac_loads = [
        pltpu.make_async_copy(jacobian_hbm.at[0, e], jac_f32[e], load_sem.at[e])
        for e in range(elems)
    ]
    for load in jac_loads:
        load.start()
    weights_load = pltpu.make_async_copy(
        weights_hbm, weights_ref.at[pl.ds(0, stats)], load_sem.at[elems + 1]
    )
    weights_load.start()

    barrier = pltpu.get_barrier_semaphore()
    partners = [{"elem": left}, {"elem": right}, {"sec": other}, {"sec": other, "elem": far}]
    partners += [{"col": lax.rem(column + j, n_col)} for j in range(1, n_col)]
    flips = []
    for r in range(rounds):
        bit = 1 << r
        upper_bit = lax.rem(block // bit, 2)
        flips.append({"elem": block + bit - 2 * bit * upper_bit})
    second_left = lax.rem(block + n_elem - 2, n_elem)
    second_right = lax.rem(block + 2, n_elem)
    partners += [{"elem": second_left}, {"elem": second_right}]
    for partner in partners + flips:
        pl.semaphore_signal(barrier, inc=1, device_id=partner, device_id_type=MESH)

    probe_load.wait()

    @pl.when(section == 0)
    def _():
        for e in range(elems):
            state[0, :, e * order : (e + 1) * order] = probes_ref[e]

    pl.semaphore_wait(barrier, len(partners) + len(flips))

    def remote(src, dst, index, target, arrival=None):
        arrival = index if arrival is None else arrival
        return pltpu.make_async_remote_copy(
            src_ref=src, dst_ref=dst, send_sem=send_sem.at[index],
            recv_sem=recv_sem.at[arrival], device_id=target, device_id_type=MESH,
        )

    FORWARD = 4 * STEPS
    BACKWARD, UPPER = FORWARD + 2, FORWARD + 4
    ACROSS, RETURN, GRAM, LOWER, HIGHER, READ = (FORWARD + 6 + i for i in range(6))
    FLIP = READ + n_col - 1
    ONCE = FLIP + rounds
    ANSWER = ONCE + 2

    def halo_copy(t, side):
        return remote(
            state.at[t, :, own_ds[side]], halo_in[1 - side].at[t], 2 * t + side,
            {"elem": neighbour[side]},
        )

    def halo_across(side):
        return remote(
            state.at[STEPS, :, own_ds[side]], halo_in[1 - side].at[0], ACROSS,
            {"sec": other, "elem": neighbour[side]}, side,
        )

    def forward(side):
        return remote(
            state.at[STEPS, :, own_ds[side]], state.at[0, :, own_ds[side]],
            FORWARD + side, {"sec": other},
        )

    def out_copy(t, side):
        return remote(
            out[side].at[t], back[1 - side].at[t], 2 * STEPS + 2 * t + side,
            {"elem": neighbour[side]},
        )

    def out_across(side):
        return remote(
            out[side].at[last], back_across, RETURN, {"sec": other, "elem": neighbour[side]}
        )

    def once_copy(side):
        start = 0 if side == LEFT else width + full
        return remote(
            once.at[:, pl.ds(start, width)], once_in[1 - side], ONCE + side,
            {"elem": neighbour[side]},
        )

    answer_copies = [
        remote(answer_out.at[part], answer_in.at[slot], ANSWER + slot, {"elem": target})
        for slot, (part, target) in enumerate(
            ((1, right), (1, second_right), (0, left), (0, second_left))
        )
    ]

    def backward(side):
        return remote(
            adjoint.at[STEPS, :, own_ds[side]], adjoint_in.at[:, own_ds[side]],
            BACKWARD + side, {"sec": other},
        )

    def half_copy(part, side):
        return remote(
            out_half.at[part], back_half, (LOWER, HIGHER)[part],
            {"sec": section if part == 0 else other, "elem": neighbour[side]},
        )

    def up(side):
        rows = pl.ds(own_elems[side].start, radius)
        return remote(upper.at[rows], upper_in.at[rows], UPPER + side, {"sec": other})

    @pl.when(section == 0)
    def _():
        halo_copy(0, LEFT).start()
        halo_copy(0, RIGHT).start()

    for e in range(elems):
        jac_loads[e].wait()

        def split_one(d, carry, e=e):
            target = lax.rem(first_elem + e + d - radius + elem_total, elem_total)
            slot = jnp.int32(0)
            for k in range(1, nbrs):
                slot = jnp.where(neighbors[e, k] == target, jnp.int32(k), slot)
            high, low = halves(jac_f32[e][slot])
            lanes = pl.ds(pl.multiple_of(d * order, order), order)
            jac_high[e][:, lanes] = high
            jac_low[e][:, lanes] = low
            return carry

        lax.fori_loop(0, nbrs, split_one, 0)

    weights_load.wait()
    weights_ref[stats:, :] = jnp.zeros((weights_ref.shape[0] - stats, order), F32)
    weights_high, weights_low = halves(weights_ref[...])
    lane_ids = lax.broadcasted_iota(jnp.int32, (cols, LANES), 1)
    station_row = jnp.full((cols, LANES), -1, jnp.int32)
    for i in range(stats):
        station_row = jnp.where(lane_ids == i, stations[i], station_row)

    def put_field(start, value):
        high, low = halves(value)
        field[:cols, start : start + value.shape[1]] = high
        field[cols:, start : start + value.shape[1]] = low

    def blocks(ref, begin, end):
        return ref[:, begin * order : end * order]

    def gathered(e, low, high):
        return product3(
            blocks(field, low, high), blocks(jac_high[e], low - e, high - e),
            blocks(jac_low[e], low - e, high - e), True,
        )

    def here(e):
        return slice(e * order, (e + 1) * order)

    def finish_tangent(t, side, away):
        halo_copy(t, 1 - side).wait_recv()
        put_field(0 if side == LEFT else width + full, halo_in[side][t])
        for e in own_elems[side]:
            span = (e, radius) if side == LEFT else (edge, e + nbrs)
            state[t + 1, :, here(e)] = state[t + 1, :, here(e)] + gathered(e, *span)
        if t < last:
            halo_copy(t + 1, side).start()
        else:
            forward(side).start()
            if away:
                halo_across(side).start()

    def tangent(t, core, away):
        finish_tangent(t, core, False)
        finish_tangent(t, away, True)

    @pl.when(section == 0)
    def _():
        for t in range(STEPS):
            put_field(width, state[t])
            for e in range(elems):
                added = gathered(e, max(e, radius), min(e + nbrs, edge))
                state[t + 1, :, here(e)] = state[t, :, here(e)] + added
            by_parity(functools.partial(tangent, t))

    def by_block(source, rows, elements, m):
        first, second = None, None
        for e in elements:
            if abs(m - e) > radius:
                continue
            low = m - e + radius
            up_term = product(source[:, here(e)], blocks(jac_high[e], low, low + 1), False)
            low_term = product(source[:rows, here(e)], blocks(jac_low[e], low, low + 1), False)
            first = up_term if first is None else first + up_term
            second = low_term if second is None else second + low_term
        return first[:rows] + (first[rows:] + second)

    def there(m):
        return slice((m + radius) * order, (m + radius + 1) * order)

    def put_rows(start, m, value):
        high, low = halves(value)
        u_high[start : start + seats, there(m)] = high
        u_low[start : start + seats, there(m)] = low

    def station_products():
        u_high[...] = jnp.zeros(u_high.shape, BF16)
        u_low[...] = jnp.zeros(u_low.shape, BF16)
        row_ids = lax.broadcasted_iota(jnp.int32, (seats, order), 0)
        station_col = jnp.full((seats, order), -1, jnp.int32)
        for i in range(stats):
            station_col = jnp.where(row_ids == i, stations[i], station_col)

        def placed(e):
            return jnp.where(station_col == first_elem + e, weights_ref[:seats, :], 0.0)

        for e in range(elems):
            high, low = halves(placed(e))
            placed_field[:seats, here(e)] = high
            placed_field[seats:, here(e)] = low
        for side, span in ((LEFT, range(-radius, 0)), (RIGHT, range(elems, elems + radius))):
            for m in span:
                once[:, there(m)] = by_block(placed_field, seats, range(elems), m)
            once_copy(side).start()
        for m in range(elems):
            value = by_block(placed_field, seats, range(elems), m) + placed(m)
            once[:, there(m)] = value
            high, low = halves(value)
            once_field[:seats, here(m)] = high
            once_field[seats:, here(m)] = low
        for m in range(-radius, elems + radius):
            value = by_block(once_field, seats, range(elems), m)
            if 0 <= m < elems:
                value = value + once[:, there(m)]
            put_rows(seats, m, value)
        for side in (LEFT, RIGHT):
            once_copy(1 - side).wait_recv()
            high, low = halves(once_in[side][...])
            once_halo[:seats, own[side]] = high
            once_halo[seats:, own[side]] = low
            reach = own_elems[side]
            for m in range(reach.start - radius, reach.stop + radius):
                value = by_block(once_halo, seats, reach, m)
                if m in reach:
                    j = (m - reach.start) * order
                    value = value + once_in[side][:, j : j + order]
                put_rows(0 if side == LEFT else 3 * seats, m, value)

    def lanes_of(side, halo):
        if halo:
            start = 0 if side == LEFT else width + full
        else:
            start = width + own[side].start
        return slice(start, start + width)

    def answered(lanes):
        return product3(field[:, lanes], u_high[:, lanes], u_low[:, lanes], True)

    def respond(core, away):
        total = None
        for side in (core, away):
            forward(side).wait_recv()
            if side == core:
                halo_copy(0, core).start()
            put_field(width + own[side].start, state[0, :, own[side]])
            part = answered(lanes_of(side, False))
            total = part if total is None else total + part
            halo_copy(0, 1 - side).wait_recv()
            put_field(lanes_of(side, True).start, halo_in[side][0])
            total = total + answered(lanes_of(side, True))
        near = lane_ids < seats
        to_left = total[:, :LANES]
        to_right = total[:, LANES:] + jnp.where(near, pltpu.roll(to_left, seats, 1), 0.0)
        answer_out[0] = to_left
        answer_out[1] = to_right
        for copy in answer_copies:
            copy.start()
        for copy in answer_copies:
            copy.wait_recv()
        from_left, beyond_left = answer_in[0], answer_in[1]
        from_right, beyond_right = answer_in[2], answer_in[3]
        upper_half = from_left + to_left
        upper_half = upper_half + pltpu.roll(jnp.where(near, from_right, beyond_left), seats, 1)
        lower = from_right + to_right
        lower = lower + pltpu.roll(jnp.where(near, beyond_right, from_left), seats, 1)
        stack = jnp.concatenate(halves(jnp.concatenate([upper_half, lower], axis=1)), axis=0)

        def returned(lanes):
            return product3(stack, u_high[:, lanes], u_low[:, lanes], False)

        out[away][last] = returned(lanes_of(away, True))
        out_across(away).start()
        adjoint[STEPS, :, own[away]] = returned(lanes_of(away, False))
        backward(away).start()
        out[core][0] = returned(lanes_of(core, True))
        out_copy(0, core).start()
        value = returned(lanes_of(core, False))
        out_copy(0, 1 - core).wait_recv()
        adjoint[STEPS, :, own[core]] = value + back[core][0]
        backward(core).start()
        readings[column] = jnp.where(near, lower, 0.0)

    @pl.when(section == 1)
    def _():
        station_products()
        by_parity(respond)

    @pl.when(section == 0)
    def _():
        reading = jnp.zeros((cols, LANES), F32)
        for e in range(elems):
            stack = jnp.concatenate(halves(state[STEPS, :, here(e)]), axis=0)
            read = product3(stack, weights_high, weights_low, True)
            read = jnp.where(station_row == first_elem + e, read, 0.0)
            reading = reading + read
            stack = jnp.concatenate(halves(read), axis=0)
            observed[:, here(e)] = product3(stack, weights_high, weights_low, False)
        readings[column] = reading

    for slot in range(n_col, readings.shape[0]):
        readings[slot] = jnp.zeros((cols, LANES), F32)
    read_copies = [
        remote(
            readings.at[column], readings.at[column], READ + j - 1,
            {"col": lax.rem(column + j, n_col)},
        )
        for j in range(1, n_col)
    ]
    for copy in read_copies:
        copy.start()
    gram_copy = remote(partial.at[rounds], partial_in.at[rounds], GRAM, {"sec": other})

    def project():
        for copy in read_copies:
            copy.wait_recv()
        everyone = readings[...].reshape(readings.shape[0] * cols, LANES)
        high, low = halves(everyone)
        stack = jnp.concatenate(halves(readings[column]), axis=0)
        partial[0] = product3(stack, high, low, True)
        for r in range(rounds):
            copy = remote(partial.at[r], partial_in.at[r], FLIP + r, flips[r])
            copy.start()
            copy.wait_recv()
            partial[r + 1] = partial[r] + partial_in[r]
            copy.wait_send()
        gram_copy.start()

    project()

    def spread(e, low, high):
        return product3(
            field[:, here(e)], blocks(jac_high[e], low - e, high - e),
            blocks(jac_low[e], low - e, high - e), False,
        )

    def send_out(t, side, away):
        put_field(own[side].start, adjoint[t, :, own[side]])
        ref = out[side]
        if side == LEFT:
            ref[t] = spread(0, 0, radius)
            for e in range(1, radius):
                ref[t, :, e * order :] = ref[t, :, e * order :] + spread(e, e, radius)
        else:
            ref[t] = spread(elems - 1, edge, edge + radius)
            for e in range(elems - radius, elems - 1):
                size = (e + nbrs - edge) * order
                ref[t, :, :size] = ref[t, :, :size] + spread(e, edge, e + nbrs)
        if t == last and away:
            for part in range(2):
                for j in range(radius):
                    lanes = slice(j * order + part * half, j * order + (part + 1) * half)
                    out_half[part, :, j * half : (j + 1) * half] = ref[t, :, lanes]
                half_copy(part, side).start()
        else:
            out_copy(t, side).start()

    def begin_adjoint(core, away):
        for side in (away, core):
            lanes = own[side]
            backward(side).wait_recv()
            total = adjoint_in[:, lanes] + observed[:, lanes]
            if side == away:
                out_across(1 - side).wait_recv()
                total = total + back_across[...]
            adjoint[0, :, lanes] = total
            send_out(0, side, side == away)

    def inner(t, side):
        begin, end = own_span[side]
        lanes = own[side]
        adjoint[t + 1, :, lanes] = adjoint[t, :, lanes]
        for e in range(elems):
            low, high = max(e, begin), min(e + nbrs, end)
            lanes = slice((low - radius) * order, (high - radius) * order)
            adjoint[t + 1, :, lanes] = adjoint[t + 1, :, lanes] + spread(e, low, high)

    def add_back(t, side):
        lanes = own[side]
        out_copy(t, 1 - side).wait_recv()
        adjoint[t + 1, :, lanes] = adjoint[t + 1, :, lanes] + back[side][t]

    def send_up(side):
        for e in own_elems[side]:
            upper[e] = adjoint[STEPS, :, e * order + half : (e + 1) * order]
        up(side).start()

    def lower_half(e):
        return adjoint[STEPS, :, e * order : e * order + half]

    def adjoint_step(t, core, away):
        if t < last:
            for side in (core, away):
                add_back(t, side)
                send_out(t + 1, side, side == away)
        else:
            inner(t, away)
            send_up(away)
            inner(t, core)
            add_back(t, core)
            send_up(core)
            for e in own_elems[core]:
                hess_ref[e] = lower_half(e)
            half_copy(0, 1 - away).wait_recv()
            for j, e in enumerate(own_elems[away]):
                hess_ref[e] = lower_half(e) + back_half[:, j * half : (j + 1) * half]

    @pl.when(section == 0)
    def _():
        by_parity(begin_adjoint)
        for t in range(STEPS):
            if t < last:
                inner(t, LEFT)
                inner(t, RIGHT)
            by_parity(functools.partial(adjoint_step, t))

    gram_copy.wait_recv()
    scale = 1.0 / (elem_total * order)
    gram_ref[...] = (partial[rounds] + partial_in[rounds]) * scale

    def close(core, away):
        @pl.when(section == 0)
        def _():
            for t in range(STEPS):
                for side in (core, away):
                    halo_copy(t, side).wait_send()
                    if t < last or side == core:
                        out_copy(t, side).wait_send()
            halo_across(away).wait_send()
            for side in (core, away):
                forward(side).wait_send()
                up(side).wait_send()
            for part in range(2):
                half_copy(part, away).wait_send()

        @pl.when(section == 1)
        def _():
            halo_copy(0, core).wait_send()
            out_copy(0, core).wait_send()
            out_across(away).wait_send()
            for copy in answer_copies:
                copy.wait_send()
            for side in (core, away):
                once_copy(side).wait_send()
                backward(side).wait_send()
                up(side).wait_recv()
            for e in own_elems[core]:
                hess_ref[e] = upper_in[e]
            half_copy(1, 1 - away).wait_recv()
            for j, e in enumerate(own_elems[away]):
                hess_ref[e] = upper_in[e] + back_half[:, j * half : (j + 1) * half]

    by_parity(close)
    gram_copy.wait_send()
    for copy in read_copies:
        copy.wait_send()


def hand_over(hess_ref, gram_ref, hess_out, gram_out):
    hess_out[...] = hess_ref[...]
    gram_out[...] = gram_ref[:, : gram_out.shape[1]]


def per_device(n_elem, n_col, probes, jacobian, neighbors, stations, obs_weights):
    cols, elems, order = probes.shape
    nbrs = neighbors.shape[1]
    stats = stations.shape[0]
    radius = (nbrs - 1) // 2
    rounds = int(math.log2(n_elem))
    slots = max(n_col, LANES // cols)
    sizes = (cols, elems, order, nbrs, stats, n_elem, n_col)
    full, width = elems * order, radius * order
    copies = 4 * STEPS + 17 + (n_col - 1) + rounds
    seats = LANES // 2
    scratch = [pltpu.VMEM((nbrs, order, order), F32)] * elems
    scratch += [pltpu.VMEM((order, nbrs * order), BF16)] * (2 * elems)
    scratch += [
        pltpu.VMEM((elems, cols, order), F32),
        pltpu.VMEM((LANES, order), F32),
        pltpu.VMEM((STEPS + 1, cols, full), F32),
        pltpu.VMEM((2 * cols, full + 2 * width), BF16),
        pltpu.VMEM((STEPS, cols, width), F32),
        pltpu.VMEM((STEPS, cols, width), F32),
        pltpu.VMEM((STEPS + 1, cols, full), F32),
        pltpu.VMEM((cols, full), F32),
        pltpu.VMEM((cols, full), F32),
        pltpu.VMEM((STEPS, cols, width), F32),
        pltpu.VMEM((STEPS, cols, width), F32),
        pltpu.VMEM((STEPS, cols, width), F32),
        pltpu.VMEM((STEPS, cols, width), F32),
        pltpu.VMEM((cols, width), F32),
        pltpu.VMEM((2, cols, width // 2), F32),
        pltpu.VMEM((cols, width // 2), F32),
        pltpu.VMEM((slots, cols, LANES), F32),
        pltpu.VMEM((rounds + 1, cols, slots * cols), F32),
        pltpu.VMEM((rounds + 1, cols, slots * cols), F32),
        pltpu.VMEM((elems, cols, order // 2), F32),
        pltpu.VMEM((elems, cols, order // 2), F32),
        pltpu.VMEM((4 * seats, full + 2 * width), BF16),
        pltpu.VMEM((4 * seats, full + 2 * width), BF16),
        pltpu.VMEM((2 * seats, full), BF16),
        pltpu.VMEM((seats, full + 2 * width), F32),
        pltpu.VMEM((2 * seats, full), BF16),
        pltpu.VMEM((2 * seats, full), BF16),
        pltpu.VMEM((seats, width), F32),
        pltpu.VMEM((seats, width), F32),
        pltpu.VMEM((2, cols, LANES), F32),
        pltpu.VMEM((4, cols, LANES), F32),
        pltpu.SemaphoreType.DMA((elems + 2,)),
        pltpu.SemaphoreType.DMA((copies,)),
        pltpu.SemaphoreType.DMA((copies,)),
    ]
    smem = pl.BlockSpec(memory_space=pltpu.SMEM)
    anywhere = pl.BlockSpec(memory_space=pl.ANY)
    vmem = pl.BlockSpec(memory_space=pltpu.VMEM)
    hess, gram = pl.pallas_call(
        functools.partial(kernel, sizes),
        out_shape=(
            jax.ShapeDtypeStruct((elems, cols, order // 2), F32),
            jax.ShapeDtypeStruct((cols, slots * cols), F32),
        ),
        in_specs=[smem, smem, anywhere, anywhere, anywhere],
        out_specs=(vmem, vmem),
        scratch_shapes=scratch,
        compiler_params=pltpu.CompilerParams(
            collective_id=0, has_side_effects=True, vmem_limit_bytes=56 * 1024 * 1024
        ),
    )(neighbors, stations, probes.transpose(1, 0, 2), jacobian, obs_weights)
    hess, gram = pl.pallas_call(
        hand_over,
        out_shape=(
            jax.ShapeDtypeStruct(hess.shape, F32),
            jax.ShapeDtypeStruct((cols, n_col * cols), F32),
        ),
        in_specs=[vmem, vmem],
        out_specs=(vmem, vmem),
    )(hess, gram)
    return hess.transpose(1, 0, 2), gram


def solution(mesh):
    in_specs = (
        P("col", "elem", None),
        P("sec", "elem", None, None, None),
        P("elem", None),
        P("elem"),
        P("elem", None),
    )
    out_specs = (P("col", "elem", "sec"), P("col", None))
    body = functools.partial(per_device, mesh.shape["elem"], mesh.shape["col"])
    return jax.shard_map(
        body, mesh=mesh, in_specs=in_specs, out_specs=out_specs, check_vma=False
    )
```

```python
import functools
import math

import jax
import jax.numpy as jnp
from jax import lax
from jax.experimental import pallas as pl
from jax.experimental.pallas import tpu as pltpu
from jax.sharding import PartitionSpec as P

STEPS = 2
MESH = pl.DeviceIdType.MESH
F32 = jnp.float32
BF16 = jnp.bfloat16
LANES = 128


def halves(value):
    high = value.astype(BF16)
    low = (value - high.astype(F32)).astype(BF16)
    return high, low


def product(a, b, transposed):
    dims = (((1,), (1 if transposed else 0,)), ((), ()))
    return lax.dot_general(a, b, dims, preferred_element_type=F32)


def product3(stack, high, low, transposed):
    rows = stack.shape[0] // 2
    first = product(stack, high, transposed)
    second = product(stack[:rows], low, transposed)
    return first[:rows] + (first[rows:] + second)


def kernel(
    sizes,
    neighbors_hbm,
    stations_hbm,
    probes_hbm,
    jacobian_hbm,
    weights_hbm,
    hess_ref,
    gram_ref,
    *scratch,
):
    cols, elems, order, nbrs, stats, n_elem, n_col = sizes
    radius = (nbrs - 1) // 2
    width = radius * order
    half = order // 2
    seats = LANES // 2
    jac_f32 = scratch[:elems]
    jac_high = scratch[elems : 2 * elems]
    jac_low = scratch[2 * elems : 3 * elems]
    (
        probes_ref, weights_ref, state, field, halo_left, halo_right,
        adjoint, adjoint_in, observed, out_left, out_right, back_left, back_right,
        out_half, back_half, readings, partial, partial_in, upper, upper_in,
        u_high, u_low, placed_field, once, once_field, once_halo, once_left, once_right,
        spill_left, spill_right, spill_in_left, spill_in_right,
        answer_out, answer_in, neighbors, stations,
        load_sem, send_sem, recv_sem,
    ) = scratch[3 * elems :]
    section = lax.axis_index("sec")
    column = lax.axis_index("col")
    block = lax.axis_index("elem")
    left = lax.rem(block + n_elem - 1, n_elem)
    right = lax.rem(block + 1, n_elem)
    even = lax.rem(block, 2) == 0
    far = jnp.where(even, left, right)
    other = 1 - section
    first_elem = block * elems
    elem_total = elems * n_elem
    rounds = int(math.log2(n_elem))
    edge = radius + elems
    full = elems * order
    last = STEPS - 1
    LEFT, RIGHT = 0, 1
    neighbour = (left, right)
    halo_in = (halo_left, halo_right)
    out = (out_left, out_right)
    back = (back_left, back_right)
    once_in = (once_left, once_right)
    spill = (spill_left, spill_right)
    spill_in = (spill_in_left, spill_in_right)
    own_rows = (slice(seats, 2 * seats), slice(0, seats))
    other_rows = (slice(0, seats), slice(seats, 2 * seats))
    own = (slice(0, width), slice(full - width, full))
    own_ds = (pl.ds(0, width), pl.ds(full - width, width))
    own_elems = (range(0, radius), range(elems - radius, elems))
    own_span = ((radius, 2 * radius), (edge - radius, edge))

    def by_parity(run):
        @pl.when(even)
        def _():
            run(RIGHT, LEFT)

        @pl.when(jnp.logical_not(even))
        def _():
            run(LEFT, RIGHT)

    probe_load = pltpu.make_async_copy(probes_hbm, probes_ref, load_sem.at[elems])
    probe_load.start()
    table_loads = [
        pltpu.make_async_copy(neighbors_hbm, neighbors, load_sem.at[elems + 2]),
        pltpu.make_async_copy(stations_hbm, stations, load_sem.at[elems + 3]),
    ]
    for load in table_loads:
        load.start()
    weights_load = pltpu.make_async_copy(
        weights_hbm, weights_ref.at[pl.ds(0, stats)], load_sem.at[elems + 1]
    )
    weights_load.start()
    jac_loads = [
        pltpu.make_async_copy(jacobian_hbm.at[0, e], jac_f32[e], load_sem.at[e])
        for e in range(elems)
    ]
    for load in jac_loads:
        load.start()

    barrier = pltpu.get_barrier_semaphore()
    partners = [{"elem": left}, {"elem": right}, {"sec": other}, {"sec": other, "elem": far}]
    partners += [{"col": lax.rem(column + j, n_col)} for j in range(1, n_col)]
    flips = []
    for r in range(rounds):
        bit = 1 << r
        upper_bit = lax.rem(block // bit, 2)
        flips.append({"elem": block + bit - 2 * bit * upper_bit})
    second_left = lax.rem(block + n_elem - 2, n_elem)
    second_right = lax.rem(block + 2, n_elem)
    partners += [{"elem": second_left}, {"elem": second_right}]
    for partner in partners + flips:
        pl.semaphore_signal(barrier, inc=1, device_id=partner, device_id_type=MESH)

    probe_load.wait()

    @pl.when(section == 0)
    def _():
        for e in range(elems):
            state[0, :, e * order : (e + 1) * order] = probes_ref[e]

    pl.semaphore_wait(barrier, len(partners) + len(flips))

    def remote(src, dst, index, target, arrival=None):
        arrival = index if arrival is None else arrival
        return pltpu.make_async_remote_copy(
            src_ref=src, dst_ref=dst, send_sem=send_sem.at[index],
            recv_sem=recv_sem.at[arrival], device_id=target, device_id_type=MESH,
        )

    FORWARD = 4 * STEPS
    BACKWARD, UPPER = FORWARD + 2, FORWARD + 4
    ACROSS, GRAM, LOWER, HIGHER, READ = (FORWARD + 6 + i for i in range(5))
    FLIP = READ + n_col - 1
    ONCE = FLIP + rounds
    ANSWER = ONCE + 2
    SPILL = ANSWER + 4

    def halo_copy(t, side):
        return remote(
            state.at[t, :, own_ds[side]], halo_in[1 - side].at[t], 2 * t + side,
            {"elem": neighbour[side]},
        )

    def halo_across(side):
        return remote(
            state.at[STEPS, :, own_ds[side]], halo_in[1 - side].at[0], ACROSS,
            {"sec": other, "elem": neighbour[side]}, side,
        )

    def forward(side):
        return remote(
            state.at[STEPS, :, own_ds[side]], state.at[0, :, own_ds[side]],
            FORWARD + side, {"sec": other},
        )

    def out_copy(t, side):
        return remote(
            out[side].at[t], back[1 - side].at[t], 2 * STEPS + 2 * t + side,
            {"elem": neighbour[side]},
        )

    def spill_copy(side, first):
        rows = own_rows[side] if first else other_rows[side]
        rows = pl.ds(rows.start, seats)
        return remote(
            spill[side].at[rows], spill_in[1 - side].at[rows], SPILL + 2 * side + int(first),
            {"elem": neighbour[side]},
        )

    def once_copy(side):
        start = 0 if side == LEFT else width + full
        return remote(
            once.at[:, pl.ds(start, width)], once_in[1 - side], ONCE + side,
            {"elem": neighbour[side]},
        )

    answer_copies = [
        remote(answer_out.at[part], answer_in.at[slot], ANSWER + slot, {"elem": target})
        for slot, (part, target) in enumerate(
            ((1, right), (1, second_right), (0, left), (0, second_left))
        )
    ]

    def backward(side):
        return remote(
            adjoint.at[STEPS, :, own_ds[side]], adjoint_in.at[:, own_ds[side]],
            BACKWARD + side, {"sec": other},
        )

    def half_copy(part, side):
        return remote(
            out_half.at[part], back_half, (LOWER, HIGHER)[part],
            {"sec": section if part == 0 else other, "elem": neighbour[side]},
        )

    def up(side):
        rows = pl.ds(own_elems[side].start, radius)
        return remote(upper.at[rows], upper_in.at[rows], UPPER + side, {"sec": other})

    @pl.when(section == 0)
    def _():
        halo_copy(0, LEFT).start()
        halo_copy(0, RIGHT).start()

    for load in table_loads:
        load.wait()

    def split(e, use):
        for d in range(nbrs):
            target = lax.rem(first_elem + e + d - radius + elem_total, elem_total)
            slot = jnp.int32(0)
            for k in range(1, nbrs):
                slot = jnp.where(neighbors[e, k] == target, jnp.int32(k), slot)
            high, low = halves(jac_f32[e][slot])
            jac_high[e][:, d * order : (d + 1) * order] = high
            jac_low[e][:, d * order : (d + 1) * order] = low
            use(e + d - radius, high, low)

    lane_ids = lax.broadcasted_iota(jnp.int32, (cols, LANES), 1)

    def take_weights():
        weights_load.wait()
        if weights_ref.shape[0] > stats:
            weights_ref[stats:, :] = jnp.zeros((weights_ref.shape[0] - stats, order), F32)

    def put_field(start, value):
        high, low = halves(value)
        field[:cols, start : start + value.shape[1]] = high
        field[cols:, start : start + value.shape[1]] = low

    def blocks(ref, begin, end):
        return ref[:, begin * order : end * order]

    def gathered(e, low, high):
        return product3(
            blocks(field, low, high), blocks(jac_high[e], low - e, high - e),
            blocks(jac_low[e], low - e, high - e), True,
        )

    def here(e):
        return slice(e * order, (e + 1) * order)

    def advance(t, e):
        added = gathered(e, max(e, radius), min(e + nbrs, edge))
        state[t + 1, :, here(e)] = state[t, :, here(e)] + added

    def finish_tangent(t, side, away):
        halo_copy(t, 1 - side).wait_recv()
        put_field(0 if side == LEFT else width + full, halo_in[side][t])
        for e in own_elems[side]:
            span = (e, radius) if side == LEFT else (edge, e + nbrs)
            state[t + 1, :, here(e)] = state[t + 1, :, here(e)] + gathered(e, *span)
        if t < last:
            halo_copy(t + 1, side).start()
        else:
            forward(side).start()
            if away:
                halo_across(side).start()

    def tangent(t, core, away):
        if t > 0:
            put_field(width, state[t])
        for side in (away, core) if t == 0 else (core, away):
            if t > 0:
                for e in own_elems[side]:
                    advance(t, e)
            finish_tangent(t, side, side == away)

    @pl.when(section == 0)
    def _():
        put_field(width, state[0])
        for e in range(elems):
            jac_loads[e].wait()
            terms = [None, None]

            def use(m, high, low):
                if 0 <= m < elems:
                    source = blocks(field, m + radius, m + radius + 1)
                    pair = product(source, high, True), product(source[:cols], low, True)
                    for i in range(2):
                        terms[i] = pair[i] if terms[i] is None else terms[i] + pair[i]

            split(e, use)
            added = terms[0][:cols] + (terms[0][cols:] + terms[1])
            state[1, :, here(e)] = state[0, :, here(e)] + added
        for t in range(STEPS):
            by_parity(functools.partial(tangent, t))

    def by_block(source, rows, elements, m):
        first, second = None, None
        for e in elements:
            if abs(m - e) > radius:
                continue
            low = m - e + radius
            up_term = product(source[:, here(e)], blocks(jac_high[e], low, low + 1), False)
            low_term = product(source[:rows, here(e)], blocks(jac_low[e], low, low + 1), False)
            first = up_term if first is None else first + up_term
            second = low_term if second is None else second + low_term
        return first[:rows] + (first[rows:] + second)

    def there(m):
        return slice((m + radius) * order, (m + radius + 1) * order)

    def put_rows(start, m, value):
        high, low = halves(value)
        u_high[start : start + seats, there(m)] = high
        u_low[start : start + seats, there(m)] = low

    def station_products():
        take_weights()
        u_high[...] = jnp.zeros(u_high.shape, BF16)
        u_low[...] = jnp.zeros(u_low.shape, BF16)
        row_ids = lax.broadcasted_iota(jnp.int32, (seats, order), 0)
        station_col = jnp.full((seats, order), -1, jnp.int32)
        for i in range(stats):
            station_col = jnp.where(row_ids == i, stations[i], station_col)

        def placed(e):
            return jnp.where(station_col == first_elem + e, weights_ref[:seats, :], 0.0)

        for e in range(elems):
            high, low = halves(placed(e))
            placed_field[:seats, here(e)] = high
            placed_field[seats:, here(e)] = low

        for e in range(elems):
            jac_loads[e].wait()

            def use(m, high, low, e=e):
                source = placed_field[:, here(e)]
                first = product(source, high, False)
                value = first[seats:] + product(source[:seats], low, False)
                value = first[:seats] + value
                if m == e:
                    value = value + placed(e)
                if e > 0 and m < e + radius:
                    value = value + once[:, there(m)]
                once[:, there(m)] = value

            split(e, use)
            if e == radius - 1:
                once_copy(LEFT).start()
        once_copy(RIGHT).start()
        for m in range(elems):
            high, low = halves(once[:, there(m)])
            once_field[:seats, here(m)] = high
            once_field[seats:, here(m)] = low
        for side, span in ((LEFT, range(-radius, 0)), (RIGHT, range(elems, elems + radius))):
            for j, m in enumerate(span):
                value = by_block(once_field, seats, range(elems), m)
                put_rows(seats, m, value)
                spill[side][own_rows[side], here(j)] = value
            spill_copy(side, True).start()
        for m in range(elems):
            value = by_block(once_field, seats, range(elems), m)
            put_rows(seats, m, value + once[:, there(m)])
        for side in (LEFT, RIGHT):
            once_copy(1 - side).wait_recv()
            high, low = halves(once_in[side][...])
            once_halo[:seats, own[side]] = high
            once_halo[seats:, own[side]] = low
            reach = own_elems[side]
            outside = range(-radius, 0) if side == LEFT else range(elems, elems + radius)
            for j, m in enumerate(outside):
                value = by_block(once_halo, seats, reach, m)
                put_rows(0 if side == LEFT else 3 * seats, m, value)
                spill[side][other_rows[side], here(j)] = value
            spill_copy(side, False).start()
            for m in range(elems):
                if m - reach.stop >= radius or reach.start - m > radius:
                    continue
                value = by_block(once_halo, seats, reach, m)
                if m in reach:
                    value = value + once_in[side][:, here(m - reach.start)]
                put_rows(0 if side == LEFT else 3 * seats, m, value)

    def merge(side):
        for part in (True, False):
            spill_copy(1 - side, part).wait_recv()
        starts = (0, seats) if side == LEFT else (seats, 3 * seats)
        for i in range(2):
            rows = slice(starts[i], starts[i] + seats)
            for j, m in enumerate(own_elems[side]):
                value = u_high[rows, there(m)].astype(F32) + u_low[rows, there(m)].astype(F32)
                value = value + spill_in[side][i * seats : (i + 1) * seats, here(j)]
                put_rows(starts[i], m, value)

    def lanes_of(side, halo):
        if halo:
            start = 0 if side == LEFT else width + full
        else:
            start = width + own[side].start
        return slice(start, start + width)

    def answered(lanes):
        return product3(field[:, lanes], u_high[:, lanes], u_low[:, lanes], True)

    def respond(core, away):
        total = None
        for side in (core, away):
            forward(side).wait_recv()
            if side == core:
                halo_copy(0, core).start()
            put_field(width + own[side].start, state[0, :, own[side]])
            part = answered(lanes_of(side, False))
            total = part if total is None else total + part
            halo_copy(0, 1 - side).wait_recv()
            put_field(lanes_of(side, True).start, halo_in[side][0])
            total = total + answered(lanes_of(side, True))
        near = lane_ids < seats
        to_left = total[:, :LANES]
        to_right = total[:, LANES:] + jnp.where(near, pltpu.roll(to_left, seats, 1), 0.0)
        answer_out[0] = to_left
        answer_out[1] = to_right
        for copy in answer_copies:
            copy.start()
        for side in (core, away):
            merge(side)
        for copy in answer_copies:
            copy.wait_recv()
        from_left, beyond_left = answer_in[0], answer_in[1]
        from_right, beyond_right = answer_in[2], answer_in[3]
        upper_half = from_left + to_left
        upper_half = upper_half + pltpu.roll(jnp.where(near, from_right, beyond_left), seats, 1)
        lower = from_right + to_right
        lower = lower + pltpu.roll(jnp.where(near, beyond_right, from_left), seats, 1)
        stack = jnp.concatenate(halves(jnp.concatenate([upper_half, lower], axis=1)), axis=0)

        def returned(lanes):
            return product3(stack, u_high[:, lanes], u_low[:, lanes], False)

        for side in (away, core):
            adjoint[STEPS, :, own[side]] = returned(lanes_of(side, False))
            backward(side).start()
        readings[column] = jnp.where(near, lower, 0.0)

    @pl.when(section == 1)
    def _():
        station_products()
        by_parity(respond)

    @pl.when(section == 0)
    def _():
        take_weights()
        weights_high, weights_low = halves(weights_ref[...])
        station_row = jnp.full((cols, LANES), -1, jnp.int32)
        for i in range(stats):
            station_row = jnp.where(lane_ids == i, stations[i], station_row)
        reading = jnp.zeros((cols, LANES), F32)
        for e in range(elems):
            stack = jnp.concatenate(halves(state[STEPS, :, here(e)]), axis=0)
            read = product3(stack, weights_high, weights_low, True)
            read = jnp.where(station_row == first_elem + e, read, 0.0)
            reading = reading + read
            stack = jnp.concatenate(halves(read), axis=0)
            observed[:, here(e)] = product3(stack, weights_high, weights_low, False)
        readings[column] = reading

    for slot in range(n_col, readings.shape[0]):
        readings[slot] = jnp.zeros((cols, LANES), F32)
    read_copies = [
        remote(
            readings.at[column], readings.at[column], READ + j - 1,
            {"col": lax.rem(column + j, n_col)},
        )
        for j in range(1, n_col)
    ]
    for copy in read_copies:
        copy.start()
    gram_copy = remote(partial.at[rounds], partial_in.at[rounds], GRAM, {"sec": other})

    def project():
        for copy in read_copies:
            copy.wait_recv()
        everyone = readings[...].reshape(readings.shape[0] * cols, LANES)
        high, low = halves(everyone)
        stack = jnp.concatenate(halves(readings[column]), axis=0)
        partial[0] = product3(stack, high, low, True)
        for r in range(rounds):
            copy = remote(partial.at[r], partial_in.at[r], FLIP + r, flips[r])
            copy.start()
            copy.wait_recv()
            partial[r + 1] = partial[r] + partial_in[r]
            copy.wait_send()
        gram_copy.start()

    project()

    def send_out(t, side, away):
        put_field(own[side].start, adjoint[t, :, own[side]])
        ref = out[side]
        start = -radius if side == LEFT else elems
        for j in range(radius):
            value = by_block(field, cols, own_elems[side], start + j)
            if t == last and away:
                for part in range(2):
                    half_lanes = slice(part * half, (part + 1) * half)
                    out_half[part, :, j * half : (j + 1) * half] = value[:, half_lanes]
            else:
                ref[t, :, here(j)] = value
        if t == last and away:
            for part in range(2):
                half_copy(part, side).start()
        else:
            out_copy(t, side).start()

    def inner(t, side, first):
        for m in range(elems):
            value = by_block(field, cols, own_elems[side], m)
            if m in own_elems[side]:
                value = value + adjoint[t, :, here(m)]
            if not first:
                value = value + adjoint[t + 1, :, here(m)]
            adjoint[t + 1, :, here(m)] = value

    def add_back(t, side):
        lanes = own[side]
        out_copy(t, 1 - side).wait_recv()
        adjoint[t + 1, :, lanes] = adjoint[t + 1, :, lanes] + back[side][t]

    def send_up(side):
        for e in own_elems[side]:
            upper[e] = adjoint[STEPS, :, e * order + half : (e + 1) * order]
        up(side).start()

    def lower_half(e):
        return adjoint[STEPS, :, e * order : e * order + half]

    def adjoint_step(t, core, away):
        order_of_sides = (away, core) if t == 0 else (core, away)
        for side in order_of_sides:
            if t == 0:
                lanes = own[side]
                backward(side).wait_recv()
                total = adjoint_in[:, lanes] + observed[:, lanes]
                adjoint[0, :, lanes] = total
            else:
                add_back(t - 1, side)
            send_out(t, side, side == away)
            inner(t, side, side == order_of_sides[0])
        if t == last:
            send_up(away)
            add_back(t, core)
            send_up(core)
            for e in own_elems[core]:
                hess_ref[e] = lower_half(e)
            half_copy(0, 1 - away).wait_recv()
            for j, e in enumerate(own_elems[away]):
                hess_ref[e] = lower_half(e) + back_half[:, j * half : (j + 1) * half]

    @pl.when(section == 0)
    def _():
        for t in range(STEPS):
            by_parity(functools.partial(adjoint_step, t))

    gram_copy.wait_recv()
    scale = 1.0 / (elem_total * order)
    gram_ref[...] = (partial[rounds] + partial_in[rounds]) * scale

    def close(core, away):
        @pl.when(section == 0)
        def _():
            for t in range(STEPS):
                for side in (core, away):
                    halo_copy(t, side).wait_send()
                    if t < last or side == core:
                        out_copy(t, side).wait_send()
            halo_across(away).wait_send()
            for side in (core, away):
                forward(side).wait_send()
                up(side).wait_send()
            for part in range(2):
                half_copy(part, away).wait_send()

        @pl.when(section == 1)
        def _():
            halo_copy(0, core).wait_send()
            for copy in answer_copies:
                copy.wait_send()
            for side in (core, away):
                once_copy(side).wait_send()
                for part in (True, False):
                    spill_copy(side, part).wait_send()
                backward(side).wait_send()
                up(side).wait_recv()
            for e in own_elems[core]:
                hess_ref[e] = upper_in[e]
            half_copy(1, 1 - away).wait_recv()
            for j, e in enumerate(own_elems[away]):
                hess_ref[e] = upper_in[e] + back_half[:, j * half : (j + 1) * half]

    by_parity(close)
    gram_copy.wait_send()
    for copy in read_copies:
        copy.wait_send()


def hand_over(hess_ref, gram_ref, hess_out, gram_out):
    hess_out[...] = hess_ref[...]
    gram_out[...] = gram_ref[:, : gram_out.shape[1]]


def per_device(n_elem, n_col, probes, jacobian, neighbors, stations, obs_weights):
    cols, elems, order = probes.shape
    nbrs = neighbors.shape[1]
    stats = stations.shape[0]
    radius = (nbrs - 1) // 2
    rounds = int(math.log2(n_elem))
    slots = max(n_col, LANES // cols)
    sizes = (cols, elems, order, nbrs, stats, n_elem, n_col)
    full, width = elems * order, radius * order
    copies = 4 * STEPS + 20 + (n_col - 1) + rounds
    seats = LANES // 2
    scratch = [pltpu.VMEM((nbrs, order, order), F32)] * elems
    scratch += [pltpu.VMEM((order, nbrs * order), BF16)] * (2 * elems)
    scratch += [
        pltpu.VMEM((elems, cols, order), F32),
        pltpu.VMEM((LANES, order), F32),
        pltpu.VMEM((STEPS + 1, cols, full), F32),
        pltpu.VMEM((2 * cols, full + 2 * width), BF16),
        pltpu.VMEM((STEPS, cols, width), F32),
        pltpu.VMEM((STEPS, cols, width), F32),
        pltpu.VMEM((STEPS + 1, cols, full), F32),
        pltpu.VMEM((cols, full), F32),
        pltpu.VMEM((cols, full), F32),
        pltpu.VMEM((STEPS, cols, width), F32),
        pltpu.VMEM((STEPS, cols, width), F32),
        pltpu.VMEM((STEPS, cols, width), F32),
        pltpu.VMEM((STEPS, cols, width), F32),
        pltpu.VMEM((2, cols, width // 2), F32),
        pltpu.VMEM((cols, width // 2), F32),
        pltpu.VMEM((slots, cols, LANES), F32),
        pltpu.VMEM((rounds + 1, cols, slots * cols), F32),
        pltpu.VMEM((rounds + 1, cols, slots * cols), F32),
        pltpu.VMEM((elems, cols, order // 2), F32),
        pltpu.VMEM((elems, cols, order // 2), F32),
        pltpu.VMEM((4 * seats, full + 2 * width), BF16),
        pltpu.VMEM((4 * seats, full + 2 * width), BF16),
        pltpu.VMEM((2 * seats, full), BF16),
        pltpu.VMEM((seats, full + 2 * width), F32),
        pltpu.VMEM((2 * seats, full), BF16),
        pltpu.VMEM((2 * seats, full), BF16),
        pltpu.VMEM((seats, width), F32),
        pltpu.VMEM((seats, width), F32),
        pltpu.VMEM((2 * seats, width), F32),
        pltpu.VMEM((2 * seats, width), F32),
        pltpu.VMEM((2 * seats, width), F32),
        pltpu.VMEM((2 * seats, width), F32),
        pltpu.VMEM((2, cols, LANES), F32),
        pltpu.VMEM((4, cols, LANES), F32),
        pltpu.SMEM((elems, nbrs), jnp.int32),
        pltpu.SMEM((stats,), jnp.int32),
        pltpu.SemaphoreType.DMA((elems + 4,)),
        pltpu.SemaphoreType.DMA((copies,)),
        pltpu.SemaphoreType.DMA((copies,)),
    ]
    anywhere = pl.BlockSpec(memory_space=pl.ANY)
    vmem = pl.BlockSpec(memory_space=pltpu.VMEM)
    hess, gram = pl.pallas_call(
        functools.partial(kernel, sizes),
        out_shape=(
            jax.ShapeDtypeStruct((elems, cols, order // 2), F32),
            jax.ShapeDtypeStruct((cols, slots * cols), F32),
        ),
        in_specs=[anywhere] * 5,
        out_specs=(vmem, vmem),
        scratch_shapes=scratch,
        compiler_params=pltpu.CompilerParams(
            collective_id=0, has_side_effects=True, vmem_limit_bytes=56 * 1024 * 1024
        ),
    )(neighbors, stations, probes.transpose(1, 0, 2), jacobian, obs_weights)
    hess, gram = pl.pallas_call(
        hand_over,
        out_shape=(
            jax.ShapeDtypeStruct(hess.shape, F32),
            jax.ShapeDtypeStruct((cols, n_col * cols), F32),
        ),
        in_specs=[vmem, vmem],
        out_specs=(vmem, vmem),
    )(hess, gram)
    return hess.transpose(1, 0, 2), gram


def solution(mesh):
    in_specs = (
        P("col", "elem", None),
        P("sec", "elem", None, None, None),
        P("elem", None),
        P("elem"),
        P("elem", None),
    )
    out_specs = (P("col", "elem", "sec"), P("col", None))
    body = functools.partial(per_device, mesh.shape["elem"], mesh.shape["col"])
    return jax.shard_map(
        body, mesh=mesh, in_specs=in_specs, out_specs=out_specs, check_vma=False
    )
```

```python
import functools
import math

import jax
import jax.numpy as jnp
from jax import lax
from jax.experimental import pallas as pl
from jax.experimental.pallas import tpu as pltpu
from jax.sharding import PartitionSpec as P

STEPS = 2
MESH = pl.DeviceIdType.MESH
F32 = jnp.float32
BF16 = jnp.bfloat16
LANES = 128


def halves(value):
    high = value.astype(BF16)
    low = (value - high.astype(F32)).astype(BF16)
    return high, low


def product(a, b, transposed):
    dims = (((1,), (1 if transposed else 0,)), ((), ()))
    return lax.dot_general(a, b, dims, preferred_element_type=F32)


def product3(stack, high, low, transposed):
    rows = stack.shape[0] // 2
    first = product(stack, high, transposed)
    second = product(stack[:rows], low, transposed)
    return first[:rows] + (first[rows:] + second)


def kernel(
    sizes,
    neighbors_hbm,
    stations_hbm,
    probes_hbm,
    jacobian_hbm,
    weights_hbm,
    hess_ref,
    gram_ref,
    *scratch,
):
    cols, elems, order, nbrs, stats, n_elem, n_col = sizes
    radius = (nbrs - 1) // 2
    width = radius * order
    half = order // 2
    seats = LANES // 2
    jac_f32 = scratch[:elems]
    jac_high = scratch[elems : 2 * elems]
    jac_low = scratch[2 * elems : 3 * elems]
    (
        probes_ref, weights_ref, state, field, halo_left, halo_right,
        adjoint, adjoint_in, observed, out_left, out_right, back_left, back_right,
        out_half, back_half, readings, partial, partial_in, upper, upper_in,
        u_high, u_low, placed_field, once, once_field, once_halo, once_left, once_right,
        spill_left, spill_right, spill_in_left, spill_in_right,
        answer_out, answer_in, answer_far, answer_far_in, neighbors, stations,
        load_sem, send_sem, recv_sem,
    ) = scratch[3 * elems :]
    section = lax.axis_index("sec")
    column = lax.axis_index("col")
    block = lax.axis_index("elem")
    left = lax.rem(block + n_elem - 1, n_elem)
    right = lax.rem(block + 1, n_elem)
    even = lax.rem(block, 2) == 0
    far = jnp.where(even, left, right)
    other = 1 - section
    first_elem = block * elems
    elem_total = elems * n_elem
    rounds = int(math.log2(n_elem))
    edge = radius + elems
    full = elems * order
    last = STEPS - 1
    LEFT, RIGHT = 0, 1
    neighbour = (left, right)
    halo_in = (halo_left, halo_right)
    out = (out_left, out_right)
    back = (back_left, back_right)
    once_in = (once_left, once_right)
    spill = (spill_left, spill_right)
    spill_in = (spill_in_left, spill_in_right)
    own_rows = (slice(seats, 2 * seats), slice(0, seats))
    other_rows = (slice(0, seats), slice(seats, 2 * seats))
    own = (slice(0, width), slice(full - width, full))
    own_ds = (pl.ds(0, width), pl.ds(full - width, width))
    own_elems = (range(0, radius), range(elems - radius, elems))
    own_span = ((radius, 2 * radius), (edge - radius, edge))

    def by_parity(run):
        @pl.when(even)
        def _():
            run(RIGHT, LEFT)

        @pl.when(jnp.logical_not(even))
        def _():
            run(LEFT, RIGHT)

    probe_load = pltpu.make_async_copy(probes_hbm, probes_ref, load_sem.at[elems])
    probe_load.start()
    table_loads = [
        pltpu.make_async_copy(neighbors_hbm, neighbors, load_sem.at[elems + 2]),
        pltpu.make_async_copy(stations_hbm, stations, load_sem.at[elems + 3]),
    ]
    for load in table_loads:
        load.start()
    weights_load = pltpu.make_async_copy(
        weights_hbm, weights_ref.at[pl.ds(0, stats)], load_sem.at[elems + 1]
    )
    weights_load.start()
    jac_loads = [
        pltpu.make_async_copy(jacobian_hbm.at[0, e], jac_f32[e], load_sem.at[e])
        for e in range(elems)
    ]
    for load in jac_loads:
        load.start()

    barrier = pltpu.get_barrier_semaphore()
    partners = [{"elem": left}, {"elem": right}, {"sec": other}, {"sec": other, "elem": far}]
    partners += [{"col": lax.rem(column + j, n_col)} for j in range(1, n_col)]
    flips = []
    for r in range(rounds):
        bit = 1 << r
        upper_bit = lax.rem(block // bit, 2)
        flips.append({"elem": block + bit - 2 * bit * upper_bit})
    second_left = lax.rem(block + n_elem - 2, n_elem)
    second_right = lax.rem(block + 2, n_elem)
    partners += [{"elem": second_left}, {"elem": second_right}]
    for partner in partners + flips:
        pl.semaphore_signal(barrier, inc=1, device_id=partner, device_id_type=MESH)

    probe_load.wait()

    @pl.when(section == 0)
    def _():
        for e in range(elems):
            state[0, :, e * order : (e + 1) * order] = probes_ref[e]

    pl.semaphore_wait(barrier, len(partners) + len(flips))

    def remote(src, dst, index, target, arrival=None):
        arrival = index if arrival is None else arrival
        return pltpu.make_async_remote_copy(
            src_ref=src, dst_ref=dst, send_sem=send_sem.at[index],
            recv_sem=recv_sem.at[arrival], device_id=target, device_id_type=MESH,
        )

    FORWARD = 4 * STEPS
    BACKWARD, UPPER = FORWARD + 2, FORWARD + 4
    ACROSS, GRAM, LOWER, HIGHER, READ = (FORWARD + 6 + i for i in range(5))
    FLIP = READ + n_col - 1
    ONCE = FLIP + rounds
    ANSWER = ONCE + 2
    SPILL = ANSWER + 4

    def halo_copy(t, side):
        return remote(
            state.at[t, :, own_ds[side]], halo_in[1 - side].at[t], 2 * t + side,
            {"elem": neighbour[side]},
        )

    def halo_across(side):
        return remote(
            state.at[STEPS, :, own_ds[side]], halo_in[1 - side].at[0], ACROSS,
            {"sec": other, "elem": neighbour[side]}, side,
        )

    def forward(side):
        return remote(
            state.at[STEPS, :, own_ds[side]], state.at[0, :, own_ds[side]],
            FORWARD + side, {"sec": other},
        )

    def out_copy(t, side):
        return remote(
            out[side].at[t], back[1 - side].at[t], 2 * STEPS + 2 * t + side,
            {"elem": neighbour[side]},
        )

    def spill_copy(side, first):
        rows = own_rows[side] if first else other_rows[side]
        rows = pl.ds(rows.start, seats)
        return remote(
            spill[side].at[rows], spill_in[1 - side].at[rows], SPILL + 2 * side + int(first),
            {"elem": neighbour[side]},
        )

    def once_copy(side):
        start = 0 if side == LEFT else width + full
        return remote(
            once.at[:, pl.ds(start, width)], once_in[1 - side], ONCE + side,
            {"elem": neighbour[side]},
        )

    answer_copies = [
        remote(source.at[part], target.at[slot], ANSWER + index, {"elem": place})
        for index, (source, target, part, slot, place) in enumerate(
            (
                (answer_out, answer_in, 1, 0, right),
                (answer_out, answer_in, 0, 1, left),
                (answer_far, answer_far_in, 1, 0, second_right),
                (answer_far, answer_far_in, 0, 1, second_left),
            )
        )
    ]

    def backward(side):
        return remote(
            adjoint.at[STEPS, :, own_ds[side]], adjoint_in.at[:, own_ds[side]],
            BACKWARD + side, {"sec": other},
        )

    def half_copy(part, side):
        return remote(
            out_half.at[part], back_half, (LOWER, HIGHER)[part],
            {"sec": section if part == 0 else other, "elem": neighbour[side]},
        )

    def up(side):
        rows = pl.ds(own_elems[side].start, radius)
        return remote(upper.at[rows], upper_in.at[rows], UPPER + side, {"sec": other})

    @pl.when(section == 0)
    def _():
        halo_copy(0, LEFT).start()
        halo_copy(0, RIGHT).start()

    for load in table_loads:
        load.wait()

    def split(e, d, use):
        target = lax.rem(first_elem + e + d - radius + elem_total, elem_total)
        slot = jnp.int32(0)
        for k in range(1, nbrs):
            slot = jnp.where(neighbors[e, k] == target, jnp.int32(k), slot)
        high, low = halves(jac_f32[e][slot])
        jac_high[e][:, d * order : (d + 1) * order] = high
        jac_low[e][:, d * order : (d + 1) * order] = low
        use(e + d - radius, high, low)

    lane_ids = lax.broadcasted_iota(jnp.int32, (cols, LANES), 1)

    def take_weights():
        weights_load.wait()
        if weights_ref.shape[0] > stats:
            weights_ref[stats:, :] = jnp.zeros((weights_ref.shape[0] - stats, order), F32)

    def put_field(start, value):
        high, low = halves(value)
        field[:cols, start : start + value.shape[1]] = high
        field[cols:, start : start + value.shape[1]] = low

    def blocks(ref, begin, end):
        return ref[:, begin * order : end * order]

    def gathered(e, low, high):
        return product3(
            blocks(field, low, high), blocks(jac_high[e], low - e, high - e),
            blocks(jac_low[e], low - e, high - e), True,
        )

    def here(e):
        return slice(e * order, (e + 1) * order)

    def advance(t, side):
        ends = [(e, max(e, radius), min(e + nbrs, edge)) for e in own_elems[side]]
        ends.sort(key=lambda span: span[2] - span[1])
        e, low, high = ends.pop()
        middle = (low + high) // 2
        spans = [ends[1], ends[0], (e, low, middle), (e, middle, high)]
        for i, (e, low, high) in enumerate(spans):
            before = state[t + 1 if i == 3 else t, :, here(e)]
            state[t + 1, :, here(e)] = before + gathered(e, low, high)

    def finish_tangent(t, side, away):
        halo_copy(t, 1 - side).wait_recv()
        put_field(0 if side == LEFT else width + full, halo_in[side][t])
        for e in (own_elems[side][1], own_elems[side][0], own_elems[side][2]):
            span = (e, radius) if side == LEFT else (edge, e + nbrs)
            state[t + 1, :, here(e)] = state[t + 1, :, here(e)] + gathered(e, *span)
        if t < last:
            halo_copy(t + 1, side).start()
        else:
            forward(side).start()
            if away:
                halo_across(side).start()

    def tangent(t, core, away):
        if t > 0:
            put_field(width, state[t])
        for side in (away, core) if t == 0 else (core, away):
            if t > 0:
                advance(t, side)
            finish_tangent(t, side, side == away)

    @pl.when(section == 0)
    def _():
        put_field(width, state[0])
        for pair in range(0, elems, 2):
            terms = {}
            for e in range(pair, pair + 2):
                jac_loads[e].wait()

            def use(e, m, high, low):
                if 0 <= m < elems:
                    source = blocks(field, m + radius, m + radius + 1)
                    both = product(source, high, True), product(source[:cols], low, True)
                    for i in range(2):
                        terms[e, i] = terms[e, i] + both[i] if (e, i) in terms else both[i]

            for d in range(nbrs):
                for e in range(pair, pair + 2):
                    split(e, d, functools.partial(use, e))
            for e in range(pair, pair + 2):
                added = terms[e, 0][:cols] + (terms[e, 0][cols:] + terms[e, 1])
                state[1, :, here(e)] = state[0, :, here(e)] + added
        for t in range(STEPS):
            by_parity(functools.partial(tangent, t))

    def by_block(source, rows, elements, m):
        first, second = None, None
        for e in elements:
            if abs(m - e) > radius:
                continue
            low = m - e + radius
            up_term = product(source[:, here(e)], blocks(jac_high[e], low, low + 1), False)
            low_term = product(source[:rows, here(e)], blocks(jac_low[e], low, low + 1), False)
            first = up_term if first is None else first + up_term
            second = low_term if second is None else second + low_term
        return first[:rows] + (first[rows:] + second)

    def there(m):
        return slice((m + radius) * order, (m + radius + 1) * order)

    def put_rows(start, m, value):
        high, low = halves(value)
        u_high[start : start + seats, there(m)] = high
        u_low[start : start + seats, there(m)] = low

    def station_products():
        take_weights()
        u_high[...] = jnp.zeros(u_high.shape, BF16)
        u_low[...] = jnp.zeros(u_low.shape, BF16)
        row_ids = lax.broadcasted_iota(jnp.int32, (seats, order), 0)
        station_col = jnp.full((seats, order), -1, jnp.int32)
        for i in range(stats):
            station_col = jnp.where(row_ids == i, stations[i], station_col)

        def placed(e):
            return jnp.where(station_col == first_elem + e, weights_ref[:seats, :], 0.0)

        for e in range(elems):
            high, low = halves(placed(e))
            placed_field[:seats, here(e)] = high
            placed_field[seats:, here(e)] = low

        for e in range(elems):
            jac_loads[e].wait()

            def use(m, high, low, e=e):
                source = placed_field[:, here(e)]
                first = product(source, high, False)
                value = first[seats:] + product(source[:seats], low, False)
                value = first[:seats] + value
                if m == e:
                    value = value + placed(e)
                if e > 0 and m < e + radius:
                    value = value + once[:, there(m)]
                once[:, there(m)] = value

            for d in range(nbrs):
                split(e, d, use)
            if e == radius - 1:
                once_copy(LEFT).start()
        once_copy(RIGHT).start()
        for m in range(elems):
            high, low = halves(once[:, there(m)])
            once_field[:seats, here(m)] = high
            once_field[seats:, here(m)] = low
        for side, span in ((LEFT, range(-radius, 0)), (RIGHT, range(elems, elems + radius))):
            for j, m in enumerate(span):
                value = by_block(once_field, seats, range(elems), m)
                put_rows(seats, m, value)
                spill[side][own_rows[side], here(j)] = value
            spill_copy(side, True).start()
        for m in range(elems):
            value = by_block(once_field, seats, range(elems), m)
            put_rows(seats, m, value + once[:, there(m)])
        for side in (LEFT, RIGHT):
            once_copy(1 - side).wait_recv()
            high, low = halves(once_in[side][...])
            once_halo[:seats, own[side]] = high
            once_halo[seats:, own[side]] = low
            reach = own_elems[side]
            outside = range(-radius, 0) if side == LEFT else range(elems, elems + radius)
            for j, m in enumerate(outside):
                value = by_block(once_halo, seats, reach, m)
                put_rows(0 if side == LEFT else 3 * seats, m, value)
                spill[side][other_rows[side], here(j)] = value
            spill_copy(side, False).start()
            for m in range(elems):
                if m - reach.stop >= radius or reach.start - m > radius:
                    continue
                value = by_block(once_halo, seats, reach, m)
                if m in reach:
                    value = value + once_in[side][:, here(m - reach.start)]
                put_rows(0 if side == LEFT else 3 * seats, m, value)

    def merge(side):
        for part in (True, False):
            spill_copy(1 - side, part).wait_recv()
        starts = (0, seats) if side == LEFT else (seats, 3 * seats)
        for i in range(2):
            rows = slice(starts[i], starts[i] + seats)
            for j, m in enumerate(own_elems[side]):
                value = u_high[rows, there(m)].astype(F32) + u_low[rows, there(m)].astype(F32)
                value = value + spill_in[side][i * seats : (i + 1) * seats, here(j)]
                put_rows(starts[i], m, value)

    def lanes_of(side, halo):
        if halo:
            start = 0 if side == LEFT else width + full
        else:
            start = width + own[side].start
        return slice(start, start + width)

    def answered(value, lanes):
        stack = jnp.concatenate(halves(value), axis=0)
        return product3(stack, u_high[:, lanes], u_low[:, lanes], True)

    def packed(value, keep):
        rows = cols // 2
        return jnp.where(keep, value[:rows], pltpu.roll(value[rows:], seats, 1))

    def unpacked(value):
        return jnp.concatenate([value, pltpu.roll(value, seats, 1)], axis=0)

    for slot in range(n_col, readings.shape[0]):
        readings[slot] = jnp.zeros((cols, LANES), F32)
    read_copies = [
        remote(
            readings.at[column], readings.at[column], READ + j - 1,
            {"col": lax.rem(column + j, n_col)},
        )
        for j in range(1, n_col)
    ]
    flip_copies = [
        remote(partial.at[r], partial_in.at[r], FLIP + r, flips[r]) for r in range(rounds)
    ]
    gram_copy = remote(partial.at[rounds], partial_in.at[rounds], GRAM, {"sec": other})

    def share(reading):
        readings[column] = reading
        for copy in read_copies:
            copy.start()

    def begin_projection():
        for copy in read_copies:
            copy.wait_recv()
        everyone = readings[...].reshape(readings.shape[0] * cols, LANES)
        high, low = halves(everyone)
        stack = jnp.concatenate(halves(readings[column]), axis=0)
        partial[0] = product3(stack, high, low, True)
        flip_copies[0].start()

    def end_projection():
        for r in range(rounds):
            flip_copies[r].wait_recv()
            partial[r + 1] = partial[r] + partial_in[r]
            if r + 1 < rounds:
                flip_copies[r + 1].start()
        gram_copy.start()

    def respond(core, away):
        total = None
        for side in (core, away):
            forward(side).wait_recv()
            if side == core:
                halo_copy(0, core).start()
            part = answered(state[0, :, own[side]], lanes_of(side, False))
            total = part if total is None else total + part
            halo_copy(0, 1 - side).wait_recv()
            total = total + answered(halo_in[side][0], lanes_of(side, True))
        near = lane_ids < seats
        to_left = total[:, :LANES]
        to_right = total[:, LANES:] + jnp.where(near, pltpu.roll(to_left, seats, 1), 0.0)
        answer_out[0] = to_left
        answer_out[1] = to_right
        near_half = near[: cols // 2]
        answer_far[0] = packed(to_left, near_half)
        answer_far[1] = packed(to_right, jnp.logical_not(near_half))
        for copy in answer_copies:
            copy.start()
        for side in (core, away):
            merge(side)
        for copy in answer_copies:
            copy.wait_recv()
        from_left, from_right = answer_in[0], answer_in[1]
        beyond_left, beyond_right = unpacked(answer_far_in[0]), unpacked(answer_far_in[1])
        upper_half = from_left + to_left
        upper_half = upper_half + pltpu.roll(jnp.where(near, from_right, beyond_left), seats, 1)
        lower = from_right + to_right
        lower = lower + pltpu.roll(jnp.where(near, beyond_right, from_left), seats, 1)
        share(jnp.where(near, lower, 0.0))
        stack = jnp.concatenate(halves(jnp.concatenate([upper_half, lower], axis=1)), axis=0)
        for side in (away, core):
            lanes = lanes_of(side, False)
            answer = product3(stack, u_high[:, lanes], u_low[:, lanes], False)
            adjoint[STEPS, :, own[side]] = answer
            if side == core:
                begin_projection()
                backward(away).wait_send()
            backward(side).start()
        end_projection()

    @pl.when(section == 1)
    def _():
        station_products()
        by_parity(respond)

    @pl.when(section == 0)
    def _():
        take_weights()
        weights_high, weights_low = halves(weights_ref[...])
        station_row = jnp.full((cols, LANES), -1, jnp.int32)
        for i in range(stats):
            station_row = jnp.where(lane_ids == i, stations[i], station_row)
        reading = jnp.zeros((cols, LANES), F32)
        for e in range(elems):
            stack = jnp.concatenate(halves(state[STEPS, :, here(e)]), axis=0)
            read = product3(stack, weights_high, weights_low, True)
            read = jnp.where(station_row == first_elem + e, read, 0.0)
            reading = reading + read
            stack = jnp.concatenate(halves(read), axis=0)
            observed[:, here(e)] = product3(stack, weights_high, weights_low, False)
        share(reading)
        begin_projection()
        end_projection()

    def send_out(t, side, away):
        put_field(own[side].start, adjoint[t, :, own[side]])
        ref = out[side]
        start = -radius if side == LEFT else elems
        for j in range(radius):
            value = by_block(field, cols, own_elems[side], start + j)
            if t == last and away:
                for part in range(2):
                    half_lanes = slice(part * half, (part + 1) * half)
                    out_half[part, :, j * half : (j + 1) * half] = value[:, half_lanes]
            else:
                ref[t, :, here(j)] = value
        if t == last and away:
            for part in range(2):
                half_copy(part, side).start()
        else:
            out_copy(t, side).start()

    def inner(t, side, first):
        for m in range(elems):
            value = by_block(field, cols, own_elems[side], m)
            if m in own_elems[side]:
                value = value + adjoint[t, :, here(m)]
            if not first:
                value = value + adjoint[t + 1, :, here(m)]
            adjoint[t + 1, :, here(m)] = value

    def add_back(t, side):
        lanes = own[side]
        out_copy(t, 1 - side).wait_recv()
        adjoint[t + 1, :, lanes] = adjoint[t + 1, :, lanes] + back[side][t]

    def send_up(side):
        for e in own_elems[side]:
            upper[e] = adjoint[STEPS, :, e * order + half : (e + 1) * order]
        up(side).start()

    def lower_half(e):
        return adjoint[STEPS, :, e * order : e * order + half]

    def adjoint_step(t, core, away):
        order_of_sides = (away, core) if t == 0 else (core, away)
        for side in order_of_sides:
            if t == 0:
                lanes = own[side]
                backward(side).wait_recv()
                total = adjoint_in[:, lanes] + observed[:, lanes]
                adjoint[0, :, lanes] = total
            else:
                add_back(t - 1, side)
            send_out(t, side, side == away)
            inner(t, side, side == order_of_sides[0])
        if t == last:
            send_up(away)
            add_back(t, core)
            send_up(core)
            for e in own_elems[core]:
                hess_ref[e] = lower_half(e)
            half_copy(0, 1 - away).wait_recv()
            for j, e in enumerate(own_elems[away]):
                hess_ref[e] = lower_half(e) + back_half[:, j * half : (j + 1) * half]

    @pl.when(section == 0)
    def _():
        for t in range(STEPS):
            by_parity(functools.partial(adjoint_step, t))

    gram_copy.wait_recv()
    scale = 1.0 / (elem_total * order)
    gram_ref[...] = (partial[rounds] + partial_in[rounds]) * scale

    def close(core, away):
        @pl.when(section == 0)
        def _():
            for t in range(STEPS):
                for side in (core, away):
                    halo_copy(t, side).wait_send()
                    if t < last or side == core:
                        out_copy(t, side).wait_send()
            halo_across(away).wait_send()
            for side in (core, away):
                forward(side).wait_send()
                up(side).wait_send()
            for part in range(2):
                half_copy(part, away).wait_send()

        @pl.when(section == 1)
        def _():
            halo_copy(0, core).wait_send()
            for copy in answer_copies:
                copy.wait_send()
            for side in (core, away):
                once_copy(side).wait_send()
                for part in (True, False):
                    spill_copy(side, part).wait_send()
                if side == core:
                    backward(side).wait_send()
                up(side).wait_recv()
            for e in own_elems[core]:
                hess_ref[e] = upper_in[e]
            half_copy(1, 1 - away).wait_recv()
            for j, e in enumerate(own_elems[away]):
                hess_ref[e] = upper_in[e] + back_half[:, j * half : (j + 1) * half]

    by_parity(close)
    gram_copy.wait_send()
    for copy in read_copies + flip_copies:
        copy.wait_send()


def hand_over(hess_ref, gram_ref, hess_out, gram_out):
    hess_out[...] = hess_ref[...]
    gram_out[...] = gram_ref[:, : gram_out.shape[1]]


def per_device(n_elem, n_col, probes, jacobian, neighbors, stations, obs_weights):
    cols, elems, order = probes.shape
    nbrs = neighbors.shape[1]
    stats = stations.shape[0]
    radius = (nbrs - 1) // 2
    rounds = int(math.log2(n_elem))
    slots = max(n_col, LANES // cols)
    sizes = (cols, elems, order, nbrs, stats, n_elem, n_col)
    full, width = elems * order, radius * order
    copies = 4 * STEPS + 20 + (n_col - 1) + rounds
    seats = LANES // 2
    scratch = [pltpu.VMEM((nbrs, order, order), F32)] * elems
    scratch += [pltpu.VMEM((order, nbrs * order), BF16)] * (2 * elems)
    scratch += [
        pltpu.VMEM((elems, cols, order), F32),
        pltpu.VMEM((LANES, order), F32),
        pltpu.VMEM((STEPS + 1, cols, full), F32),
        pltpu.VMEM((2 * cols, full + 2 * width), BF16),
        pltpu.VMEM((STEPS, cols, width), F32),
        pltpu.VMEM((STEPS, cols, width), F32),
        pltpu.VMEM((STEPS + 1, cols, full), F32),
        pltpu.VMEM((cols, full), F32),
        pltpu.VMEM((cols, full), F32),
        pltpu.VMEM((STEPS, cols, width), F32),
        pltpu.VMEM((STEPS, cols, width), F32),
        pltpu.VMEM((STEPS, cols, width), F32),
        pltpu.VMEM((STEPS, cols, width), F32),
        pltpu.VMEM((2, cols, width // 2), F32),
        pltpu.VMEM((cols, width // 2), F32),
        pltpu.VMEM((slots, cols, LANES), F32),
        pltpu.VMEM((rounds + 1, cols, slots * cols), F32),
        pltpu.VMEM((rounds + 1, cols, slots * cols), F32),
        pltpu.VMEM((elems, cols, order // 2), F32),
        pltpu.VMEM((elems, cols, order // 2), F32),
        pltpu.VMEM((4 * seats, full + 2 * width), BF16),
        pltpu.VMEM((4 * seats, full + 2 * width), BF16),
        pltpu.VMEM((2 * seats, full), BF16),
        pltpu.VMEM((seats, full + 2 * width), F32),
        pltpu.VMEM((2 * seats, full), BF16),
        pltpu.VMEM((2 * seats, full), BF16),
        pltpu.VMEM((seats, width), F32),
        pltpu.VMEM((seats, width), F32),
        pltpu.VMEM((2 * seats, width), F32),
        pltpu.VMEM((2 * seats, width), F32),
        pltpu.VMEM((2 * seats, width), F32),
        pltpu.VMEM((2 * seats, width), F32),
        pltpu.VMEM((2, cols, LANES), F32),
        pltpu.VMEM((2, cols, LANES), F32),
        pltpu.VMEM((2, cols // 2, LANES), F32),
        pltpu.VMEM((2, cols // 2, LANES), F32),
        pltpu.SMEM((elems, nbrs), jnp.int32),
        pltpu.SMEM((stats,), jnp.int32),
        pltpu.SemaphoreType.DMA((elems + 4,)),
        pltpu.SemaphoreType.DMA((copies,)),
        pltpu.SemaphoreType.DMA((copies,)),
    ]
    anywhere = pl.BlockSpec(memory_space=pl.ANY)
    vmem = pl.BlockSpec(memory_space=pltpu.VMEM)
    hess, gram = pl.pallas_call(
        functools.partial(kernel, sizes),
        out_shape=(
            jax.ShapeDtypeStruct((elems, cols, order // 2), F32),
            jax.ShapeDtypeStruct((cols, slots * cols), F32),
        ),
        in_specs=[anywhere] * 5,
        out_specs=(vmem, vmem),
        scratch_shapes=scratch,
        compiler_params=pltpu.CompilerParams(
            collective_id=0, has_side_effects=True, vmem_limit_bytes=56 * 1024 * 1024
        ),
    )(neighbors, stations, probes.transpose(1, 0, 2), jacobian, obs_weights)
    hess, gram = pl.pallas_call(
        hand_over,
        out_shape=(
            jax.ShapeDtypeStruct(hess.shape, F32),
            jax.ShapeDtypeStruct((cols, n_col * cols), F32),
        ),
        in_specs=[vmem, vmem],
        out_specs=(vmem, vmem),
    )(hess, gram)
    return hess.transpose(1, 0, 2), gram


def solution(mesh):
    in_specs = (
        P("col", "elem", None),
        P("sec", "elem", None, None, None),
        P("elem", None),
        P("elem"),
        P("elem", None),
    )
    out_specs = (P("col", "elem", "sec"), P("col", None))
    body = functools.partial(per_device, mesh.shape["elem"], mesh.shape["col"])
    return jax.shard_map(
        body, mesh=mesh, in_specs=in_specs, out_specs=out_specs, check_vma=False
    )
```

```python
import functools
import math

import jax
import jax.numpy as jnp
from jax import lax
from jax.experimental import pallas as pl
from jax.experimental.pallas import tpu as pltpu
from jax.sharding import PartitionSpec as P

STEPS = 2
MESH = pl.DeviceIdType.MESH
F32 = jnp.float32
BF16 = jnp.bfloat16
LANES = 128


def halves(value):
    high = value.astype(BF16)
    low = (value - high.astype(F32)).astype(BF16)
    return high, low


def product(a, b, transposed):
    dims = (((1,), (1 if transposed else 0,)), ((), ()))
    return lax.dot_general(a, b, dims, preferred_element_type=F32)


def product3(stack, high, low, transposed):
    rows = stack.shape[0] // 2
    first = product(stack, high, transposed)
    second = product(stack[:rows], low, transposed)
    return first[:rows] + (first[rows:] + second)


def kernel(
    sizes,
    neighbors_hbm,
    stations_hbm,
    probes_hbm,
    jacobian_hbm,
    weights_hbm,
    hess_ref,
    gram_ref,
    *scratch,
):
    cols, elems, order, nbrs, stats, n_elem, n_col = sizes
    radius = (nbrs - 1) // 2
    width = radius * order
    half = order // 2
    seats = LANES // 2
    jac_f32 = scratch[:elems]
    jac_high = scratch[elems : 2 * elems]
    jac_low = scratch[2 * elems : 3 * elems]
    (
        probes_ref, weights_ref, state, field, halo_left, halo_right,
        adjoint, adjoint_in, observed, out_left, out_right, back_left, back_right,
        out_half, back_half, readings, partial, partial_in, upper, upper_in,
        u_high, u_low, placed_field, once, once_field, once_halo, once_left, once_right,
        spill_left, spill_right, spill_in_left, spill_in_right,
        answer_out, answer_in, answer_far, answer_far_in, neighbors, stations,
        lower_part,
        load_sem, send_sem, recv_sem,
    ) = scratch[3 * elems :]
    section = lax.axis_index("sec")
    column = lax.axis_index("col")
    block = lax.axis_index("elem")
    left = lax.rem(block + n_elem - 1, n_elem)
    right = lax.rem(block + 1, n_elem)
    even = lax.rem(block, 2) == 0
    far = jnp.where(even, left, right)
    other = 1 - section
    first_elem = block * elems
    elem_total = elems * n_elem
    rounds = int(math.log2(n_elem))
    edge = radius + elems
    full = elems * order
    last = STEPS - 1
    LEFT, RIGHT = 0, 1
    neighbour = (left, right)
    halo_in = (halo_left, halo_right)
    out = (out_left, out_right)
    back = (back_left, back_right)
    once_in = (once_left, once_right)
    spill = (spill_left, spill_right)
    spill_in = (spill_in_left, spill_in_right)
    own_rows = (slice(seats, 2 * seats), slice(0, seats))
    other_rows = (slice(0, seats), slice(seats, 2 * seats))
    own = (slice(0, width), slice(full - width, full))
    own_ds = (pl.ds(0, width), pl.ds(full - width, width))
    own_elems = (range(0, radius), range(elems - radius, elems))
    own_span = ((radius, 2 * radius), (edge - radius, edge))

    def by_parity(run):
        @pl.when(even)
        def _():
            run(RIGHT, LEFT)

        @pl.when(jnp.logical_not(even))
        def _():
            run(LEFT, RIGHT)

    probe_load = pltpu.make_async_copy(probes_hbm, probes_ref, load_sem.at[elems])
    probe_load.start()
    table_loads = [
        pltpu.make_async_copy(neighbors_hbm, neighbors, load_sem.at[elems + 2]),
        pltpu.make_async_copy(stations_hbm, stations, load_sem.at[elems + 3]),
    ]
    for load in table_loads:
        load.start()
    weights_load = pltpu.make_async_copy(
        weights_hbm, weights_ref.at[pl.ds(0, stats)], load_sem.at[elems + 1]
    )
    weights_load.start()
    jac_loads = [
        pltpu.make_async_copy(jacobian_hbm.at[0, e], jac_f32[e], load_sem.at[e])
        for e in range(elems)
    ]
    for load in jac_loads:
        load.start()

    barrier = pltpu.get_barrier_semaphore()
    partners = [{"elem": left}, {"elem": right}, {"sec": other}, {"sec": other, "elem": far}]
    partners += [{"col": lax.rem(column + j, n_col)} for j in range(1, n_col)]
    flips = []
    for r in range(rounds):
        bit = 1 << r
        upper_bit = lax.rem(block // bit, 2)
        flips.append({"elem": block + bit - 2 * bit * upper_bit})
    second_left = lax.rem(block + n_elem - 2, n_elem)
    second_right = lax.rem(block + 2, n_elem)
    partners += [{"elem": second_left}, {"elem": second_right}]
    for partner in partners + flips:
        pl.semaphore_signal(barrier, inc=1, device_id=partner, device_id_type=MESH)

    probe_load.wait()

    @pl.when(section == 0)
    def _():
        for e in range(elems):
            state[0, :, e * order : (e + 1) * order] = probes_ref[e]

    pl.semaphore_wait(barrier, len(partners) + len(flips))

    def remote(src, dst, index, target, arrival=None):
        arrival = index if arrival is None else arrival
        return pltpu.make_async_remote_copy(
            src_ref=src, dst_ref=dst, send_sem=send_sem.at[index],
            recv_sem=recv_sem.at[arrival], device_id=target, device_id_type=MESH,
        )

    FORWARD = 4 * STEPS
    BACKWARD, UPPER = FORWARD + 2, FORWARD + 4
    ACROSS, GRAM, LOWER, HIGHER, READ = (FORWARD + 6 + i for i in range(5))
    FLIP = READ + n_col - 1
    ONCE = FLIP + rounds
    ANSWER = ONCE + 2
    SPILL = ANSWER + 4
    PART = SPILL + 4

    def halo_copy(t, side):
        return remote(
            state.at[t, :, own_ds[side]], halo_in[1 - side].at[t], 2 * t + side,
            {"elem": neighbour[side]},
        )

    def halo_across(side):
        return remote(
            state.at[STEPS, :, own_ds[side]], halo_in[1 - side].at[0], ACROSS,
            {"sec": other, "elem": neighbour[side]}, side,
        )

    def forward(side):
        return remote(
            state.at[STEPS, :, own_ds[side]], state.at[0, :, own_ds[side]],
            FORWARD + side, {"sec": other},
        )

    def out_copy(t, side):
        return remote(
            out[side].at[t], back[1 - side].at[t], 2 * STEPS + 2 * t + side,
            {"elem": neighbour[side]},
        )

    def spill_copy(side, first):
        rows = own_rows[side] if first else other_rows[side]
        rows = pl.ds(rows.start, seats)
        return remote(
            spill[side].at[rows], spill_in[1 - side].at[rows], SPILL + 2 * side + int(first),
            {"elem": neighbour[side]},
        )

    def once_copy(side):
        start = 0 if side == LEFT else width + full
        return remote(
            once.at[:, pl.ds(start, width)], once_in[1 - side], ONCE + side,
            {"elem": neighbour[side]},
        )

    answer_copies = [
        remote(source.at[part], target.at[slot], ANSWER + index, {"elem": place})
        for index, (source, target, part, slot, place) in enumerate(
            (
                (answer_out, answer_in, 1, 0, right),
                (answer_out, answer_in, 0, 1, left),
                (answer_far, answer_far_in, 1, 0, second_right),
                (answer_far, answer_far_in, 0, 1, second_left),
            )
        )
    ]

    def backward_part(side, j):
        lanes = pl.ds(own[side].start + j * order, order)
        return remote(
            adjoint.at[STEPS, :, lanes], adjoint_in.at[:, lanes], PART + j, {"sec": other}
        )

    def backward(side):
        return remote(
            adjoint.at[STEPS, :, own_ds[side]], adjoint_in.at[:, own_ds[side]],
            BACKWARD + side, {"sec": other},
        )

    def half_copy(part, side):
        return remote(
            out_half.at[part], back_half, (LOWER, HIGHER)[part],
            {"sec": section if part == 0 else other, "elem": neighbour[side]},
        )

    def up(side):
        rows = pl.ds(own_elems[side].start, radius)
        return remote(upper.at[rows], upper_in.at[rows], UPPER + side, {"sec": other})

    @pl.when(section == 0)
    def _():
        halo_copy(0, LEFT).start()
        halo_copy(0, RIGHT).start()

    for load in table_loads:
        load.wait()

    def split(e, d, use):
        target = lax.rem(first_elem + e + d - radius + elem_total, elem_total)
        slot = jnp.int32(0)
        for k in range(1, nbrs):
            slot = jnp.where(neighbors[e, k] == target, jnp.int32(k), slot)
        high, low = halves(jac_f32[e][slot])
        jac_high[e][:, d * order : (d + 1) * order] = high
        jac_low[e][:, d * order : (d + 1) * order] = low
        use(e + d - radius, high, low)

    lane_ids = lax.broadcasted_iota(jnp.int32, (cols, LANES), 1)

    def take_weights():
        weights_load.wait()
        if weights_ref.shape[0] > stats:
            weights_ref[stats:, :] = jnp.zeros((weights_ref.shape[0] - stats, order), F32)

    def put_field(start, value):
        high, low = halves(value)
        field[:cols, start : start + value.shape[1]] = high
        field[cols:, start : start + value.shape[1]] = low

    def blocks(ref, begin, end):
        return ref[:, begin * order : end * order]

    def gathered(e, low, high):
        return product3(
            blocks(field, low, high), blocks(jac_high[e], low - e, high - e),
            blocks(jac_low[e], low - e, high - e), True,
        )

    def here(e):
        return slice(e * order, (e + 1) * order)

    def advance(t, side):
        ends = [(e, max(e, radius), min(e + nbrs, edge)) for e in own_elems[side]]
        ends.sort(key=lambda span: span[2] - span[1])
        e, low, high = ends.pop()
        middle = (low + high) // 2
        spans = [ends[1], ends[0], (e, low, middle), (e, middle, high)]
        for i, (e, low, high) in enumerate(spans):
            before = state[t + 1 if i == 3 else t, :, here(e)]
            state[t + 1, :, here(e)] = before + gathered(e, low, high)

    def finish_tangent(t, side, away):
        halo_copy(t, 1 - side).wait_recv()
        put_field(0 if side == LEFT else width + full, halo_in[side][t])
        for e in (own_elems[side][1], own_elems[side][0], own_elems[side][2]):
            span = (e, radius) if side == LEFT else (edge, e + nbrs)
            state[t + 1, :, here(e)] = state[t + 1, :, here(e)] + gathered(e, *span)
        if t < last:
            halo_copy(t + 1, side).start()
        else:
            forward(side).start()
            if away:
                halo_across(side).start()

    def tangent(t, core, away):
        if t > 0:
            put_field(width, state[t])
        for side in (LEFT, RIGHT) if t == 0 else (core, away):
            if t > 0:
                advance(t, side)
            finish_tangent(t, side, side == away)

    @pl.when(section == 0)
    def _():
        put_field(width, state[0])
        for pair in range(0, elems, 2):
            terms = {}
            for e in range(pair, pair + 2):
                jac_loads[e].wait()

            def use(e, m, high, low):
                if 0 <= m < elems:
                    source = blocks(field, m + radius, m + radius + 1)
                    both = product(source, high, True), product(source[:cols], low, True)
                    for i in range(2):
                        terms[e, i] = terms[e, i] + both[i] if (e, i) in terms else both[i]

            for d in range(nbrs):
                for e in range(pair, pair + 2):
                    split(e, d, functools.partial(use, e))
            for e in range(pair, pair + 2):
                added = terms[e, 0][:cols] + (terms[e, 0][cols:] + terms[e, 1])
                state[1, :, here(e)] = state[0, :, here(e)] + added
        for t in range(STEPS):
            by_parity(functools.partial(tangent, t))

    def by_block(source, rows, elements, m, part=None):
        first, second = None, None
        for e in elements:
            if abs(m - e) > radius:
                continue
            lanes = here(m - e + radius)
            if part is not None:
                lanes = slice(lanes.start + part * half, lanes.start + (part + 1) * half)
            up_term = product(source[:, here(e)], jac_high[e][:, lanes], False)
            low_term = product(source[:rows, here(e)], jac_low[e][:, lanes], False)
            first = up_term if first is None else first + up_term
            second = low_term if second is None else second + low_term
        return first[:rows] + (first[rows:] + second)

    def there(m):
        return slice((m + radius) * order, (m + radius + 1) * order)

    def put_rows(start, m, value):
        high, low = halves(value)
        u_high[start : start + seats, there(m)] = high
        u_low[start : start + seats, there(m)] = low

    def station_products():
        take_weights()
        u_high[...] = jnp.zeros(u_high.shape, BF16)
        u_low[...] = jnp.zeros(u_low.shape, BF16)
        row_ids = lax.broadcasted_iota(jnp.int32, (seats, order), 0)
        station_col = jnp.full((seats, order), -1, jnp.int32)
        for i in range(stats):
            station_col = jnp.where(row_ids == i, stations[i], station_col)

        def placed(e):
            return jnp.where(station_col == first_elem + e, weights_ref[:seats, :], 0.0)

        for e in range(elems):
            high, low = halves(placed(e))
            placed_field[:seats, here(e)] = high
            placed_field[seats:, here(e)] = low

        for e in range(elems):
            jac_loads[e].wait()

            def use(m, high, low, e=e):
                source = placed_field[:, here(e)]
                first = product(source, high, False)
                value = first[seats:] + product(source[:seats], low, False)
                value = first[:seats] + value
                if m == e:
                    value = value + placed(e)
                if e > 0 and m < e + radius:
                    value = value + once[:, there(m)]
                once[:, there(m)] = value

            for d in range(nbrs):
                split(e, d, use)
            if e == radius - 1:
                once_copy(LEFT).start()
        once_copy(RIGHT).start()
        for m in range(elems):
            high, low = halves(once[:, there(m)])
            once_field[:seats, here(m)] = high
            once_field[seats:, here(m)] = low
        for side, span in ((LEFT, range(-radius, 0)), (RIGHT, range(elems, elems + radius))):
            for j, m in enumerate(span):
                value = by_block(once_field, seats, range(elems), m)
                put_rows(seats, m, value)
                spill[side][own_rows[side], here(j)] = value
            spill_copy(side, True).start()
        for m in range(elems):
            value = by_block(once_field, seats, range(elems), m)
            put_rows(seats, m, value + once[:, there(m)])
        for side in (LEFT, RIGHT):
            once_copy(1 - side).wait_recv()
            high, low = halves(once_in[side][...])
            once_halo[:seats, own[side]] = high
            once_halo[seats:, own[side]] = low
            reach = own_elems[side]
            outside = range(-radius, 0) if side == LEFT else range(elems, elems + radius)
            for j, m in enumerate(outside):
                value = by_block(once_halo, seats, reach, m)
                put_rows(0 if side == LEFT else 3 * seats, m, value)
                spill[side][other_rows[side], here(j)] = value
            spill_copy(side, False).start()
            for m in range(elems):
                if m - reach.stop >= radius or reach.start - m > radius:
                    continue
                value = by_block(once_halo, seats, reach, m)
                if m in reach:
                    value = value + once_in[side][:, here(m - reach.start)]
                put_rows(0 if side == LEFT else 3 * seats, m, value)

    def merge(side):
        for part in (True, False):
            spill_copy(1 - side, part).wait_recv()
        starts = (0, seats) if side == LEFT else (seats, 3 * seats)
        for i in range(2):
            rows = slice(starts[i], starts[i] + seats)
            for j, m in enumerate(own_elems[side]):
                value = u_high[rows, there(m)].astype(F32) + u_low[rows, there(m)].astype(F32)
                value = value + spill_in[side][i * seats : (i + 1) * seats, here(j)]
                put_rows(starts[i], m, value)

    def lanes_of(side, halo):
        if halo:
            start = 0 if side == LEFT else width + full
        else:
            start = width + own[side].start
        return slice(start, start + width)

    def answered(value, lanes):
        stack = jnp.concatenate(halves(value), axis=0)
        return product3(stack, u_high[:, lanes], u_low[:, lanes], True)

    def packed(value, keep):
        rows = cols // 2
        return jnp.where(keep, value[:rows], pltpu.roll(value[rows:], seats, 1))

    def unpacked(value):
        return jnp.concatenate([value, pltpu.roll(value, seats, 1)], axis=0)

    for slot in range(n_col, readings.shape[0]):
        readings[slot] = jnp.zeros((cols, LANES), F32)
    read_copies = [
        remote(
            readings.at[column], readings.at[column], READ + j - 1,
            {"col": lax.rem(column + j, n_col)},
        )
        for j in range(1, n_col)
    ]
    flip_copies = [
        remote(partial.at[r], partial_in.at[r], FLIP + r, flips[r]) for r in range(rounds)
    ]
    gram_copy = remote(partial.at[rounds], partial_in.at[rounds], GRAM, {"sec": other})

    def share(reading):
        readings[column] = reading
        for copy in read_copies:
            copy.start()

    def begin_projection():
        for copy in read_copies:
            copy.wait_recv()
        everyone = readings[...].reshape(readings.shape[0] * cols, LANES)
        high, low = halves(everyone)
        stack = jnp.concatenate(halves(readings[column]), axis=0)
        partial[0] = product3(stack, high, low, True)
        flip_copies[0].start()

    def end_projection():
        for r in range(rounds):
            flip_copies[r].wait_recv()
            partial[r + 1] = partial[r] + partial_in[r]
            if r + 1 < rounds:
                flip_copies[r + 1].start()
        gram_copy.start()

    def respond(core, away):
        total = None
        for side in (core, away):
            forward(side).wait_recv()
            if side == core:
                halo_copy(0, core).start()
            part = answered(state[0, :, own[side]], lanes_of(side, False))
            total = part if total is None else total + part
            halo_copy(0, 1 - side).wait_recv()
            total = total + answered(halo_in[side][0], lanes_of(side, True))
        near = lane_ids < seats
        to_left = total[:, :LANES]
        to_right = total[:, LANES:] + jnp.where(near, pltpu.roll(to_left, seats, 1), 0.0)
        answer_out[0] = to_left
        answer_out[1] = to_right
        near_half = near[: cols // 2]
        answer_far[0] = packed(to_left, near_half)
        answer_far[1] = packed(to_right, jnp.logical_not(near_half))
        for copy in answer_copies:
            copy.start()
        for side in (core, away):
            merge(side)
        for copy in answer_copies:
            copy.wait_recv()
        from_left, from_right = answer_in[0], answer_in[1]
        beyond_left, beyond_right = unpacked(answer_far_in[0]), unpacked(answer_far_in[1])
        upper_half = from_left + to_left
        upper_half = upper_half + pltpu.roll(jnp.where(near, from_right, beyond_left), seats, 1)
        lower = from_right + to_right
        lower = lower + pltpu.roll(jnp.where(near, beyond_right, from_left), seats, 1)
        share(jnp.where(near, lower, 0.0))
        stack = jnp.concatenate(halves(jnp.concatenate([upper_half, lower], axis=1)), axis=0)
        for side in (away, core):
            lanes = lanes_of(side, False)
            answer = product3(stack, u_high[:, lanes], u_low[:, lanes], False)
            adjoint[STEPS, :, own[side]] = answer
            if side == away:
                for j in range(radius):
                    backward_part(away, j).start()
                backward_part(away, 1).wait_send()
            else:
                backward(core).start()
                begin_projection()
        end_projection()

    @pl.when(section == 1)
    def _():
        station_products()
        by_parity(respond)

    @pl.when(section == 0)
    def _():
        take_weights()
        weights_high, weights_low = halves(weights_ref[...])
        station_row = jnp.full((cols, LANES), -1, jnp.int32)
        for i in range(stats):
            station_row = jnp.where(lane_ids == i, stations[i], station_row)
        reading = jnp.zeros((cols, LANES), F32)
        for e in range(elems):
            stack = jnp.concatenate(halves(state[STEPS, :, here(e)]), axis=0)
            read = product3(stack, weights_high, weights_low, True)
            read = jnp.where(station_row == first_elem + e, read, 0.0)
            reading = reading + read
            stack = jnp.concatenate(halves(read), axis=0)
            observed[:, here(e)] = product3(stack, weights_high, weights_low, False)
        share(reading)
        begin_projection()
        end_projection()

    def send_out(t, side):
        put_field(own[side].start, adjoint[t, :, own[side]])
        start = -radius if side == LEFT else elems
        for j in range(radius):
            out[side][t, :, here(j)] = by_block(field, cols, own_elems[side], start + j)
        out_copy(t, side).start()

    def inner(t, side, first):
        for m in range(elems):
            value = by_block(field, cols, own_elems[side], m)
            if m in own_elems[side]:
                value = value + adjoint[t, :, here(m)]
            if not first:
                value = value + adjoint[t + 1, :, here(m)]
            adjoint[t + 1, :, here(m)] = value

    def add_back(t, side):
        lanes = own[side]
        out_copy(t, 1 - side).wait_recv()
        adjoint[t + 1, :, lanes] = adjoint[t + 1, :, lanes] + back[side][t]

    def finish(core, away):
        add_back(last - 1, away)
        put_field(own[away].start, adjoint[last, :, own[away]])
        start = -radius if away == LEFT else elems
        for j in range(radius):
            value = by_block(field, cols, own_elems[away], start + j)
            for part in range(2):
                half_lanes = slice(part * half, (part + 1) * half)
                out_half[part, :, j * half : (j + 1) * half] = value[:, half_lanes]
        for part in range(2):
            half_copy(part, away).start()
        for part in (1, 0):
            for side in (away, core):
                if side == core and part == 1:
                    out_copy(last, 1 - core).wait_recv()
                for j, m in enumerate(own_elems[side]):
                    lanes = slice(m * order + part * half, m * order + (part + 1) * half)
                    value = by_block(field, cols, own_elems[away], m, part)
                    value = value + adjoint[STEPS, :, lanes]
                    if side == away:
                        value = value + adjoint[last, :, lanes]
                    else:
                        inside = slice(j * order + part * half, j * order + (part + 1) * half)
                        value = value + back[core][last, :, inside]
                    if part == 1:
                        upper[m] = value
                    elif side == core:
                        hess_ref[m] = value
                    else:
                        lower_part[j] = value
                if part == 1:
                    up(side).start()
        half_copy(0, 1 - away).wait_recv()
        for j, e in enumerate(own_elems[away]):
            hess_ref[e] = lower_part[j] + back_half[:, j * half : (j + 1) * half]

    def adjoint_step(t, core, away):
        order_of_sides = (away, core) if t == 0 else (core, away)
        for side in order_of_sides:
            if t == last and side == away:
                finish(core, away)
                continue
            if t == 0:
                lanes = own[side]
                if side == away:
                    for j in range(radius):
                        backward_part(away, j).wait_recv()
                else:
                    backward(core).wait_recv()
                total = adjoint_in[:, lanes] + observed[:, lanes]
                adjoint[0, :, lanes] = total
            else:
                add_back(t - 1, side)
            send_out(t, side)
            inner(t, side, side == order_of_sides[0])

    @pl.when(section == 0)
    def _():
        for t in range(STEPS):
            by_parity(functools.partial(adjoint_step, t))

    gram_copy.wait_recv()
    scale = 1.0 / (elem_total * order)
    gram_ref[...] = (partial[rounds] + partial_in[rounds]) * scale

    def close(core, away):
        @pl.when(section == 0)
        def _():
            for t in range(STEPS):
                for side in (core, away):
                    halo_copy(t, side).wait_send()
                    if t < last or side == core:
                        out_copy(t, side).wait_send()
            halo_across(away).wait_send()
            for side in (core, away):
                forward(side).wait_send()
                up(side).wait_send()
            for part in range(2):
                half_copy(part, away).wait_send()

        @pl.when(section == 1)
        def _():
            halo_copy(0, core).wait_send()
            for j in range(radius):
                if j != 1:
                    backward_part(away, j).wait_send()
            for copy in answer_copies:
                copy.wait_send()
            for side in (core, away):
                once_copy(side).wait_send()
                for part in (True, False):
                    spill_copy(side, part).wait_send()
                if side == core:
                    backward(core).wait_send()
                up(side).wait_recv()
            for e in own_elems[core]:
                hess_ref[e] = upper_in[e]
            half_copy(1, 1 - away).wait_recv()
            for j, e in enumerate(own_elems[away]):
                hess_ref[e] = upper_in[e] + back_half[:, j * half : (j + 1) * half]

    by_parity(close)
    gram_copy.wait_send()
    for copy in read_copies + flip_copies:
        copy.wait_send()


def hand_over(hess_ref, gram_ref, hess_out, gram_out):
    hess_out[...] = hess_ref[...]
    gram_out[...] = gram_ref[:, : gram_out.shape[1]]


def per_device(n_elem, n_col, probes, jacobian, neighbors, stations, obs_weights):
    cols, elems, order = probes.shape
    nbrs = neighbors.shape[1]
    stats = stations.shape[0]
    radius = (nbrs - 1) // 2
    rounds = int(math.log2(n_elem))
    slots = max(n_col, LANES // cols)
    sizes = (cols, elems, order, nbrs, stats, n_elem, n_col)
    full, width = elems * order, radius * order
    copies = 4 * STEPS + 20 + radius + (n_col - 1) + rounds
    seats = LANES // 2
    scratch = [pltpu.VMEM((nbrs, order, order), F32)] * elems
    scratch += [pltpu.VMEM((order, nbrs * order), BF16)] * (2 * elems)
    scratch += [
        pltpu.VMEM((elems, cols, order), F32),
        pltpu.VMEM((LANES, order), F32),
        pltpu.VMEM((STEPS + 1, cols, full), F32),
        pltpu.VMEM((2 * cols, full + 2 * width), BF16),
        pltpu.VMEM((STEPS, cols, width), F32),
        pltpu.VMEM((STEPS, cols, width), F32),
        pltpu.VMEM((STEPS + 1, cols, full), F32),
        pltpu.VMEM((cols, full), F32),
        pltpu.VMEM((cols, full), F32),
        pltpu.VMEM((STEPS, cols, width), F32),
        pltpu.VMEM((STEPS, cols, width), F32),
        pltpu.VMEM((STEPS, cols, width), F32),
        pltpu.VMEM((STEPS, cols, width), F32),
        pltpu.VMEM((2, cols, width // 2), F32),
        pltpu.VMEM((cols, width // 2), F32),
        pltpu.VMEM((slots, cols, LANES), F32),
        pltpu.VMEM((rounds + 1, cols, slots * cols), F32),
        pltpu.VMEM((rounds + 1, cols, slots * cols), F32),
        pltpu.VMEM((elems, cols, order // 2), F32),
        pltpu.VMEM((elems, cols, order // 2), F32),
        pltpu.VMEM((4 * seats, full + 2 * width), BF16),
        pltpu.VMEM((4 * seats, full + 2 * width), BF16),
        pltpu.VMEM((2 * seats, full), BF16),
        pltpu.VMEM((seats, full + 2 * width), F32),
        pltpu.VMEM((2 * seats, full), BF16),
        pltpu.VMEM((2 * seats, full), BF16),
        pltpu.VMEM((seats, width), F32),
        pltpu.VMEM((seats, width), F32),
        pltpu.VMEM((2 * seats, width), F32),
        pltpu.VMEM((2 * seats, width), F32),
        pltpu.VMEM((2 * seats, width), F32),
        pltpu.VMEM((2 * seats, width), F32),
        pltpu.VMEM((2, cols, LANES), F32),
        pltpu.VMEM((2, cols, LANES), F32),
        pltpu.VMEM((2, cols // 2, LANES), F32),
        pltpu.VMEM((2, cols // 2, LANES), F32),
        pltpu.SMEM((elems, nbrs), jnp.int32),
        pltpu.SMEM((stats,), jnp.int32),
        pltpu.VMEM((radius, cols, order // 2), F32),
        pltpu.SemaphoreType.DMA((elems + 4,)),
        pltpu.SemaphoreType.DMA((copies,)),
        pltpu.SemaphoreType.DMA((copies,)),
    ]
    anywhere = pl.BlockSpec(memory_space=pl.ANY)
    vmem = pl.BlockSpec(memory_space=pltpu.VMEM)
    hess, gram = pl.pallas_call(
        functools.partial(kernel, sizes),
        out_shape=(
            jax.ShapeDtypeStruct((elems, cols, order // 2), F32),
            jax.ShapeDtypeStruct((cols, slots * cols), F32),
        ),
        in_specs=[anywhere] * 5,
        out_specs=(vmem, vmem),
        scratch_shapes=scratch,
        compiler_params=pltpu.CompilerParams(
            collective_id=0, has_side_effects=True, vmem_limit_bytes=56 * 1024 * 1024
        ),
    )(neighbors, stations, probes.transpose(1, 0, 2), jacobian, obs_weights)
    hess, gram = pl.pallas_call(
        hand_over,
        out_shape=(
            jax.ShapeDtypeStruct(hess.shape, F32),
            jax.ShapeDtypeStruct((cols, n_col * cols), F32),
        ),
        in_specs=[vmem, vmem],
        out_specs=(vmem, vmem),
    )(hess, gram)
    return hess.transpose(1, 0, 2), gram


def solution(mesh):
    in_specs = (
        P("col", "elem", None),
        P("sec", "elem", None, None, None),
        P("elem", None),
        P("elem"),
        P("elem", None),
    )
    out_specs = (P("col", "elem", "sec"), P("col", None))
    body = functools.partial(per_device, mesh.shape["elem"], mesh.shape["col"])
    return jax.shard_map(
        body, mesh=mesh, in_specs=in_specs, out_specs=out_specs, check_vma=False
    )
```

```python
import functools
import math

import jax
import jax.numpy as jnp
from jax import lax
from jax.experimental import pallas as pl
from jax.experimental.pallas import tpu as pltpu
from jax.sharding import PartitionSpec as P

STEPS = 2
MESH = pl.DeviceIdType.MESH
F32 = jnp.float32
BF16 = jnp.bfloat16
LANES = 128


def halves(value):
    high = value.astype(BF16)
    low = (value - high.astype(F32)).astype(BF16)
    return high, low


def product(a, b, transposed):
    dims = (((1,), (1 if transposed else 0,)), ((), ()))
    return lax.dot_general(a, b, dims, preferred_element_type=F32)


def product3(stack, high, low, transposed):
    rows = stack.shape[0] // 2
    first = product(stack, high, transposed)
    second = product(stack[:rows], low, transposed)
    return first[:rows] + (first[rows:] + second)


def kernel(
    sizes,
    neighbors_hbm,
    stations_hbm,
    probes_hbm,
    jacobian_hbm,
    weights_hbm,
    hess_hbm,
    extra_hbm,
    gram_hbm,
    *scratch,
):
    cols, elems, order, nbrs, stats, n_elem, n_col = sizes
    radius = (nbrs - 1) // 2
    width = radius * order
    half = order // 2
    seats = LANES // 2
    jac_f32 = scratch[:elems]
    jac_high = scratch[elems : 2 * elems]
    jac_low = scratch[2 * elems : 3 * elems]
    (
        probes_ref, weights_ref, state, field, halo_left, halo_right,
        adjoint, adjoint_in, observed, out_left, out_right, back_left, back_right,
        out_half, readings, partial, partial_in, upper,
        u_high, u_low, placed_field, once, once_field, once_halo, once_left, once_right,
        spill_left, spill_right, spill_in_left, spill_in_right,
        answer_out, answer_in, answer_far, answer_far_in, neighbors, stations,
        lower, gram_ref, store_sem,
        load_sem, send_sem, recv_sem,
    ) = scratch[3 * elems :]
    section = lax.axis_index("sec")
    column = lax.axis_index("col")
    block = lax.axis_index("elem")
    left = lax.rem(block + n_elem - 1, n_elem)
    right = lax.rem(block + 1, n_elem)
    even = lax.rem(block, 2) == 0
    far = jnp.where(even, left, right)
    other = 1 - section
    first_elem = block * elems
    elem_total = elems * n_elem
    rounds = int(math.log2(n_elem))
    edge = radius + elems
    full = elems * order
    last = STEPS - 1
    LEFT, RIGHT = 0, 1
    neighbour = (left, right)
    halo_in = (halo_left, halo_right)
    out = (out_left, out_right)
    back = (back_left, back_right)
    once_in = (once_left, once_right)
    spill = (spill_left, spill_right)
    spill_in = (spill_in_left, spill_in_right)
    own_rows = (slice(seats, 2 * seats), slice(0, seats))
    other_rows = (slice(0, seats), slice(seats, 2 * seats))
    own = (slice(0, width), slice(full - width, full))
    own_ds = (pl.ds(0, width), pl.ds(full - width, width))
    own_elems = (range(0, radius), range(elems - radius, elems))
    own_span = ((radius, 2 * radius), (edge - radius, edge))

    def by_parity(run):
        @pl.when(even)
        def _():
            run(RIGHT, LEFT)

        @pl.when(jnp.logical_not(even))
        def _():
            run(LEFT, RIGHT)

    probe_load = pltpu.make_async_copy(probes_hbm, probes_ref, load_sem.at[elems])
    probe_load.start()
    table_loads = [
        pltpu.make_async_copy(neighbors_hbm, neighbors, load_sem.at[elems + 2]),
        pltpu.make_async_copy(stations_hbm, stations, load_sem.at[elems + 3]),
    ]
    for load in table_loads:
        load.start()
    weights_load = pltpu.make_async_copy(
        weights_hbm, weights_ref.at[pl.ds(0, stats)], load_sem.at[elems + 1]
    )
    weights_load.start()
    jac_loads = [
        pltpu.make_async_copy(jacobian_hbm.at[0, e], jac_f32[e], load_sem.at[e])
        for e in range(elems)
    ]
    for load in jac_loads:
        load.start()

    barrier = pltpu.get_barrier_semaphore()
    partners = [{"elem": left}, {"elem": right}, {"sec": other}, {"sec": other, "elem": far}]
    partners += [{"col": lax.rem(column + j, n_col)} for j in range(1, n_col)]
    flips = []
    for r in range(rounds):
        bit = 1 << r
        upper_bit = lax.rem(block // bit, 2)
        flips.append({"elem": block + bit - 2 * bit * upper_bit})
    second_left = lax.rem(block + n_elem - 2, n_elem)
    second_right = lax.rem(block + 2, n_elem)
    partners += [{"elem": second_left}, {"elem": second_right}]
    for partner in partners + flips:
        pl.semaphore_signal(barrier, inc=1, device_id=partner, device_id_type=MESH)

    probe_load.wait()

    @pl.when(section == 0)
    def _():
        for e in range(elems):
            state[0, :, e * order : (e + 1) * order] = probes_ref[e]

    pl.semaphore_wait(barrier, len(partners) + len(flips))

    def remote(src, dst, index, target, arrival=None):
        arrival = index if arrival is None else arrival
        return pltpu.make_async_remote_copy(
            src_ref=src, dst_ref=dst, send_sem=send_sem.at[index],
            recv_sem=recv_sem.at[arrival], device_id=target, device_id_type=MESH,
        )

    FORWARD = 4 * STEPS
    BACKWARD, UPPER = FORWARD + 2, FORWARD + 4
    GRAM, LOWER, HIGHER, READ = (FORWARD + 6 + i for i in range(4))
    FLIP = READ + n_col - 1
    ONCE = FLIP + rounds
    ANSWER = ONCE + 2
    SPILL = ANSWER + 4
    PART = SPILL + 4
    ACROSS = PART + radius
    FORWARD_PART = ACROSS + radius

    def halo_copy(t, side):
        return remote(
            state.at[t, :, own_ds[side]], halo_in[1 - side].at[t], 2 * t + side,
            {"elem": neighbour[side]},
        )

    def part_lanes(side, j):
        return pl.ds(own[side].start + j * order, order)

    def across_part(side, j):
        return remote(
            state.at[STEPS, :, part_lanes(side, j)], halo_in[1 - side].at[0, :, here_ds(j)],
            ACROSS + j, {"sec": other, "elem": neighbour[side]},
        )

    def forward_part(side, j):
        lanes = part_lanes(side, j)
        return remote(
            state.at[STEPS, :, lanes], state.at[0, :, lanes], FORWARD_PART + j, {"sec": other}
        )

    def here_ds(j):
        return pl.ds(j * order, order)

    def forward(side):
        return remote(
            state.at[STEPS, :, own_ds[side]], state.at[0, :, own_ds[side]],
            FORWARD + side, {"sec": other},
        )

    def out_copy(t, side):
        return remote(
            out[side].at[t], back[1 - side].at[t], 2 * STEPS + 2 * t + side,
            {"elem": neighbour[side]},
        )

    def spill_copy(side, first):
        rows = own_rows[side] if first else other_rows[side]
        rows = pl.ds(rows.start, seats)
        return remote(
            spill[side].at[rows], spill_in[1 - side].at[rows], SPILL + 2 * side + int(first),
            {"elem": neighbour[side]},
        )

    def once_copy(side):
        start = 0 if side == LEFT else width + full
        return remote(
            once.at[:, pl.ds(start, width)], once_in[1 - side], ONCE + side,
            {"elem": neighbour[side]},
        )

    answer_copies = [
        remote(source.at[part], target.at[slot], ANSWER + index, {"elem": place})
        for index, (source, target, part, slot, place) in enumerate(
            (
                (answer_out, answer_in, 1, 0, right),
                (answer_out, answer_in, 0, 1, left),
                (answer_far, answer_far_in, 1, 0, second_right),
                (answer_far, answer_far_in, 0, 1, second_left),
            )
        )
    ]

    def backward_part(side, j):
        lanes = part_lanes(side, j)
        return remote(
            adjoint.at[STEPS, :, lanes], adjoint_in.at[:, lanes], PART + j, {"sec": other}
        )

    def backward(side):
        return remote(
            adjoint.at[STEPS, :, own_ds[side]], adjoint_in.at[:, own_ds[side]],
            BACKWARD + side, {"sec": other},
        )

    def half_copy(part, side):
        return remote(
            out_half.at[part], extra_hbm, (LOWER, HIGHER)[part],
            {"sec": section if part == 0 else other, "elem": neighbour[side]},
        )

    def up(side):
        rows = pl.ds(own_elems[side].start, radius)
        return remote(upper.at[rows], hess_hbm.at[rows], UPPER + side, {"sec": other})

    @pl.when(section == 0)
    def _():
        halo_copy(0, LEFT).start()
        halo_copy(0, RIGHT).start()

    for load in table_loads:
        load.wait()

    def split(e, d, use):
        target = lax.rem(first_elem + e + d - radius + elem_total, elem_total)
        slot = jnp.int32(0)
        for k in range(1, nbrs):
            slot = jnp.where(neighbors[e, k] == target, jnp.int32(k), slot)
        high, low = halves(jac_f32[e][slot])
        jac_high[e][:, d * order : (d + 1) * order] = high
        jac_low[e][:, d * order : (d + 1) * order] = low
        use(e + d - radius, high, low)

    lane_ids = lax.broadcasted_iota(jnp.int32, (cols, LANES), 1)

    def take_weights():
        weights_load.wait()
        if weights_ref.shape[0] > stats:
            weights_ref[stats:, :] = jnp.zeros((weights_ref.shape[0] - stats, order), F32)

    def put_field(start, value):
        high, low = halves(value)
        field[:cols, start : start + value.shape[1]] = high
        field[cols:, start : start + value.shape[1]] = low

    def blocks(ref, begin, end):
        return ref[:, begin * order : end * order]

    def gathered(e, low, high):
        return product3(
            blocks(field, low, high), blocks(jac_high[e], low - e, high - e),
            blocks(jac_low[e], low - e, high - e), True,
        )

    def here(e):
        return slice(e * order, (e + 1) * order)

    def advance(t, side):
        ends = [(e, max(e, radius), min(e + nbrs, edge)) for e in own_elems[side]]
        ends.sort(key=lambda span: span[2] - span[1])
        e, low, high = ends.pop()
        middle = (low + high) // 2
        spans = [ends[1], ends[0], (e, low, middle), (e, middle, high)]
        for i, (e, low, high) in enumerate(spans):
            before = state[t + 1 if i == 3 else t, :, here(e)]
            state[t + 1, :, here(e)] = before + gathered(e, low, high)

    def finish_tangent(t, side, away):
        halo_copy(t, 1 - side).wait_recv()
        put_field(0 if side == LEFT else width + full, halo_in[side][t])
        for e in (own_elems[side][1], own_elems[side][0], own_elems[side][2]):
            span = (e, radius) if side == LEFT else (edge, e + nbrs)
            state[t + 1, :, here(e)] = state[t + 1, :, here(e)] + gathered(e, *span)
            if t == last and away:
                j = e - own_elems[side].start
                forward_part(side, j).start()
                across_part(side, j).start()
        if t < last:
            halo_copy(t + 1, side).start()
        else:
            if not away:
                forward(side).start()

    def tangent(t, core, away):
        if t > 0:
            put_field(width, state[t])
        for side in (LEFT, RIGHT) if t == 0 else (core, away):
            if t > 0:
                advance(t, side)
            finish_tangent(t, side, side == away)

    @pl.when(section == 0)
    def _():
        put_field(width, state[0])
        for pair in range(0, elems, 2):
            terms = {}
            for e in range(pair, pair + 2):
                jac_loads[e].wait()

            def use(e, m, high, low):
                if 0 <= m < elems:
                    source = blocks(field, m + radius, m + radius + 1)
                    both = product(source, high, True), product(source[:cols], low, True)
                    for i in range(2):
                        terms[e, i] = terms[e, i] + both[i] if (e, i) in terms else both[i]

            for d in range(nbrs):
                for e in range(pair, pair + 2):
                    split(e, d, functools.partial(use, e))
            for e in range(pair, pair + 2):
                added = terms[e, 0][:cols] + (terms[e, 0][cols:] + terms[e, 1])
                state[1, :, here(e)] = state[0, :, here(e)] + added
        for t in range(STEPS):
            by_parity(functools.partial(tangent, t))

    def by_block(source, rows, elements, m, part=None):
        first, second = None, None
        for e in elements:
            if abs(m - e) > radius:
                continue
            lanes = here(m - e + radius)
            if part is not None:
                lanes = slice(lanes.start + part * half, lanes.start + (part + 1) * half)
            up_term = product(source[:, here(e)], jac_high[e][:, lanes], False)
            low_term = product(source[:rows, here(e)], jac_low[e][:, lanes], False)
            first = up_term if first is None else first + up_term
            second = low_term if second is None else second + low_term
        return first[:rows] + (first[rows:] + second)

    def there(m):
        return slice((m + radius) * order, (m + radius + 1) * order)

    def put_rows(start, m, value):
        high, low = halves(value)
        u_high[start : start + seats, there(m)] = high
        u_low[start : start + seats, there(m)] = low

    def station_products():
        take_weights()
        u_high[...] = jnp.zeros(u_high.shape, BF16)
        u_low[...] = jnp.zeros(u_low.shape, BF16)
        row_ids = lax.broadcasted_iota(jnp.int32, (seats, order), 0)
        station_col = jnp.full((seats, order), -1, jnp.int32)
        for i in range(stats):
            station_col = jnp.where(row_ids == i, stations[i], station_col)

        def placed(e):
            return jnp.where(station_col == first_elem + e, weights_ref[:seats, :], 0.0)

        for e in range(elems):
            high, low = halves(placed(e))
            placed_field[:seats, here(e)] = high
            placed_field[seats:, here(e)] = low

        for e in range(elems):
            jac_loads[e].wait()

            def use(m, high, low, e=e):
                source = placed_field[:, here(e)]
                first = product(source, high, False)
                value = first[seats:] + product(source[:seats], low, False)
                value = first[:seats] + value
                if m == e:
                    value = value + placed(e)
                if e > 0 and m < e + radius:
                    value = value + once[:, there(m)]
                once[:, there(m)] = value

            for d in range(nbrs):
                split(e, d, use)
            if e == radius - 1:
                once_copy(LEFT).start()
        once_copy(RIGHT).start()
        for m in range(elems):
            high, low = halves(once[:, there(m)])
            once_field[:seats, here(m)] = high
            once_field[seats:, here(m)] = low
        for side, span in ((LEFT, range(-radius, 0)), (RIGHT, range(elems, elems + radius))):
            for j, m in enumerate(span):
                value = by_block(once_field, seats, range(elems), m)
                put_rows(seats, m, value)
                spill[side][own_rows[side], here(j)] = value
            spill_copy(side, True).start()
        for m in range(elems):
            value = by_block(once_field, seats, range(elems), m)
            put_rows(seats, m, value + once[:, there(m)])
        for side in (LEFT, RIGHT):
            once_copy(1 - side).wait_recv()
            high, low = halves(once_in[side][...])
            once_halo[:seats, own[side]] = high
            once_halo[seats:, own[side]] = low
            reach = own_elems[side]
            outside = range(-radius, 0) if side == LEFT else range(elems, elems + radius)
            for j, m in enumerate(outside):
                value = by_block(once_halo, seats, reach, m)
                put_rows(0 if side == LEFT else 3 * seats, m, value)
                spill[side][other_rows[side], here(j)] = value
            spill_copy(side, False).start()
            for m in range(elems):
                if m - reach.stop >= radius or reach.start - m > radius:
                    continue
                value = by_block(once_halo, seats, reach, m)
                if m in reach:
                    value = value + once_in[side][:, here(m - reach.start)]
                put_rows(0 if side == LEFT else 3 * seats, m, value)

    def merge(side):
        for part in (True, False):
            spill_copy(1 - side, part).wait_recv()
        starts = (0, seats) if side == LEFT else (seats, 3 * seats)
        for i in range(2):
            rows = slice(starts[i], starts[i] + seats)
            for j, m in enumerate(own_elems[side]):
                value = u_high[rows, there(m)].astype(F32) + u_low[rows, there(m)].astype(F32)
                value = value + spill_in[side][i * seats : (i + 1) * seats, here(j)]
                put_rows(starts[i], m, value)

    def lanes_of(side, halo):
        if halo:
            start = 0 if side == LEFT else width + full
        else:
            start = width + own[side].start
        return slice(start, start + width)

    def answered(value, lanes):
        stack = jnp.concatenate(halves(value), axis=0)
        return product3(stack, u_high[:, lanes], u_low[:, lanes], True)

    def packed(value, keep):
        rows = cols // 2
        return jnp.where(keep, value[:rows], pltpu.roll(value[rows:], seats, 1))

    def unpacked(value):
        return jnp.concatenate([value, pltpu.roll(value, seats, 1)], axis=0)

    for slot in range(n_col, readings.shape[0]):
        readings[slot] = jnp.zeros((cols, LANES), F32)
    read_copies = [
        remote(
            readings.at[column], readings.at[column], READ + j - 1,
            {"col": lax.rem(column + j, n_col)},
        )
        for j in range(1, n_col)
    ]
    flip_copies = [
        remote(partial.at[r], partial_in.at[r], FLIP + r, flips[r]) for r in range(rounds)
    ]
    gram_copy = remote(partial.at[rounds], partial_in.at[rounds], GRAM, {"sec": other})

    gram_store = pltpu.make_async_copy(gram_ref, gram_hbm, store_sem.at[2])

    def store(side):
        rows = pl.ds(own_elems[side].start, radius)
        return pltpu.make_async_copy(lower.at[rows], hess_hbm.at[rows], store_sem.at[side])

    def store_gram():
        gram_copy.wait_recv()
        scale = 1.0 / (elem_total * order)
        gram_ref[...] = (partial[rounds] + partial_in[rounds]) * scale
        gram_store.start()

    def share(reading):
        readings[column] = reading
        for copy in read_copies:
            copy.start()

    def begin_projection():
        for copy in read_copies:
            copy.wait_recv()
        everyone = readings[...].reshape(readings.shape[0] * cols, LANES)
        high, low = halves(everyone)
        stack = jnp.concatenate(halves(readings[column]), axis=0)
        partial[0] = product3(stack, high, low, True)
        flip_copies[0].start()

    def end_projection():
        for r in range(rounds):
            flip_copies[r].wait_recv()
            partial[r + 1] = partial[r] + partial_in[r]
            if r + 1 < rounds:
                flip_copies[r + 1].start()
        gram_copy.start()

    def part_slice(side, j):
        return slice(own[side].start + j * order, own[side].start + (j + 1) * order)

    def respond(core, away):
        forward(core).wait_recv()
        halo_copy(0, core).start()
        total = answered(state[0, :, own[core]], lanes_of(core, False))
        halo_copy(0, 1 - core).wait_recv()
        total = total + answered(halo_in[core][0], lanes_of(core, True))
        own_start, halo_start = (lanes_of(away, halo).start for halo in (False, True))
        for j in (1, 0, 2):
            forward_part(away, j).wait_recv()
            across_part(1 - away, j).wait_recv()
            near_lanes = slice(own_start + j * order, own_start + (j + 1) * order)
            far_lanes = slice(halo_start + j * order, halo_start + (j + 1) * order)
            total = total + answered(state[0, :, part_slice(away, j)], near_lanes)
            total = total + answered(halo_in[away][0, :, here(j)], far_lanes)
        near = lane_ids < seats
        to_left = total[:, :LANES]
        to_right = total[:, LANES:] + jnp.where(near, pltpu.roll(to_left, seats, 1), 0.0)
        answer_out[0] = to_left
        answer_out[1] = to_right
        near_half = near[: cols // 2]
        answer_far[0] = packed(to_left, near_half)
        answer_far[1] = packed(to_right, jnp.logical_not(near_half))
        for copy in answer_copies:
            copy.start()
        for side in (core, away):
            merge(side)
        for copy in answer_copies:
            copy.wait_recv()
        from_left, from_right = answer_in[0], answer_in[1]
        beyond_left, beyond_right = unpacked(answer_far_in[0]), unpacked(answer_far_in[1])
        upper_half = from_left + to_left
        upper_half = upper_half + pltpu.roll(jnp.where(near, from_right, beyond_left), seats, 1)
        lower_answer = from_right + to_right
        lower_answer = lower_answer + pltpu.roll(jnp.where(near, beyond_right, from_left), seats, 1)
        share(jnp.where(near, lower_answer, 0.0))
        stack = jnp.concatenate(halves(jnp.concatenate([upper_half, lower_answer], axis=1)), axis=0)
        for j in range(radius):
            lanes = slice(own_start + j * order, own_start + (j + 1) * order)
            answer = product3(stack, u_high[:, lanes], u_low[:, lanes], False)
            adjoint[STEPS, :, part_slice(away, j)] = answer
            backward_part(away, j).start()
        lanes = lanes_of(core, False)
        answer = product3(stack, u_high[:, lanes], u_low[:, lanes], False)
        adjoint[STEPS, :, own[core]] = answer
        backward_part(away, 1).wait_send()
        backward(core).start()
        begin_projection()
        end_projection()
        store_gram()

    @pl.when(section == 1)
    def _():
        station_products()
        by_parity(respond)

    @pl.when(section == 0)
    def _():
        take_weights()
        weights_high, weights_low = halves(weights_ref[...])
        station_row = jnp.full((cols, LANES), -1, jnp.int32)
        for i in range(stats):
            station_row = jnp.where(lane_ids == i, stations[i], station_row)
        reading = jnp.zeros((cols, LANES), F32)
        for e in range(elems):
            stack = jnp.concatenate(halves(state[STEPS, :, here(e)]), axis=0)
            read = product3(stack, weights_high, weights_low, True)
            read = jnp.where(station_row == first_elem + e, read, 0.0)
            reading = reading + read
            stack = jnp.concatenate(halves(read), axis=0)
            observed[:, here(e)] = product3(stack, weights_high, weights_low, False)
        share(reading)
        begin_projection()
        end_projection()

    def send_out(t, side):
        put_field(own[side].start, adjoint[t, :, own[side]])
        start = -radius if side == LEFT else elems
        for j in range(radius):
            out[side][t, :, here(j)] = by_block(field, cols, own_elems[side], start + j)
        out_copy(t, side).start()

    def inner(t, side, first):
        for m in range(elems):
            value = by_block(field, cols, own_elems[side], m)
            if m in own_elems[side]:
                value = value + adjoint[t, :, here(m)]
            if not first:
                value = value + adjoint[t + 1, :, here(m)]
            adjoint[t + 1, :, here(m)] = value

    def add_back(t, side):
        lanes = own[side]
        out_copy(t, 1 - side).wait_recv()
        adjoint[t + 1, :, lanes] = adjoint[t + 1, :, lanes] + back[side][t]

    def finish(core, away):
        add_back(last - 1, away)
        put_field(own[away].start, adjoint[last, :, own[away]])
        start = -radius if away == LEFT else elems
        for j in range(radius):
            value = by_block(field, cols, own_elems[away], start + j)
            for part in range(2):
                half_lanes = slice(part * half, (part + 1) * half)
                out_half[part, j] = value[:, half_lanes]
        for part in range(2):
            half_copy(part, away).start()
        for part in (1, 0):
            for side in (away, core):
                if side == core and part == 1:
                    out_copy(last, 1 - core).wait_recv()
                for j, m in enumerate(own_elems[side]):
                    lanes = slice(m * order + part * half, m * order + (part + 1) * half)
                    value = by_block(field, cols, own_elems[away], m, part)
                    value = value + adjoint[STEPS, :, lanes]
                    if side == away:
                        value = value + adjoint[last, :, lanes]
                    else:
                        inside = slice(j * order + part * half, j * order + (part + 1) * half)
                        value = value + back[core][last, :, inside]
                    if part == 1:
                        upper[m] = value
                    else:
                        lower[m] = value
                if part == 1:
                    up(side).start()
                else:
                    store(side).start()
        store_gram()
        half_copy(0, 1 - away).wait_recv()

    def adjoint_step(t, core, away):
        order_of_sides = (away, core) if t == 0 else (core, away)
        for side in order_of_sides:
            if t == last and side == away:
                finish(core, away)
                continue
            if t == 0:
                lanes = own[side]
                if side == away:
                    for j in range(radius):
                        backward_part(away, j).wait_recv()
                else:
                    backward(core).wait_recv()
                total = adjoint_in[:, lanes] + observed[:, lanes]
                adjoint[0, :, lanes] = total
            else:
                add_back(t - 1, side)
            send_out(t, side)
            inner(t, side, side == order_of_sides[0])

    @pl.when(section == 0)
    def _():
        for t in range(STEPS):
            by_parity(functools.partial(adjoint_step, t))

    def close(core, away):
        @pl.when(section == 0)
        def _():
            for t in range(STEPS):
                for side in (core, away):
                    halo_copy(t, side).wait_send()
                    if t < last or side == core:
                        out_copy(t, side).wait_send()
            forward(core).wait_send()
            for j in range(radius):
                across_part(away, j).wait_send()
                forward_part(away, j).wait_send()
            for side in (core, away):
                up(side).wait_send()
                store(side).wait()
            for part in range(2):
                half_copy(part, away).wait_send()

        @pl.when(section == 1)
        def _():
            halo_copy(0, core).wait_send()
            for j in range(radius):
                if j != 1:
                    backward_part(away, j).wait_send()
            for copy in answer_copies:
                copy.wait_send()
            for side in (core, away):
                once_copy(side).wait_send()
                for part in (True, False):
                    spill_copy(side, part).wait_send()
                if side == core:
                    backward(core).wait_send()
                up(side).wait_recv()
            half_copy(1, 1 - away).wait_recv()

    by_parity(close)
    gram_copy.wait_send()
    gram_store.wait()
    for copy in read_copies + flip_copies:
        copy.wait_send()


def hand_over(radius, hess_ref, extra_ref, gram_ref, hess_out, gram_out):
    elems = hess_ref.shape[0]
    odd = lax.rem(lax.axis_index("elem"), 2)
    hess_out[...] = hess_ref[...]
    rows = pl.ds(odd * (elems - radius), radius)
    hess_out[rows] = hess_ref[rows] + extra_ref[...]
    gram_out[...] = gram_ref[:, : gram_out.shape[1]]


def per_device(n_elem, n_col, probes, jacobian, neighbors, stations, obs_weights):
    cols, elems, order = probes.shape
    nbrs = neighbors.shape[1]
    stats = stations.shape[0]
    radius = (nbrs - 1) // 2
    rounds = int(math.log2(n_elem))
    slots = max(n_col, LANES // cols)
    sizes = (cols, elems, order, nbrs, stats, n_elem, n_col)
    full, width = elems * order, radius * order
    copies = 4 * STEPS + 19 + 3 * radius + (n_col - 1) + rounds
    seats = LANES // 2
    scratch = [pltpu.VMEM((nbrs, order, order), F32)] * elems
    scratch += [pltpu.VMEM((order, nbrs * order), BF16)] * (2 * elems)
    scratch += [
        pltpu.VMEM((elems, cols, order), F32),
        pltpu.VMEM((LANES, order), F32),
        pltpu.VMEM((STEPS + 1, cols, full), F32),
        pltpu.VMEM((2 * cols, full + 2 * width), BF16),
        pltpu.VMEM((STEPS, cols, width), F32),
        pltpu.VMEM((STEPS, cols, width), F32),
        pltpu.VMEM((STEPS + 1, cols, full), F32),
        pltpu.VMEM((cols, full), F32),
        pltpu.VMEM((cols, full), F32),
        pltpu.VMEM((STEPS, cols, width), F32),
        pltpu.VMEM((STEPS, cols, width), F32),
        pltpu.VMEM((STEPS, cols, width), F32),
        pltpu.VMEM((STEPS, cols, width), F32),
        pltpu.VMEM((2, radius, cols, order // 2), F32),
        pltpu.VMEM((slots, cols, LANES), F32),
        pltpu.VMEM((rounds + 1, cols, slots * cols), F32),
        pltpu.VMEM((rounds + 1, cols, slots * cols), F32),
        pltpu.VMEM((elems, cols, order // 2), F32),
        pltpu.VMEM((4 * seats, full + 2 * width), BF16),
        pltpu.VMEM((4 * seats, full + 2 * width), BF16),
        pltpu.VMEM((2 * seats, full), BF16),
        pltpu.VMEM((seats, full + 2 * width), F32),
        pltpu.VMEM((2 * seats, full), BF16),
        pltpu.VMEM((2 * seats, full), BF16),
        pltpu.VMEM((seats, width), F32),
        pltpu.VMEM((seats, width), F32),
        pltpu.VMEM((2 * seats, width), F32),
        pltpu.VMEM((2 * seats, width), F32),
        pltpu.VMEM((2 * seats, width), F32),
        pltpu.VMEM((2 * seats, width), F32),
        pltpu.VMEM((2, cols, LANES), F32),
        pltpu.VMEM((2, cols, LANES), F32),
        pltpu.VMEM((2, cols // 2, LANES), F32),
        pltpu.VMEM((2, cols // 2, LANES), F32),
        pltpu.SMEM((elems, nbrs), jnp.int32),
        pltpu.SMEM((stats,), jnp.int32),
        pltpu.VMEM((elems, cols, order // 2), F32),
        pltpu.VMEM((cols, slots * cols), F32),
        pltpu.SemaphoreType.DMA((3,)),
        pltpu.SemaphoreType.DMA((elems + 4,)),
        pltpu.SemaphoreType.DMA((copies,)),
        pltpu.SemaphoreType.DMA((copies,)),
    ]
    anywhere = pl.BlockSpec(memory_space=pl.ANY)
    vmem = pl.BlockSpec(memory_space=pltpu.VMEM)
    hess, extra, gram = pl.pallas_call(
        functools.partial(kernel, sizes),
        out_shape=(
            jax.ShapeDtypeStruct((elems, cols, order // 2), F32),
            jax.ShapeDtypeStruct((radius, cols, order // 2), F32),
            jax.ShapeDtypeStruct((cols, slots * cols), F32),
        ),
        in_specs=[anywhere] * 5,
        out_specs=(anywhere,) * 3,
        scratch_shapes=scratch,
        compiler_params=pltpu.CompilerParams(
            collective_id=0, has_side_effects=True, vmem_limit_bytes=56 * 1024 * 1024
        ),
    )(neighbors, stations, probes.transpose(1, 0, 2), jacobian, obs_weights)
    hess, gram = pl.pallas_call(
        functools.partial(hand_over, radius),
        out_shape=(
            jax.ShapeDtypeStruct(hess.shape, F32),
            jax.ShapeDtypeStruct((cols, n_col * cols), F32),
        ),
        in_specs=[vmem] * 3,
        out_specs=(vmem, vmem),
    )(hess, extra, gram)
    return hess.transpose(1, 0, 2), gram


def solution(mesh):
    in_specs = (
        P("col", "elem", None),
        P("sec", "elem", None, None, None),
        P("elem", None),
        P("elem"),
        P("elem", None),
    )
    out_specs = (P("col", "elem", "sec"), P("col", None))
    body = functools.partial(per_device, mesh.shape["elem"], mesh.shape["col"])
    return jax.shard_map(
        body, mesh=mesh, in_specs=in_specs, out_specs=out_specs, check_vma=False
    )
```

```python
import functools
import math

import jax
import jax.numpy as jnp
from jax import lax
from jax.experimental import pallas as pl
from jax.experimental.pallas import tpu as pltpu
from jax.sharding import PartitionSpec as P

STEPS = 2
MESH = pl.DeviceIdType.MESH
F32 = jnp.float32
BF16 = jnp.bfloat16
LANES = 128


def halves(value):
    high = value.astype(BF16)
    low = (value - high.astype(F32)).astype(BF16)
    return high, low


def product(a, b, transposed):
    dims = (((1,), (1 if transposed else 0,)), ((), ()))
    return lax.dot_general(a, b, dims, preferred_element_type=F32)


def product3(stack, high, low, transposed):
    rows = stack.shape[0] // 2
    first = product(stack, high, transposed)
    second = product(stack[:rows], low, transposed)
    return first[:rows] + (first[rows:] + second)


def kernel(
    sizes,
    neighbors_hbm,
    stations_hbm,
    probes_hbm,
    jacobian_hbm,
    weights_hbm,
    hess_hbm,
    extra_hbm,
    gram_hbm,
    *scratch,
):
    cols, elems, order, nbrs, stats, n_elem, n_col = sizes
    radius = (nbrs - 1) // 2
    width = radius * order
    half = order // 2
    seats = LANES // 2
    jac_f32 = scratch[:elems]
    jac_high = scratch[elems : 2 * elems]
    jac_low = scratch[2 * elems : 3 * elems]
    turned_high = scratch[3 * elems : 4 * elems]
    turned_low = scratch[4 * elems : 5 * elems]
    (
        probes_ref, weights_ref, state, field, halo_left, halo_right,
        adjoint, adjoint_in, observed, out_left, out_right, back_left, back_right,
        out_half, readings, partial, partial_in, upper,
        u_high, u_low, placed_field, once, once_field, once_halo, once_left, once_right,
        spill_left, spill_right, spill_in_left, spill_in_right,
        answer_out, answer_in, answer_far, answer_far_in, neighbors, stations,
        lower, gram_ref, store_sem,
        load_sem, send_sem, recv_sem,
    ) = scratch[5 * elems :]
    section = lax.axis_index("sec")
    column = lax.axis_index("col")
    block = lax.axis_index("elem")
    left = lax.rem(block + n_elem - 1, n_elem)
    right = lax.rem(block + 1, n_elem)
    even = lax.rem(block, 2) == 0
    far = jnp.where(even, left, right)
    other = 1 - section
    first_elem = block * elems
    elem_total = elems * n_elem
    rounds = int(math.log2(n_elem))
    edge = radius + elems
    full = elems * order
    last = STEPS - 1
    LEFT, RIGHT = 0, 1
    neighbour = (left, right)
    halo_in = (halo_left, halo_right)
    out = (out_left, out_right)
    back = (back_left, back_right)
    once_in = (once_left, once_right)
    spill = (spill_left, spill_right)
    spill_in = (spill_in_left, spill_in_right)
    own_rows = (slice(seats, 2 * seats), slice(0, seats))
    other_rows = (slice(0, seats), slice(seats, 2 * seats))
    own = (slice(0, width), slice(full - width, full))
    own_ds = (pl.ds(0, width), pl.ds(full - width, width))
    own_elems = (range(0, radius), range(elems - radius, elems))
    own_span = ((radius, 2 * radius), (edge - radius, edge))

    def by_parity(run):
        @pl.when(even)
        def _():
            run(RIGHT, LEFT)

        @pl.when(jnp.logical_not(even))
        def _():
            run(LEFT, RIGHT)

    probe_load = pltpu.make_async_copy(probes_hbm, probes_ref, load_sem.at[elems])
    probe_load.start()
    table_loads = [
        pltpu.make_async_copy(neighbors_hbm, neighbors, load_sem.at[elems + 2]),
        pltpu.make_async_copy(stations_hbm, stations, load_sem.at[elems + 3]),
    ]
    for load in table_loads:
        load.start()
    weights_load = pltpu.make_async_copy(
        weights_hbm, weights_ref.at[pl.ds(0, stats)], load_sem.at[elems + 1]
    )
    weights_load.start()
    jac_loads = [
        pltpu.make_async_copy(jacobian_hbm.at[0, e], jac_f32[e], load_sem.at[e])
        for e in range(elems)
    ]
    backwards = (section == 1) & jnp.logical_not(even)

    @pl.when(backwards)
    def _():
        for load in reversed(jac_loads):
            load.start()

    @pl.when(jnp.logical_not(backwards))
    def _():
        for load in jac_loads:
            load.start()


    barrier = pltpu.get_barrier_semaphore()
    partners = [{"elem": left}, {"elem": right}, {"sec": other}, {"sec": other, "elem": far}]
    partners += [{"col": lax.rem(column + j, n_col)} for j in range(1, n_col)]
    flips = []
    for r in range(rounds):
        bit = 1 << r
        upper_bit = lax.rem(block // bit, 2)
        flips.append({"elem": block + bit - 2 * bit * upper_bit})
    second_left = lax.rem(block + n_elem - 2, n_elem)
    second_right = lax.rem(block + 2, n_elem)
    partners += [{"elem": second_left}, {"elem": second_right}]
    for partner in partners + flips:
        pl.semaphore_signal(barrier, inc=1, device_id=partner, device_id_type=MESH)

    probe_load.wait()

    @pl.when(section == 0)
    def _():
        for e in range(elems):
            state[0, :, e * order : (e + 1) * order] = probes_ref[e]

    pl.semaphore_wait(barrier, len(partners) + len(flips))

    def remote(src, dst, index, target, arrival=None):
        arrival = index if arrival is None else arrival
        return pltpu.make_async_remote_copy(
            src_ref=src, dst_ref=dst, send_sem=send_sem.at[index],
            recv_sem=recv_sem.at[arrival], device_id=target, device_id_type=MESH,
        )

    FORWARD = 4 * STEPS
    BACKWARD, UPPER = FORWARD + 2, FORWARD + 4
    GRAM, LOWER, HIGHER, READ = (FORWARD + 6 + i for i in range(4))
    FLIP = READ + n_col - 1
    ONCE = FLIP + rounds
    ANSWER = ONCE + 2
    SPILL = ANSWER + 4
    PART = SPILL + 4
    ACROSS = PART + radius
    FORWARD_PART = ACROSS + radius

    def halo_copy(t, side):
        return remote(
            state.at[t, :, own_ds[side]], halo_in[1 - side].at[t], 2 * t + side,
            {"elem": neighbour[side]},
        )

    def part_lanes(side, j):
        return pl.ds(own[side].start + j * order, order)

    def across_part(side, j):
        return remote(
            state.at[STEPS, :, part_lanes(side, j)], halo_in[1 - side].at[0, :, here_ds(j)],
            ACROSS + j, {"sec": other, "elem": neighbour[side]},
        )

    def forward_part(side, j):
        lanes = part_lanes(side, j)
        return remote(
            state.at[STEPS, :, lanes], state.at[0, :, lanes], FORWARD_PART + j, {"sec": other}
        )

    def here_ds(j):
        return pl.ds(j * order, order)

    def forward(side):
        return remote(
            state.at[STEPS, :, own_ds[side]], state.at[0, :, own_ds[side]],
            FORWARD + side, {"sec": other},
        )

    def out_copy(t, side):
        return remote(
            out[side].at[t], back[1 - side].at[t], 2 * STEPS + 2 * t + side,
            {"elem": neighbour[side]},
        )

    def spill_copy(side, first):
        rows = own_rows[side] if first else other_rows[side]
        rows = pl.ds(rows.start, seats)
        return remote(
            spill[side].at[rows], spill_in[1 - side].at[rows], SPILL + 2 * side + int(first),
            {"elem": neighbour[side]},
        )

    def once_copy(side):
        start = 0 if side == LEFT else width + full
        return remote(
            once.at[:, pl.ds(start, width)], once_in[1 - side], ONCE + side,
            {"elem": neighbour[side]},
        )

    answer_copies = [
        remote(source.at[part], target.at[slot], ANSWER + index, {"elem": place})
        for index, (source, target, part, slot, place) in enumerate(
            (
                (answer_out, answer_in, 1, 0, right),
                (answer_out, answer_in, 0, 1, left),
                (answer_far, answer_far_in, 1, 0, second_right),
                (answer_far, answer_far_in, 0, 1, second_left),
            )
        )
    ]

    def backward_part(side, j):
        lanes = part_lanes(side, j)
        return remote(
            adjoint.at[STEPS, :, lanes], adjoint_in.at[:, lanes], PART + j, {"sec": other}
        )

    def backward(side):
        return remote(
            adjoint.at[STEPS, :, own_ds[side]], adjoint_in.at[:, own_ds[side]],
            BACKWARD + side, {"sec": other},
        )

    def half_copy(part, side):
        return remote(
            out_half.at[part], extra_hbm, (LOWER, HIGHER)[part],
            {"sec": section if part == 0 else other, "elem": neighbour[side]},
        )

    def up(side):
        rows = pl.ds(own_elems[side].start, radius)
        return remote(upper.at[rows], hess_hbm.at[rows], UPPER + side, {"sec": other})

    @pl.when(section == 0)
    def _():
        halo_copy(0, LEFT).start()
        halo_copy(0, RIGHT).start()

    for load in table_loads:
        load.wait()

    def block_at(e, d):
        target = lax.rem(first_elem + e + d - radius + elem_total, elem_total)
        slot = jnp.int32(0)
        for k in range(1, nbrs):
            slot = jnp.where(neighbors[e, k] == target, jnp.int32(k), slot)
        return jac_f32[e][slot]

    def turn(e, d, use):
        high, low = halves(block_at(e, d).T)
        turned_high[e][here(d), :] = high
        turned_low[e][here(d), :] = low
        use(e + d - radius, high, low)

    def split(e, d, use):
        high, low = halves(block_at(e, d))
        jac_high[e][:, d * order : (d + 1) * order] = high
        jac_low[e][:, d * order : (d + 1) * order] = low
        use(e + d - radius, high, low)

    lane_ids = lax.broadcasted_iota(jnp.int32, (cols, LANES), 1)

    def take_weights():
        weights_load.wait()
        if weights_ref.shape[0] > stats:
            weights_ref[stats:, :] = jnp.zeros((weights_ref.shape[0] - stats, order), F32)

    def put_field(start, value):
        high, low = halves(value)
        field[:cols, start : start + value.shape[1]] = high
        field[cols:, start : start + value.shape[1]] = low

    def blocks(ref, begin, end):
        return ref[:, begin * order : end * order]

    def gathered(e, low, high):
        rows = slice((low - e) * order, (high - e) * order)
        return product3(
            blocks(field, low, high), turned_high[e][rows, :], turned_low[e][rows, :], False
        )

    def here(e):
        return slice(e * order, (e + 1) * order)

    def advance(t, side):
        ends = [(e, max(e, radius), min(e + nbrs, edge)) for e in own_elems[side]]
        ends.sort(key=lambda span: span[2] - span[1])
        e, low, high = ends.pop()
        middle = (low + high) // 2
        spans = [ends[1], ends[0], (e, low, middle), (e, middle, high)]
        for i, (e, low, high) in enumerate(spans):
            before = state[t + 1 if i == 3 else t, :, here(e)]
            state[t + 1, :, here(e)] = before + gathered(e, low, high)

    def finish_tangent(t, side, away):
        halo_copy(t, 1 - side).wait_recv()
        put_field(0 if side == LEFT else width + full, halo_in[side][t])
        for e in (own_elems[side][1], own_elems[side][0], own_elems[side][2]):
            span = (e, radius) if side == LEFT else (edge, e + nbrs)
            state[t + 1, :, here(e)] = state[t + 1, :, here(e)] + gathered(e, *span)
            if t == last and away:
                j = e - own_elems[side].start
                forward_part(side, j).start()
                across_part(side, j).start()
        if t < last:
            halo_copy(t + 1, side).start()
        else:
            if not away:
                forward(side).start()

    def tangent(t, core, away):
        if t > 0:
            put_field(width, state[t])
        for side in (LEFT, RIGHT) if t == 0 else (core, away):
            if t > 0:
                advance(t, side)
            finish_tangent(t, side, side == away)

    @pl.when(section == 0)
    def _():
        put_field(width, state[0])
        for pair in range(0, elems, 2):
            terms = {}
            for e in range(pair, pair + 2):
                jac_loads[e].wait()

            def use(e, m, high, low):
                if 0 <= m < elems:
                    source = blocks(field, m + radius, m + radius + 1)
                    both = product(source, high, False), product(source[:cols], low, False)
                    for i in range(2):
                        terms[e, i] = terms[e, i] + both[i] if (e, i) in terms else both[i]

            for d in range(nbrs):
                for e in range(pair, pair + 2):
                    turn(e, d, functools.partial(use, e))
            for e in range(pair, pair + 2):
                added = terms[e, 0][:cols] + (terms[e, 0][cols:] + terms[e, 1])
                state[1, :, here(e)] = state[0, :, here(e)] + added
        for t in range(STEPS):
            by_parity(functools.partial(tangent, t))

    def by_block(source, rows, elements, m, part=None):
        first, second = None, None
        for e in elements:
            if abs(m - e) > radius:
                continue
            lanes = here(m - e + radius)
            if part is not None:
                lanes = slice(lanes.start + part * half, lanes.start + (part + 1) * half)
            up_term = product(source[:, here(e)], jac_high[e][:, lanes], False)
            low_term = product(source[:rows, here(e)], jac_low[e][:, lanes], False)
            first = up_term if first is None else first + up_term
            second = low_term if second is None else second + low_term
        return first[:rows] + (first[rows:] + second)

    def there(m):
        return slice((m + radius) * order, (m + radius + 1) * order)

    def put_rows(start, m, value):
        high, low = halves(value)
        u_high[start : start + seats, there(m)] = high
        u_low[start : start + seats, there(m)] = low

    def station_products():
        take_weights()
        u_high[...] = jnp.zeros(u_high.shape, BF16)
        u_low[...] = jnp.zeros(u_low.shape, BF16)
        row_ids = lax.broadcasted_iota(jnp.int32, (seats, order), 0)
        station_col = jnp.full((seats, order), -1, jnp.int32)
        for i in range(stats):
            station_col = jnp.where(row_ids == i, stations[i], station_col)

        def placed(e):
            return jnp.where(station_col == first_elem + e, weights_ref[:seats, :], 0.0)

        for e in range(elems):
            high, low = halves(placed(e))
            placed_field[:seats, here(e)] = high
            placed_field[seats:, here(e)] = low

        def collect(core, away):
            seen = set()
            sequence = range(elems) if away == LEFT else range(elems - 1, -1, -1)
            for i, e in enumerate(sequence):
                jac_loads[e].wait()

                def use(m, high, low, e=e):
                    source = placed_field[:, here(e)]
                    first = product(source, high, False)
                    value = first[seats:] + product(source[:seats], low, False)
                    value = first[:seats] + value
                    if m == e:
                        value = value + placed(e)
                    if m in seen:
                        value = value + once[:, there(m)]
                    seen.add(m)
                    once[:, there(m)] = value

                for d in range(nbrs):
                    split(e, d, use)
                if i == radius - 1:
                    once_copy(away).start()
            once_copy(core).start()

        by_parity(collect)
        for m in range(elems):
            high, low = halves(once[:, there(m)])
            once_field[:seats, here(m)] = high
            once_field[seats:, here(m)] = low
        for side, span in ((LEFT, range(-radius, 0)), (RIGHT, range(elems, elems + radius))):
            for j, m in enumerate(span):
                value = by_block(once_field, seats, range(elems), m)
                put_rows(seats, m, value)
                spill[side][own_rows[side], here(j)] = value
            spill_copy(side, True).start()
        for m in range(elems):
            value = by_block(once_field, seats, range(elems), m)
            put_rows(seats, m, value + once[:, there(m)])
        for side in (LEFT, RIGHT):
            once_copy(1 - side).wait_recv()
            high, low = halves(once_in[side][...])
            once_halo[:seats, own[side]] = high
            once_halo[seats:, own[side]] = low
            reach = own_elems[side]
            outside = range(-radius, 0) if side == LEFT else range(elems, elems + radius)
            for j, m in enumerate(outside):
                value = by_block(once_halo, seats, reach, m)
                put_rows(0 if side == LEFT else 3 * seats, m, value)
                spill[side][other_rows[side], here(j)] = value
            spill_copy(side, False).start()
            for m in range(elems):
                if m - reach.stop >= radius or reach.start - m > radius:
                    continue
                value = by_block(once_halo, seats, reach, m)
                if m in reach:
                    value = value + once_in[side][:, here(m - reach.start)]
                put_rows(0 if side == LEFT else 3 * seats, m, value)

    def merge(side):
        for part in (True, False):
            spill_copy(1 - side, part).wait_recv()
        starts = (0, seats) if side == LEFT else (seats, 3 * seats)
        for i in range(2):
            rows = slice(starts[i], starts[i] + seats)
            for j, m in enumerate(own_elems[side]):
                value = u_high[rows, there(m)].astype(F32) + u_low[rows, there(m)].astype(F32)
                value = value + spill_in[side][i * seats : (i + 1) * seats, here(j)]
                put_rows(starts[i], m, value)

    def lanes_of(side, halo):
        if halo:
            start = 0 if side == LEFT else width + full
        else:
            start = width + own[side].start
        return slice(start, start + width)

    def answered(value, lanes):
        stack = jnp.concatenate(halves(value), axis=0)
        return product3(stack, u_high[:, lanes], u_low[:, lanes], True)

    def packed(value, keep):
        rows = cols // 2
        return jnp.where(keep, value[:rows], pltpu.roll(value[rows:], seats, 1))

    def unpacked(value):
        return jnp.concatenate([value, pltpu.roll(value, seats, 1)], axis=0)

    for slot in range(n_col, readings.shape[0]):
        readings[slot] = jnp.zeros((cols, LANES), F32)
    read_copies = [
        remote(
            readings.at[column], readings.at[column], READ + j - 1,
            {"col": lax.rem(column + j, n_col)},
        )
        for j in range(1, n_col)
    ]
    flip_copies = [
        remote(partial.at[r], partial_in.at[r], FLIP + r, flips[r]) for r in range(rounds)
    ]
    gram_copy = remote(partial.at[rounds], partial_in.at[rounds], GRAM, {"sec": other})

    gram_store = pltpu.make_async_copy(gram_ref, gram_hbm, store_sem.at[2])

    def store(side):
        rows = pl.ds(own_elems[side].start, radius)
        return pltpu.make_async_copy(lower.at[rows], hess_hbm.at[rows], store_sem.at[side])

    def store_gram():
        gram_copy.wait_recv()
        scale = 1.0 / (elem_total * order)
        gram_ref[...] = (partial[rounds] + partial_in[rounds]) * scale
        gram_store.start()

    def share(reading):
        readings[column] = reading
        for copy in read_copies:
            copy.start()

    def begin_projection():
        for copy in read_copies:
            copy.wait_recv()
        everyone = readings[...].reshape(readings.shape[0] * cols, LANES)
        high, low = halves(everyone)
        stack = jnp.concatenate(halves(readings[column]), axis=0)
        partial[0] = product3(stack, high, low, True)
        flip_copies[0].start()

    def end_projection():
        for r in range(rounds):
            flip_copies[r].wait_recv()
            partial[r + 1] = partial[r] + partial_in[r]
            if r + 1 < rounds:
                flip_copies[r + 1].start()
        gram_copy.start()

    def part_slice(side, j):
        return slice(own[side].start + j * order, own[side].start + (j + 1) * order)

    def respond(core, away):
        forward(core).wait_recv()
        halo_copy(0, core).start()
        total = answered(state[0, :, own[core]], lanes_of(core, False))
        halo_copy(0, 1 - core).wait_recv()
        total = total + answered(halo_in[core][0], lanes_of(core, True))
        own_start, halo_start = (lanes_of(away, halo).start for halo in (False, True))
        for j in (1, 0, 2):
            forward_part(away, j).wait_recv()
            across_part(1 - away, j).wait_recv()
            near_lanes = slice(own_start + j * order, own_start + (j + 1) * order)
            far_lanes = slice(halo_start + j * order, halo_start + (j + 1) * order)
            total = total + answered(state[0, :, part_slice(away, j)], near_lanes)
            total = total + answered(halo_in[away][0, :, here(j)], far_lanes)
        near = lane_ids < seats
        to_left = total[:, :LANES]
        to_right = total[:, LANES:] + jnp.where(near, pltpu.roll(to_left, seats, 1), 0.0)
        answer_out[0] = to_left
        answer_out[1] = to_right
        near_half = near[: cols // 2]
        answer_far[0] = packed(to_left, near_half)
        answer_far[1] = packed(to_right, jnp.logical_not(near_half))
        for copy in answer_copies:
            copy.start()
        for side in (core, away):
            merge(side)
        for copy in answer_copies:
            copy.wait_recv()
        from_left, from_right = answer_in[0], answer_in[1]
        beyond_left, beyond_right = unpacked(answer_far_in[0]), unpacked(answer_far_in[1])
        upper_half = from_left + to_left
        upper_half = upper_half + pltpu.roll(jnp.where(near, from_right, beyond_left), seats, 1)
        lower_answer = from_right + to_right
        lower_answer = lower_answer + pltpu.roll(jnp.where(near, beyond_right, from_left), seats, 1)
        share(jnp.where(near, lower_answer, 0.0))
        stack = jnp.concatenate(halves(jnp.concatenate([upper_half, lower_answer], axis=1)), axis=0)
        for j in range(radius):
            lanes = slice(own_start + j * order, own_start + (j + 1) * order)
            answer = product3(stack, u_high[:, lanes], u_low[:, lanes], False)
            adjoint[STEPS, :, part_slice(away, j)] = answer
            backward_part(away, j).start()
        lanes = lanes_of(core, False)
        answer = product3(stack, u_high[:, lanes], u_low[:, lanes], False)
        adjoint[STEPS, :, own[core]] = answer
        backward_part(away, 1).wait_send()
        backward(core).start()
        begin_projection()
        end_projection()
        store_gram()

    @pl.when(section == 1)
    def _():
        station_products()
        by_parity(respond)

    @pl.when(section == 0)
    def _():
        take_weights()
        weights_high, weights_low = halves(weights_ref[...])
        station_row = jnp.full((cols, LANES), -1, jnp.int32)
        for i in range(stats):
            station_row = jnp.where(lane_ids == i, stations[i], station_row)
        reading = jnp.zeros((cols, LANES), F32)
        for e in range(elems):
            stack = jnp.concatenate(halves(state[STEPS, :, here(e)]), axis=0)
            read = product3(stack, weights_high, weights_low, True)
            read = jnp.where(station_row == first_elem + e, read, 0.0)
            reading = reading + read
            stack = jnp.concatenate(halves(read), axis=0)
            observed[:, here(e)] = product3(stack, weights_high, weights_low, False)
        share(reading)
        for e in range(elems):
            for d in range(nbrs):
                split(e, d, lambda m, high, low: None)
            if e == radius:
                begin_projection()
        end_projection()

    def send_out(t, side):
        put_field(own[side].start, adjoint[t, :, own[side]])
        start = -radius if side == LEFT else elems
        for j in range(radius):
            out[side][t, :, here(j)] = by_block(field, cols, own_elems[side], start + j)
        out_copy(t, side).start()

    def inner(t, side, first):
        for m in range(elems):
            value = by_block(field, cols, own_elems[side], m)
            if m in own_elems[side]:
                value = value + adjoint[t, :, here(m)]
            if not first:
                value = value + adjoint[t + 1, :, here(m)]
            adjoint[t + 1, :, here(m)] = value

    def add_back(t, side):
        lanes = own[side]
        out_copy(t, 1 - side).wait_recv()
        adjoint[t + 1, :, lanes] = adjoint[t + 1, :, lanes] + back[side][t]

    def finish(core, away):
        add_back(last - 1, away)
        put_field(own[away].start, adjoint[last, :, own[away]])
        start = -radius if away == LEFT else elems
        for j in range(radius):
            value = by_block(field, cols, own_elems[away], start + j)
            for part in range(2):
                half_lanes = slice(part * half, (part + 1) * half)
                out_half[part, j] = value[:, half_lanes]
        for part in range(2):
            half_copy(part, away).start()
        for part in (1, 0):
            for side in (away, core):
                if side == core and part == 1:
                    out_copy(last, 1 - core).wait_recv()
                for j, m in enumerate(own_elems[side]):
                    lanes = slice(m * order + part * half, m * order + (part + 1) * half)
                    value = by_block(field, cols, own_elems[away], m, part)
                    value = value + adjoint[STEPS, :, lanes]
                    if side == away:
                        value = value + adjoint[last, :, lanes]
                    else:
                        inside = slice(j * order + part * half, j * order + (part + 1) * half)
                        value = value + back[core][last, :, inside]
                    if part == 1:
                        upper[m] = value
                    else:
                        lower[m] = value
                if part == 1:
                    up(side).start()
                else:
                    store(side).start()
        store_gram()
        half_copy(0, 1 - away).wait_recv()

    def adjoint_step(t, core, away):
        order_of_sides = (away, core) if t == 0 else (core, away)
        for side in order_of_sides:
            if t == last and side == away:
                finish(core, away)
                continue
            if t == 0:
                lanes = own[side]
                if side == away:
                    for j in range(radius):
                        backward_part(away, j).wait_recv()
                else:
                    backward(core).wait_recv()
                total = adjoint_in[:, lanes] + observed[:, lanes]
                adjoint[0, :, lanes] = total
            else:
                add_back(t - 1, side)
            send_out(t, side)
            inner(t, side, side == order_of_sides[0])

    @pl.when(section == 0)
    def _():
        for t in range(STEPS):
            by_parity(functools.partial(adjoint_step, t))

    def close(core, away):
        @pl.when(section == 0)
        def _():
            for t in range(STEPS):
                for side in (core, away):
                    halo_copy(t, side).wait_send()
                    if t < last or side == core:
                        out_copy(t, side).wait_send()
            forward(core).wait_send()
            for j in range(radius):
                across_part(away, j).wait_send()
                forward_part(away, j).wait_send()
            for side in (core, away):
                up(side).wait_send()
                store(side).wait()
            for part in range(2):
                half_copy(part, away).wait_send()

        @pl.when(section == 1)
        def _():
            halo_copy(0, core).wait_send()
            for j in range(radius):
                if j != 1:
                    backward_part(away, j).wait_send()
            for copy in answer_copies:
                copy.wait_send()
            for side in (core, away):
                once_copy(side).wait_send()
                for part in (True, False):
                    spill_copy(side, part).wait_send()
                if side == core:
                    backward(core).wait_send()
                up(side).wait_recv()
            half_copy(1, 1 - away).wait_recv()

    by_parity(close)
    gram_copy.wait_send()
    gram_store.wait()
    for copy in read_copies + flip_copies:
        copy.wait_send()


def hand_over(radius, hess_ref, extra_ref, gram_ref, hess_out, gram_out):
    elems = hess_ref.shape[0]
    odd = lax.rem(lax.axis_index("elem"), 2)
    hess_out[...] = hess_ref[...]
    rows = pl.ds(odd * (elems - radius), radius)
    hess_out[rows] = hess_ref[rows] + extra_ref[...]
    gram_out[...] = gram_ref[:, : gram_out.shape[1]]


def per_device(n_elem, n_col, probes, jacobian, neighbors, stations, obs_weights):
    cols, elems, order = probes.shape
    nbrs = neighbors.shape[1]
    stats = stations.shape[0]
    radius = (nbrs - 1) // 2
    rounds = int(math.log2(n_elem))
    slots = max(n_col, LANES // cols)
    sizes = (cols, elems, order, nbrs, stats, n_elem, n_col)
    full, width = elems * order, radius * order
    copies = 4 * STEPS + 19 + 3 * radius + (n_col - 1) + rounds
    seats = LANES // 2
    scratch = [pltpu.VMEM((nbrs, order, order), F32)] * elems
    scratch += [pltpu.VMEM((order, nbrs * order), BF16)] * (2 * elems)
    scratch += [pltpu.VMEM((nbrs * order, order), BF16)] * (2 * elems)
    scratch += [
        pltpu.VMEM((elems, cols, order), F32),
        pltpu.VMEM((LANES, order), F32),
        pltpu.VMEM((STEPS + 1, cols, full), F32),
        pltpu.VMEM((2 * cols, full + 2 * width), BF16),
        pltpu.VMEM((STEPS, cols, width), F32),
        pltpu.VMEM((STEPS, cols, width), F32),
        pltpu.VMEM((STEPS + 1, cols, full), F32),
        pltpu.VMEM((cols, full), F32),
        pltpu.VMEM((cols, full), F32),
        pltpu.VMEM((STEPS, cols, width), F32),
        pltpu.VMEM((STEPS, cols, width), F32),
        pltpu.VMEM((STEPS, cols, width), F32),
        pltpu.VMEM((STEPS, cols, width), F32),
        pltpu.VMEM((2, radius, cols, order // 2), F32),
        pltpu.VMEM((slots, cols, LANES), F32),
        pltpu.VMEM((rounds + 1, cols, slots * cols), F32),
        pltpu.VMEM((rounds + 1, cols, slots * cols), F32),
        pltpu.VMEM((elems, cols, order // 2), F32),
        pltpu.VMEM((4 * seats, full + 2 * width), BF16),
        pltpu.VMEM((4 * seats, full + 2 * width), BF16),
        pltpu.VMEM((2 * seats, full), BF16),
        pltpu.VMEM((seats, full + 2 * width), F32),
        pltpu.VMEM((2 * seats, full), BF16),
        pltpu.VMEM((2 * seats, full), BF16),
        pltpu.VMEM((seats, width), F32),
        pltpu.VMEM((seats, width), F32),
        pltpu.VMEM((2 * seats, width), F32),
        pltpu.VMEM((2 * seats, width), F32),
        pltpu.VMEM((2 * seats, width), F32),
        pltpu.VMEM((2 * seats, width), F32),
        pltpu.VMEM((2, cols, LANES), F32),
        pltpu.VMEM((2, cols, LANES), F32),
        pltpu.VMEM((2, cols // 2, LANES), F32),
        pltpu.VMEM((2, cols // 2, LANES), F32),
        pltpu.SMEM((elems, nbrs), jnp.int32),
        pltpu.SMEM((stats,), jnp.int32),
        pltpu.VMEM((elems, cols, order // 2), F32),
        pltpu.VMEM((cols, slots * cols), F32),
        pltpu.SemaphoreType.DMA((3,)),
        pltpu.SemaphoreType.DMA((elems + 4,)),
        pltpu.SemaphoreType.DMA((copies,)),
        pltpu.SemaphoreType.DMA((copies,)),
    ]
    anywhere = pl.BlockSpec(memory_space=pl.ANY)
    vmem = pl.BlockSpec(memory_space=pltpu.VMEM)
    hess, extra, gram = pl.pallas_call(
        functools.partial(kernel, sizes),
        out_shape=(
            jax.ShapeDtypeStruct((elems, cols, order // 2), F32),
            jax.ShapeDtypeStruct((radius, cols, order // 2), F32),
            jax.ShapeDtypeStruct((cols, slots * cols), F32),
        ),
        in_specs=[anywhere] * 5,
        out_specs=(anywhere,) * 3,
        scratch_shapes=scratch,
        compiler_params=pltpu.CompilerParams(
            collective_id=0, has_side_effects=True, vmem_limit_bytes=56 * 1024 * 1024
        ),
    )(neighbors, stations, probes.transpose(1, 0, 2), jacobian, obs_weights)
    hess, gram = pl.pallas_call(
        functools.partial(hand_over, radius),
        out_shape=(
            jax.ShapeDtypeStruct(hess.shape, F32),
            jax.ShapeDtypeStruct((cols, n_col * cols), F32),
        ),
        in_specs=[vmem] * 3,
        out_specs=(vmem, vmem),
    )(hess, extra, gram)
    return hess.transpose(1, 0, 2), gram


def solution(mesh):
    in_specs = (
        P("col", "elem", None),
        P("sec", "elem", None, None, None),
        P("elem", None),
        P("elem"),
        P("elem", None),
    )
    out_specs = (P("col", "elem", "sec"), P("col", None))
    body = functools.partial(per_device, mesh.shape["elem"], mesh.shape["col"])
    return jax.shard_map(
        body, mesh=mesh, in_specs=in_specs, out_specs=out_specs, check_vma=False
    )
```

```python
import functools
import math

import jax
import jax.numpy as jnp
from jax import lax
from jax.experimental import pallas as pl
from jax.experimental.pallas import tpu as pltpu
from jax.sharding import PartitionSpec as P

STEPS = 2
MESH = pl.DeviceIdType.MESH
F32 = jnp.float32
BF16 = jnp.bfloat16
LANES = 128


def halves(value):
    high = value.astype(BF16)
    low = (value - high.astype(F32)).astype(BF16)
    return high, low


def product(a, b, transposed):
    dims = (((1,), (1 if transposed else 0,)), ((), ()))
    return lax.dot_general(a, b, dims, preferred_element_type=F32)


def product3(stack, high, low, transposed):
    rows = stack.shape[0] // 2
    first = product(stack, high, transposed)
    second = product(stack[:rows], low, transposed)
    return first[:rows] + (first[rows:] + second)


def kernel(
    sizes,
    neighbors_hbm,
    stations_hbm,
    probes_hbm,
    jacobian_hbm,
    weights_hbm,
    hess_hbm,
    extra_hbm,
    gram_hbm,
    *scratch,
):
    cols, elems, order, nbrs, stats, n_elem, n_col = sizes
    radius = (nbrs - 1) // 2
    width = radius * order
    half = order // 2
    seats = LANES // 2
    jac_f32 = scratch[:elems]
    jac_high = scratch[elems : 2 * elems]
    jac_low = scratch[2 * elems : 3 * elems]
    turned_high = scratch[3 * elems : 4 * elems]
    turned_low = scratch[4 * elems : 5 * elems]
    (
        probes_ref, weights_ref, state, field, halo_left, halo_right,
        adjoint, adjoint_in, observed, out_left, out_right, back_left, back_right,
        out_half, readings, partial, partial_in, upper,
        u_high, u_low, placed_field, once, once_field, once_halo, once_left, once_right,
        spill_left, spill_right, spill_in_left, spill_in_right,
        answer_out, answer_in, answer_far, answer_far_in, neighbors, stations,
        lower, gram_ref, store_sem,
        load_sem, send_sem, recv_sem,
    ) = scratch[5 * elems :]
    section = lax.axis_index("sec")
    column = lax.axis_index("col")
    block = lax.axis_index("elem")
    left = lax.rem(block + n_elem - 1, n_elem)
    right = lax.rem(block + 1, n_elem)
    even = lax.rem(block, 2) == 0
    far = jnp.where(even, left, right)
    other = 1 - section
    first_elem = block * elems
    elem_total = elems * n_elem
    rounds = int(math.log2(n_elem))
    edge = radius + elems
    full = elems * order
    last = STEPS - 1
    LEFT, RIGHT = 0, 1
    neighbour = (left, right)
    halo_in = (halo_left, halo_right)
    out = (out_left, out_right)
    back = (back_left, back_right)
    once_in = (once_left, once_right)
    spill = (spill_left, spill_right)
    spill_in = (spill_in_left, spill_in_right)
    own_rows = (slice(seats, 2 * seats), slice(0, seats))
    other_rows = (slice(0, seats), slice(seats, 2 * seats))
    own = (slice(0, width), slice(full - width, full))
    own_ds = (pl.ds(0, width), pl.ds(full - width, width))
    own_elems = (range(0, radius), range(elems - radius, elems))
    own_span = ((radius, 2 * radius), (edge - radius, edge))

    def by_parity(run):
        @pl.when(even)
        def _():
            run(RIGHT, LEFT)

        @pl.when(jnp.logical_not(even))
        def _():
            run(LEFT, RIGHT)

    probe_load = pltpu.make_async_copy(probes_hbm, probes_ref, load_sem.at[elems])
    probe_load.start()
    table_loads = [
        pltpu.make_async_copy(neighbors_hbm, neighbors, load_sem.at[elems + 2]),
        pltpu.make_async_copy(stations_hbm, stations, load_sem.at[elems + 3]),
    ]
    for load in table_loads:
        load.start()
    weights_load = pltpu.make_async_copy(
        weights_hbm, weights_ref.at[pl.ds(0, stats)], load_sem.at[elems + 1]
    )
    weights_load.start()
    jac_loads = [
        pltpu.make_async_copy(jacobian_hbm.at[0, e], jac_f32[e], load_sem.at[e])
        for e in range(elems)
    ]
    backwards = (section == 1) & jnp.logical_not(even)

    @pl.when(backwards)
    def _():
        for load in reversed(jac_loads):
            load.start()

    @pl.when(jnp.logical_not(backwards))
    def _():
        for load in jac_loads:
            load.start()


    barrier = pltpu.get_barrier_semaphore()
    partners = [{"elem": left}, {"elem": right}, {"sec": other}, {"sec": other, "elem": far}]
    partners += [{"col": lax.rem(column + j, n_col)} for j in range(1, n_col)]
    flips = []
    for r in range(rounds):
        bit = 1 << r
        upper_bit = lax.rem(block // bit, 2)
        flips.append({"elem": block + bit - 2 * bit * upper_bit})
    second_left = lax.rem(block + n_elem - 2, n_elem)
    second_right = lax.rem(block + 2, n_elem)
    partners += [{"elem": second_left}, {"elem": second_right}]
    for partner in partners + flips:
        pl.semaphore_signal(barrier, inc=1, device_id=partner, device_id_type=MESH)

    probe_load.wait()

    @pl.when(section == 0)
    def _():
        for e in range(elems):
            state[0, :, e * order : (e + 1) * order] = probes_ref[e]

    def everyone_in():
        pl.semaphore_wait(barrier, len(partners) + len(flips))

    @pl.when(section == 0)
    def _():
        everyone_in()


    def remote(src, dst, index, target, arrival=None):
        arrival = index if arrival is None else arrival
        return pltpu.make_async_remote_copy(
            src_ref=src, dst_ref=dst, send_sem=send_sem.at[index],
            recv_sem=recv_sem.at[arrival], device_id=target, device_id_type=MESH,
        )

    FORWARD = 4 * STEPS
    BACKWARD, UPPER = FORWARD + 2, FORWARD + 4
    GRAM, LOWER, HIGHER, READ = (FORWARD + 6 + i for i in range(4))
    FLIP = READ + n_col - 1
    ONCE = FLIP + rounds
    ANSWER = ONCE + 2
    SPILL = ANSWER + 4
    PART = SPILL + 4
    ACROSS = PART + radius
    FORWARD_PART = ACROSS + radius

    def halo_copy(t, side):
        return remote(
            state.at[t, :, own_ds[side]], halo_in[1 - side].at[t], 2 * t + side,
            {"elem": neighbour[side]},
        )

    def part_lanes(side, j):
        return pl.ds(own[side].start + j * order, order)

    def across_part(side, j):
        return remote(
            state.at[STEPS, :, part_lanes(side, j)], halo_in[1 - side].at[0, :, here_ds(j)],
            ACROSS + j, {"sec": other, "elem": neighbour[side]},
        )

    def forward_part(side, j):
        lanes = part_lanes(side, j)
        return remote(
            state.at[STEPS, :, lanes], state.at[0, :, lanes], FORWARD_PART + j, {"sec": other}
        )

    def here_ds(j):
        return pl.ds(j * order, order)

    def forward(side):
        return remote(
            state.at[STEPS, :, own_ds[side]], state.at[0, :, own_ds[side]],
            FORWARD + side, {"sec": other},
        )

    def out_copy(t, side):
        return remote(
            out[side].at[t], back[1 - side].at[t], 2 * STEPS + 2 * t + side,
            {"elem": neighbour[side]},
        )

    def spill_copy(side, first):
        rows = own_rows[side] if first else other_rows[side]
        rows = pl.ds(rows.start, seats)
        return remote(
            spill[side].at[rows], spill_in[1 - side].at[rows], SPILL + 2 * side + int(first),
            {"elem": neighbour[side]},
        )

    def once_copy(side):
        start = 0 if side == LEFT else width + full
        return remote(
            once.at[:, pl.ds(start, width)], once_in[1 - side], ONCE + side,
            {"elem": neighbour[side]},
        )

    answer_copies = [
        remote(source.at[part], target.at[slot], ANSWER + index, {"elem": place})
        for index, (source, target, part, slot, place) in enumerate(
            (
                (answer_out, answer_in, 1, 0, right),
                (answer_out, answer_in, 0, 1, left),
                (answer_far, answer_far_in, 1, 0, second_right),
                (answer_far, answer_far_in, 0, 1, second_left),
            )
        )
    ]

    def backward_part(side, j):
        lanes = part_lanes(side, j)
        return remote(
            adjoint.at[STEPS, :, lanes], adjoint_in.at[:, lanes], PART + j, {"sec": other}
        )

    def backward(side):
        return remote(
            adjoint.at[STEPS, :, own_ds[side]], adjoint_in.at[:, own_ds[side]],
            BACKWARD + side, {"sec": other},
        )

    def half_copy(part, side):
        return remote(
            out_half.at[part], extra_hbm, (LOWER, HIGHER)[part],
            {"sec": section if part == 0 else other, "elem": neighbour[side]},
        )

    def up(side):
        rows = pl.ds(own_elems[side].start, radius)
        return remote(upper.at[rows], hess_hbm.at[rows], UPPER + side, {"sec": other})

    @pl.when(section == 0)
    def _():
        halo_copy(0, LEFT).start()
        halo_copy(0, RIGHT).start()

    for load in table_loads:
        load.wait()

    def block_at(e, d):
        target = lax.rem(first_elem + e + d - radius + elem_total, elem_total)
        slot = jnp.int32(0)
        for k in range(1, nbrs):
            slot = jnp.where(neighbors[e, k] == target, jnp.int32(k), slot)
        return jac_f32[e][slot]

    def turn(e, d, use):
        high, low = halves(block_at(e, d).T)
        turned_high[e][here(d), :] = high
        turned_low[e][here(d), :] = low
        use(e + d - radius, high, low)

    def split(e, d, use):
        high, low = halves(block_at(e, d))
        jac_high[e][:, d * order : (d + 1) * order] = high
        jac_low[e][:, d * order : (d + 1) * order] = low
        use(e + d - radius, high, low)

    lane_ids = lax.broadcasted_iota(jnp.int32, (cols, LANES), 1)

    def take_weights():
        weights_load.wait()
        if weights_ref.shape[0] > stats:
            weights_ref[stats:, :] = jnp.zeros((weights_ref.shape[0] - stats, order), F32)

    def put_field(start, value):
        high, low = halves(value)
        field[:cols, start : start + value.shape[1]] = high
        field[cols:, start : start + value.shape[1]] = low

    def blocks(ref, begin, end):
        return ref[:, begin * order : end * order]

    def gathered(e, low, high):
        rows = slice((low - e) * order, (high - e) * order)
        return product3(
            blocks(field, low, high), turned_high[e][rows, :], turned_low[e][rows, :], False
        )

    def here(e):
        return slice(e * order, (e + 1) * order)

    def advance(t, side):
        ends = [(e, max(e, radius), min(e + nbrs, edge)) for e in own_elems[side]]
        ends.sort(key=lambda span: span[2] - span[1])
        e, low, high = ends.pop()
        middle = (low + high) // 2
        spans = [ends[1], ends[0], (e, low, middle), (e, middle, high)]
        for i, (e, low, high) in enumerate(spans):
            before = state[t + 1 if i == 3 else t, :, here(e)]
            state[t + 1, :, here(e)] = before + gathered(e, low, high)

    def finish_tangent(t, side, away):
        halo_copy(t, 1 - side).wait_recv()
        put_field(0 if side == LEFT else width + full, halo_in[side][t])
        for e in (own_elems[side][1], own_elems[side][0], own_elems[side][2]):
            span = (e, radius) if side == LEFT else (edge, e + nbrs)
            state[t + 1, :, here(e)] = state[t + 1, :, here(e)] + gathered(e, *span)
            if t == last and away:
                j = e - own_elems[side].start
                forward_part(side, j).start()
                across_part(side, j).start()
        if t < last:
            halo_copy(t + 1, side).start()
        else:
            if not away:
                forward(side).start()

    def tangent(t, core, away):
        if t > 0:
            put_field(width, state[t])
        for side in (LEFT, RIGHT) if t == 0 else (core, away):
            if t > 0:
                advance(t, side)
            finish_tangent(t, side, side == away)

    @pl.when(section == 0)
    def _():
        put_field(width, state[0])
        for pair in range(0, elems, 2):
            terms = {}
            for e in range(pair, pair + 2):
                jac_loads[e].wait()

            def use(e, m, high, low):
                if 0 <= m < elems:
                    source = blocks(field, m + radius, m + radius + 1)
                    both = product(source, high, False), product(source[:cols], low, False)
                    for i in range(2):
                        terms[e, i] = terms[e, i] + both[i] if (e, i) in terms else both[i]

            for d in range(nbrs):
                for e in range(pair, pair + 2):
                    turn(e, d, functools.partial(use, e))
            for e in range(pair, pair + 2):
                added = terms[e, 0][:cols] + (terms[e, 0][cols:] + terms[e, 1])
                state[1, :, here(e)] = state[0, :, here(e)] + added
        for t in range(STEPS):
            by_parity(functools.partial(tangent, t))

    def by_block(source, rows, elements, m, part=None):
        first, second = None, None
        for e in elements:
            if abs(m - e) > radius:
                continue
            lanes = here(m - e + radius)
            if part is not None:
                lanes = slice(lanes.start + part * half, lanes.start + (part + 1) * half)
            up_term = product(source[:, here(e)], jac_high[e][:, lanes], False)
            low_term = product(source[:rows, here(e)], jac_low[e][:, lanes], False)
            first = up_term if first is None else first + up_term
            second = low_term if second is None else second + low_term
        return first[:rows] + (first[rows:] + second)

    def there(m):
        return slice((m + radius) * order, (m + radius + 1) * order)

    def put_rows(start, m, value):
        high, low = halves(value)
        u_high[start : start + seats, there(m)] = high
        u_low[start : start + seats, there(m)] = low

    def station_products():
        take_weights()
        u_high[...] = jnp.zeros(u_high.shape, BF16)
        u_low[...] = jnp.zeros(u_low.shape, BF16)
        row_ids = lax.broadcasted_iota(jnp.int32, (seats, order), 0)
        station_col = jnp.full((seats, order), -1, jnp.int32)
        for i in range(stats):
            station_col = jnp.where(row_ids == i, stations[i], station_col)

        def placed(e):
            return jnp.where(station_col == first_elem + e, weights_ref[:seats, :], 0.0)

        for e in range(elems):
            high, low = halves(placed(e))
            placed_field[:seats, here(e)] = high
            placed_field[seats:, here(e)] = low

        def collect(core, away):
            seen = set()
            sequence = range(elems) if away == LEFT else range(elems - 1, -1, -1)
            for i, e in enumerate(sequence):
                jac_loads[e].wait()

                def use(m, high, low, e=e):
                    source = placed_field[:, here(e)]
                    first = product(source, high, False)
                    value = first[seats:] + product(source[:seats], low, False)
                    value = first[:seats] + value
                    if m == e:
                        value = value + placed(e)
                    if m in seen:
                        value = value + once[:, there(m)]
                    seen.add(m)
                    once[:, there(m)] = value

                for d in range(nbrs):
                    split(e, d, use)
                if i == radius - 1:
                    everyone_in()
                    once_copy(away).start()
            once_copy(core).start()

        by_parity(collect)
        for m in range(elems):
            high, low = halves(once[:, there(m)])
            once_field[:seats, here(m)] = high
            once_field[seats:, here(m)] = low
        for side, span in ((LEFT, range(-radius, 0)), (RIGHT, range(elems, elems + radius))):
            for j, m in enumerate(span):
                value = by_block(once_field, seats, range(elems), m)
                put_rows(seats, m, value)
                spill[side][own_rows[side], here(j)] = value
            spill_copy(side, True).start()
        for m in range(elems):
            value = by_block(once_field, seats, range(elems), m)
            put_rows(seats, m, value + once[:, there(m)])
        for side in (LEFT, RIGHT):
            once_copy(1 - side).wait_recv()
            high, low = halves(once_in[side][...])
            once_halo[:seats, own[side]] = high
            once_halo[seats:, own[side]] = low
            reach = own_elems[side]
            outside = range(-radius, 0) if side == LEFT else range(elems, elems + radius)
            for j, m in enumerate(outside):
                value = by_block(once_halo, seats, reach, m)
                put_rows(0 if side == LEFT else 3 * seats, m, value)
                spill[side][other_rows[side], here(j)] = value
            spill_copy(side, False).start()
            for m in range(elems):
                if m - reach.stop >= radius or reach.start - m > radius:
                    continue
                value = by_block(once_halo, seats, reach, m)
                if m in reach:
                    value = value + once_in[side][:, here(m - reach.start)]
                put_rows(0 if side == LEFT else 3 * seats, m, value)

    def merge(side):
        for part in (True, False):
            spill_copy(1 - side, part).wait_recv()
        starts = (0, seats) if side == LEFT else (seats, 3 * seats)
        for i in range(2):
            rows = slice(starts[i], starts[i] + seats)
            for j, m in enumerate(own_elems[side]):
                value = u_high[rows, there(m)].astype(F32) + u_low[rows, there(m)].astype(F32)
                value = value + spill_in[side][i * seats : (i + 1) * seats, here(j)]
                put_rows(starts[i], m, value)

    def lanes_of(side, halo):
        if halo:
            start = 0 if side == LEFT else width + full
        else:
            start = width + own[side].start
        return slice(start, start + width)

    def answered(value, lanes):
        stack = jnp.concatenate(halves(value), axis=0)
        return product3(stack, u_high[:, lanes], u_low[:, lanes], True)

    def packed(value, keep):
        rows = cols // 2
        return jnp.where(keep, value[:rows], pltpu.roll(value[rows:], seats, 1))

    def unpacked(value):
        return jnp.concatenate([value, pltpu.roll(value, seats, 1)], axis=0)

    for slot in range(n_col, readings.shape[0]):
        readings[slot] = jnp.zeros((cols, LANES), F32)
    read_copies = [
        remote(
            readings.at[column], readings.at[column], READ + j - 1,
            {"col": lax.rem(column + j, n_col)},
        )
        for j in range(1, n_col)
    ]
    flip_copies = [
        remote(partial.at[r], partial_in.at[r], FLIP + r, flips[r]) for r in range(rounds)
    ]
    gram_copy = remote(partial.at[rounds], partial_in.at[rounds], GRAM, {"sec": other})

    gram_store = pltpu.make_async_copy(gram_ref, gram_hbm, store_sem.at[2])

    def store(side):
        rows = pl.ds(own_elems[side].start, radius)
        return pltpu.make_async_copy(lower.at[rows], hess_hbm.at[rows], store_sem.at[side])

    def store_gram():
        gram_copy.wait_recv()
        scale = 1.0 / (elem_total * order)
        gram_ref[...] = (partial[rounds] + partial_in[rounds]) * scale
        gram_store.start()

    def share(reading):
        readings[column] = reading
        for copy in read_copies:
            copy.start()

    def begin_projection():
        for copy in read_copies:
            copy.wait_recv()
        everyone = readings[...].reshape(readings.shape[0] * cols, LANES)
        high, low = halves(everyone)
        stack = jnp.concatenate(halves(readings[column]), axis=0)
        partial[0] = product3(stack, high, low, True)
        flip_copies[0].start()

    def end_projection():
        for r in range(rounds):
            flip_copies[r].wait_recv()
            partial[r + 1] = partial[r] + partial_in[r]
            if r + 1 < rounds:
                flip_copies[r + 1].start()
        gram_copy.start()

    def part_slice(side, j):
        return slice(own[side].start + j * order, own[side].start + (j + 1) * order)

    def respond(core, away):
        forward(core).wait_recv()
        halo_copy(0, core).start()
        total = answered(state[0, :, own[core]], lanes_of(core, False))
        halo_copy(0, 1 - core).wait_recv()
        total = total + answered(halo_in[core][0], lanes_of(core, True))
        own_start, halo_start = (lanes_of(away, halo).start for halo in (False, True))
        for j in (1, 0, 2):
            forward_part(away, j).wait_recv()
            across_part(1 - away, j).wait_recv()
            near_lanes = slice(own_start + j * order, own_start + (j + 1) * order)
            far_lanes = slice(halo_start + j * order, halo_start + (j + 1) * order)
            total = total + answered(state[0, :, part_slice(away, j)], near_lanes)
            total = total + answered(halo_in[away][0, :, here(j)], far_lanes)
        near = lane_ids < seats
        to_left = total[:, :LANES]
        to_right = total[:, LANES:] + jnp.where(near, pltpu.roll(to_left, seats, 1), 0.0)
        answer_out[0] = to_left
        answer_out[1] = to_right
        near_half = near[: cols // 2]
        answer_far[0] = packed(to_left, near_half)
        answer_far[1] = packed(to_right, jnp.logical_not(near_half))
        for copy in answer_copies:
            copy.start()
        for side in (core, away):
            merge(side)
        for copy in answer_copies:
            copy.wait_recv()
        from_left, from_right = answer_in[0], answer_in[1]
        beyond_left, beyond_right = unpacked(answer_far_in[0]), unpacked(answer_far_in[1])
        upper_half = from_left + to_left
        upper_half = upper_half + pltpu.roll(jnp.where(near, from_right, beyond_left), seats, 1)
        lower_answer = from_right + to_right
        lower_answer = lower_answer + pltpu.roll(jnp.where(near, beyond_right, from_left), seats, 1)
        share(jnp.where(near, lower_answer, 0.0))
        stack = jnp.concatenate(halves(jnp.concatenate([upper_half, lower_answer], axis=1)), axis=0)
        for j in range(radius):
            lanes = slice(own_start + j * order, own_start + (j + 1) * order)
            answer = product3(stack, u_high[:, lanes], u_low[:, lanes], False)
            adjoint[STEPS, :, part_slice(away, j)] = answer
            backward_part(away, j).start()
        lanes = lanes_of(core, False)
        answer = product3(stack, u_high[:, lanes], u_low[:, lanes], False)
        adjoint[STEPS, :, own[core]] = answer
        backward_part(away, 1).wait_send()
        backward(core).start()
        begin_projection()
        end_projection()
        store_gram()

    @pl.when(section == 1)
    def _():
        station_products()
        by_parity(respond)

    @pl.when(section == 0)
    def _():
        take_weights()
        weights_high, weights_low = halves(weights_ref[...])
        station_row = jnp.full((cols, LANES), -1, jnp.int32)
        for i in range(stats):
            station_row = jnp.where(lane_ids == i, stations[i], station_row)
        reading = jnp.zeros((cols, LANES), F32)
        for e in range(elems):
            stack = jnp.concatenate(halves(state[STEPS, :, here(e)]), axis=0)
            read = product3(stack, weights_high, weights_low, True)
            read = jnp.where(station_row == first_elem + e, read, 0.0)
            reading = reading + read
            stack = jnp.concatenate(halves(read), axis=0)
            observed[:, here(e)] = product3(stack, weights_high, weights_low, False)
        share(reading)
        for e in range(elems):
            for d in range(nbrs):
                split(e, d, lambda m, high, low: None)
            if e == radius:
                begin_projection()
        end_projection()

    def send_out(t, side):
        put_field(own[side].start, adjoint[t, :, own[side]])
        start = -radius if side == LEFT else elems
        for j in range(radius):
            out[side][t, :, here(j)] = by_block(field, cols, own_elems[side], start + j)
        out_copy(t, side).start()

    def inner(t, side, first):
        for m in range(elems):
            value = by_block(field, cols, own_elems[side], m)
            if m in own_elems[side]:
                value = value + adjoint[t, :, here(m)]
            if not first:
                value = value + adjoint[t + 1, :, here(m)]
            adjoint[t + 1, :, here(m)] = value

    def add_back(t, side):
        lanes = own[side]
        out_copy(t, 1 - side).wait_recv()
        adjoint[t + 1, :, lanes] = adjoint[t + 1, :, lanes] + back[side][t]

    def finish(core, away):
        add_back(last - 1, away)
        put_field(own[away].start, adjoint[last, :, own[away]])
        start = -radius if away == LEFT else elems
        for j in range(radius):
            value = by_block(field, cols, own_elems[away], start + j)
            for part in range(2):
                half_lanes = slice(part * half, (part + 1) * half)
                out_half[part, j] = value[:, half_lanes]
        for part in range(2):
            half_copy(part, away).start()
        for part in (1, 0):
            for side in (away, core):
                if side == core and part == 1:
                    out_copy(last, 1 - core).wait_recv()
                for j, m in enumerate(own_elems[side]):
                    lanes = slice(m * order + part * half, m * order + (part + 1) * half)
                    value = by_block(field, cols, own_elems[away], m, part)
                    value = value + adjoint[STEPS, :, lanes]
                    if side == away:
                        value = value + adjoint[last, :, lanes]
                    else:
                        inside = slice(j * order + part * half, j * order + (part + 1) * half)
                        value = value + back[core][last, :, inside]
                    if part == 1:
                        upper[m] = value
                    else:
                        lower[m] = value
                if part == 1:
                    up(side).start()
                else:
                    store(side).start()
        store_gram()
        half_copy(0, 1 - away).wait_recv()

    def adjoint_step(t, core, away):
        order_of_sides = (away, core) if t == 0 else (core, away)
        for side in order_of_sides:
            if t == last and side == away:
                finish(core, away)
                continue
            if t == 0:
                lanes = own[side]
                if side == away:
                    for j in range(radius):
                        backward_part(away, j).wait_recv()
                else:
                    backward(core).wait_recv()
                total = adjoint_in[:, lanes] + observed[:, lanes]
                adjoint[0, :, lanes] = total
            else:
                add_back(t - 1, side)
            send_out(t, side)
            inner(t, side, side == order_of_sides[0])

    @pl.when(section == 0)
    def _():
        for t in range(STEPS):
            by_parity(functools.partial(adjoint_step, t))

    def close(core, away):
        @pl.when(section == 0)
        def _():
            for t in range(STEPS):
                for side in (core, away):
                    halo_copy(t, side).wait_send()
                    if t < last or side == core:
                        out_copy(t, side).wait_send()
            forward(core).wait_send()
            for j in range(radius):
                across_part(away, j).wait_send()
                forward_part(away, j).wait_send()
            for side in (core, away):
                up(side).wait_send()
                store(side).wait()
            for part in range(2):
                half_copy(part, away).wait_send()

        @pl.when(section == 1)
        def _():
            halo_copy(0, core).wait_send()
            for j in range(radius):
                if j != 1:
                    backward_part(away, j).wait_send()
            for copy in answer_copies:
                copy.wait_send()
            for side in (core, away):
                once_copy(side).wait_send()
                for part in (True, False):
                    spill_copy(side, part).wait_send()
                if side == core:
                    backward(core).wait_send()
                up(side).wait_recv()
            half_copy(1, 1 - away).wait_recv()

    by_parity(close)
    gram_copy.wait_send()
    gram_store.wait()
    for copy in read_copies + flip_copies:
        copy.wait_send()


def hand_over(radius, hess_ref, extra_ref, gram_ref, hess_out, gram_out):
    elems = hess_ref.shape[0]
    odd = lax.rem(lax.axis_index("elem"), 2)
    hess_out[...] = hess_ref[...]
    rows = pl.ds(odd * (elems - radius), radius)
    hess_out[rows] = hess_ref[rows] + extra_ref[...]
    gram_out[...] = gram_ref[:, : gram_out.shape[1]]


def per_device(n_elem, n_col, probes, jacobian, neighbors, stations, obs_weights):
    cols, elems, order = probes.shape
    nbrs = neighbors.shape[1]
    stats = stations.shape[0]
    radius = (nbrs - 1) // 2
    rounds = int(math.log2(n_elem))
    slots = max(n_col, LANES // cols)
    sizes = (cols, elems, order, nbrs, stats, n_elem, n_col)
    full, width = elems * order, radius * order
    copies = 4 * STEPS + 19 + 3 * radius + (n_col - 1) + rounds
    seats = LANES // 2
    scratch = [pltpu.VMEM((nbrs, order, order), F32)] * elems
    scratch += [pltpu.VMEM((order, nbrs * order), BF16)] * (2 * elems)
    scratch += [pltpu.VMEM((nbrs * order, order), BF16)] * (2 * elems)
    scratch += [
        pltpu.VMEM((elems, cols, order), F32),
        pltpu.VMEM((LANES, order), F32),
        pltpu.VMEM((STEPS + 1, cols, full), F32),
        pltpu.VMEM((2 * cols, full + 2 * width), BF16),
        pltpu.VMEM((STEPS, cols, width), F32),
        pltpu.VMEM((STEPS, cols, width), F32),
        pltpu.VMEM((STEPS + 1, cols, full), F32),
        pltpu.VMEM((cols, full), F32),
        pltpu.VMEM((cols, full), F32),
        pltpu.VMEM((STEPS, cols, width), F32),
        pltpu.VMEM((STEPS, cols, width), F32),
        pltpu.VMEM((STEPS, cols, width), F32),
        pltpu.VMEM((STEPS, cols, width), F32),
        pltpu.VMEM((2, radius, cols, order // 2), F32),
        pltpu.VMEM((slots, cols, LANES), F32),
        pltpu.VMEM((rounds + 1, cols, slots * cols), F32),
        pltpu.VMEM((rounds + 1, cols, slots * cols), F32),
        pltpu.VMEM((elems, cols, order // 2), F32),
        pltpu.VMEM((4 * seats, full + 2 * width), BF16),
        pltpu.VMEM((4 * seats, full + 2 * width), BF16),
        pltpu.VMEM((2 * seats, full), BF16),
        pltpu.VMEM((seats, full + 2 * width), F32),
        pltpu.VMEM((2 * seats, full), BF16),
        pltpu.VMEM((2 * seats, full), BF16),
        pltpu.VMEM((seats, width), F32),
        pltpu.VMEM((seats, width), F32),
        pltpu.VMEM((2 * seats, width), F32),
        pltpu.VMEM((2 * seats, width), F32),
        pltpu.VMEM((2 * seats, width), F32),
        pltpu.VMEM((2 * seats, width), F32),
        pltpu.VMEM((2, cols, LANES), F32),
        pltpu.VMEM((2, cols, LANES), F32),
        pltpu.VMEM((2, cols // 2, LANES), F32),
        pltpu.VMEM((2, cols // 2, LANES), F32),
        pltpu.SMEM((elems, nbrs), jnp.int32),
        pltpu.SMEM((stats,), jnp.int32),
        pltpu.VMEM((elems, cols, order // 2), F32),
        pltpu.VMEM((cols, slots * cols), F32),
        pltpu.SemaphoreType.DMA((3,)),
        pltpu.SemaphoreType.DMA((elems + 4,)),
        pltpu.SemaphoreType.DMA((copies,)),
        pltpu.SemaphoreType.DMA((copies,)),
    ]
    anywhere = pl.BlockSpec(memory_space=pl.ANY)
    vmem = pl.BlockSpec(memory_space=pltpu.VMEM)
    hess, extra, gram = pl.pallas_call(
        functools.partial(kernel, sizes),
        out_shape=(
            jax.ShapeDtypeStruct((elems, cols, order // 2), F32),
            jax.ShapeDtypeStruct((radius, cols, order // 2), F32),
            jax.ShapeDtypeStruct((cols, slots * cols), F32),
        ),
        in_specs=[anywhere] * 5,
        out_specs=(anywhere,) * 3,
        scratch_shapes=scratch,
        compiler_params=pltpu.CompilerParams(
            collective_id=0, has_side_effects=True, vmem_limit_bytes=56 * 1024 * 1024
        ),
    )(neighbors, stations, probes.transpose(1, 0, 2), jacobian, obs_weights)
    hess, gram = pl.pallas_call(
        functools.partial(hand_over, radius),
        out_shape=(
            jax.ShapeDtypeStruct(hess.shape, F32),
            jax.ShapeDtypeStruct((cols, n_col * cols), F32),
        ),
        in_specs=[vmem] * 3,
        out_specs=(vmem, vmem),
    )(hess, extra, gram)
    return hess.transpose(1, 0, 2), gram


def solution(mesh):
    in_specs = (
        P("col", "elem", None),
        P("sec", "elem", None, None, None),
        P("elem", None),
        P("elem"),
        P("elem", None),
    )
    out_specs = (P("col", "elem", "sec"), P("col", None))
    body = functools.partial(per_device, mesh.shape["elem"], mesh.shape["col"])
    return jax.shard_map(
        body, mesh=mesh, in_specs=in_specs, out_specs=out_specs, check_vma=False
    )
```
